32 devices in a mesh: groups: 1, ctx: 16 (over z, y, core), uly: 2 (over x), rep: 1.
Axes of the slice: x: 2, y: 2, z: 4, core: 2. Of those that a mesh axis runs over, the one named last changes fastest.
Arguments:
- q_proj: bfloat16 [4096, 5120], P(('groups', 'ctx', 'rep', 'uly')), may hold values from -8 to 8
- k_proj: bfloat16 [4096, 5120], P(('groups', 'ctx', 'rep', 'uly')), may hold values from -8 to 8
- v_proj: bfloat16 [4096, 5120], P(('groups', 'ctx', 'rep', 'uly')), may hold values from -4 to 4
- kv_list: int32 [32, 16], P('groups'), may hold values from -1 to 31, as said below
Outputs:
- attended: bfloat16 [4096, 5120], P(('groups', 'ctx', 'rep', 'uly'))
The draws below stay inside these ranges and needn't reach their ends.
Inputs may be any that keep to these rules, and one draw needn't show every extreme that they name: `kv_list`: frame f holds blocks f * 2 to (f + 1) * 2 - 1. Row i lists, in ascending order and padded with -1 at the end, the key blocks that query block i attends: all 2 blocks of its own frame and some blocks of frames at distance 1 to 7. For a query frame f and a distance d whose frame f + d exists, the blocks of frame f + d listed by the query blocks of f are exactly 1 distinct blocks if |d| = 1 and exactly one block if 2 <= |d| <= 7; up to |d| = 3 every query block of f lists all of them.
All inputs are finite; a program needn't handle non-finite values.
Results may differ from the reference program's by a relative error of at most 0.014.
Values may be sent and summed in bfloat16 or wider, within the bound.
A program may use at most 128 MiB of HBM per device.

```python
import jax
import jax.numpy as jnp
from jax import lax

HEADS = 40
HD = 128
BLK = 128
BPF = 2
REACH = 7
FULL_REACH = 3
WIDTH = 5120
NEAR = 1
FRAMES = 16
BLOCKS = 32
SEQ = 4096


def draw_q_proj(key, part):
    base_draw = jnp.clip(jax.random.normal(jax.random.fold_in(key, 21), (SEQ, WIDTH), jnp.float32), -4.0, 4.0)
    return base_draw.astype(jnp.bfloat16)


def draw_k_proj(key, part):
    base_draw = jnp.clip(jax.random.normal(jax.random.fold_in(key, 31), (SEQ, WIDTH), jnp.float32), -4.0, 4.0)
    return base_draw.astype(jnp.bfloat16)


def draw_kv_list(key, part):
    offsets = [offset for offset in range(-REACH, REACH + 1) if offset != 0]
    frame_of = jnp.arange(BLOCKS, dtype=jnp.int32) // BPF
    place_in = jnp.arange(BLOCKS, dtype=jnp.int32) % BPF
    heavy_block = jax.random.randint(jax.random.fold_in(key, 1), (FRAMES,), 0, BPF)
    coin_flip = jax.random.randint(jax.random.fold_in(key, 2), (BLOCKS, len(offsets)), 0, 2)
    rank_draw = jax.random.randint(jax.random.fold_in(key, 3), (FRAMES, len(offsets), BPF), 0, 1 << 20)
    block_order = jnp.argsort(rank_draw * BPF + jnp.arange(BPF, dtype=jnp.int32), axis=-1).astype(jnp.int32)
    pieces = [frame_of[:, None] * BPF + jnp.arange(BPF, dtype=jnp.int32)[None, :]]
    for column, offset in enumerate(offsets):
        keep_count = NEAR if abs(offset) == 1 else 1
        source = frame_of + offset
        inside = (source >= 0) & (source < FRAMES)
        if abs(offset) <= FULL_REACH:
            listed = inside
        else:
            listed = inside & ((coin_flip[:, column] == 1) | (place_in == heavy_block[frame_of]))
        chosen = block_order[frame_of, column, :keep_count] + source[:, None] * BPF
        pieces.append(jnp.where(listed[:, None], chosen, -1))
    entries = jnp.concatenate(pieces, axis=1)
    beyond = BLOCKS + 1
    ordered = jnp.sort(jnp.where(entries >= 0, entries, beyond), axis=-1)
    return jnp.where(ordered == beyond, -1, ordered).astype(jnp.int32)


def level_of(stream_key, dims, cuts, least, high):
    loudness = 1.0
    for position, shards_of in cuts:
        steps = jax.random.uniform(jax.random.fold_in(jax.random.fold_in(stream_key, 6), position), (shards_of,), jnp.float32, least / len(cuts), high / len(cuts))
        loudness = loudness * jnp.repeat(jnp.exp(steps), dims[position] // shards_of).reshape((-1,) + (1,) * (len(dims) - 1 - position))
    return loudness


def scatter_about(rng, dims, scale, reach, cuts=(), kind=jnp.bfloat16):
    values = jax.random.normal(rng, dims, jnp.float32) * scale
    if len(cuts) > 0:
        values = level_of(rng, dims, cuts, -0.22, 0.18) * values
    return jnp.clip(values, min=-reach, max=reach).astype(kind)


def setup_inputs(seed: int = 0, part: int = 0) -> dict:
    seeds = jax.random.split(jax.random.key(seed), 5)
    part_splits = jax.random.split(jax.random.fold_in(seeds[4], part), 5)
    return {
        "q_proj": draw_q_proj(jax.random.fold_in(jax.random.fold_in(seeds[4], part), 71), part),
        "k_proj": draw_k_proj(jax.random.fold_in(jax.random.fold_in(seeds[4], part), 71), part),
        "v_proj": scatter_about(part_splits[2], (SEQ, WIDTH), 1.0, 4.0, ((0, 32),)),
        "kv_list": draw_kv_list(jax.random.fold_in(jax.random.fold_in(seeds[4], part), 71), part),
    }


def reference(q_proj, k_proj, v_proj, kv_list):
    seq_len, width = q_proj.shape
    block_count = seq_len // BLK
    q_tiles = q_proj.reshape(block_count, BLK, HEADS, HD)
    k_tiles = k_proj.reshape(block_count, BLK, HEADS, HD)
    v_tiles = v_proj.reshape(block_count, BLK, HEADS, HD)
    score_scale = HD ** -0.5

    def one_block(inputs):
        query, listed = inputs
        usable = listed >= 0
        safe_ids = jnp.where(usable, listed, 0).astype(jnp.int32)
        key_rows = jnp.take(k_tiles, safe_ids, axis=0).astype(jnp.float32)
        value_rows = jnp.take(v_tiles, safe_ids, axis=0).astype(jnp.float32)
        scores = jnp.einsum("qhd,lkhd->hqlk", query.astype(jnp.float32), key_rows) * score_scale
        scores = jnp.where(usable[None, None, :, None], scores, -jnp.inf)
        row_max = jnp.max(scores, axis=(2, 3), keepdims=True)
        exp_scores = jnp.exp(scores - row_max)
        row_total = jnp.sum(exp_scores, axis=(2, 3))
        weights = lax.optimization_barrier(exp_scores.astype(jnp.bfloat16)).astype(jnp.float32)
        mixed = jnp.einsum("hqlk,lkhd->qhd", weights, value_rows)
        return (mixed / jnp.transpose(row_total)[:, :, None]).astype(jnp.bfloat16)

    attended = lax.map(one_block, (q_tiles, kv_list))
    return attended.reshape(seq_len, width)
```

```python
import functools
import math

import jax
import jax.numpy as jnp
from jax import lax
from jax.experimental import pallas as pl
from jax.experimental.pallas import tpu as pltpu
from jax.sharding import PartitionSpec as P

HD = 128
BLK = 128
BPF = 2
FRAME = BLK * BPF
REACH = 7
GROUP = 8
SLOTS = 2 * REACH
KEYS = (SLOTS + BPF) * BLK

very_low = -1e30
scale2 = math.log2(math.e) / math.sqrt(HD)
MESH = pl.DeviceIdType.MESH


def ring_kernel(sizes, sel_ref, bias_ref, q_ref, k_ref, v_ref, out_ref, kv, qb, ob, ks, vs,
           first_in, kv_in, q_in, kv_sent, q_sent, ring_in, ring_sent, out_in, out_sent):
    ctx, rep, uly, tokens, heads = sizes
    inner = GROUP // (rep * uly)
    here = GROUP * tokens
    frames_here = here // FRAME
    places = ctx // inner
    hops = -(-REACH // frames_here)
    c = lax.axis_index("ctx")
    r = lax.axis_index("rep")
    u = lax.axis_index("uly")
    place = c // inner
    me = (c % inner) * (rep * uly) + r * uly + u

    def member(j):
        return {"ctx": place * inner + j // (rep * uly), "rep": (j // uly) % rep, "uly": j % uly}

    def beside(step):
        return {"ctx": c + step * inner}

    has_left, has_right = place >= 1, place <= places - 2

    barrier = pltpu.get_barrier_semaphore()
    for k in range(1, GROUP):
        pl.semaphore_signal(barrier, inc=1, device_id=member((me + k) % GROUP), device_id_type=MESH)

    @pl.when(has_left)
    def _():
        pl.semaphore_signal(barrier, inc=1, device_id=beside(-1), device_id_type=MESH)

    @pl.when(has_right)
    def _():
        pl.semaphore_signal(barrier, inc=1, device_id=beside(1), device_id_type=MESH)

    neighbours = jnp.minimum(place, 1) + jnp.minimum(places - 1 - place, 1)
    pl.semaphore_wait(barrier, GROUP - 1 + neighbours)

    def columns(owner, h):
        return pl.ds(pl.multiple_of((owner * heads + h) * HD, HD), HD)

    own_rows = pl.ds(pl.multiple_of(REACH * FRAME + me * tokens, tokens), tokens)
    q_rows = pl.ds(pl.multiple_of(me * tokens, tokens), tokens)

    def share_kv(h, arrived):
        for k in range(1, GROUP):
            j = (me + k) % GROUP
            for which, src in enumerate((k_ref, v_ref)):
                pltpu.make_async_remote_copy(
                    src_ref=src.at[:, columns(j, h)], dst_ref=kv.at[h, which, own_rows],
                    send_sem=kv_sent.at[h], recv_sem=arrived(k),
                    device_id=member(j), device_id_type=MESH,
                ).start()
        for which, src in enumerate((k_ref, v_ref)):
            pltpu.make_async_copy(
                src.at[:, columns(me, h)], kv.at[h, which, own_rows], arrived(0)
            ).start()

    def share_later(h, carry):
        share_kv(h, lambda k: kv_in.at[h])
        return carry

    def share_q(h, carry):
        for k in range(1, GROUP):
            j = (me + k) % GROUP
            pltpu.make_async_remote_copy(
                src_ref=q_ref.at[:, columns(j, h)], dst_ref=qb.at[h, q_rows],
                send_sem=q_sent.at[h], recv_sem=q_in.at[h],
                device_id=member(j), device_id_type=MESH,
            ).start()
        pltpu.make_async_copy(q_ref.at[:, columns(me, h)], qb.at[h, q_rows], q_in.at[h]).start()
        return carry

    share_kv(0, lambda k: first_in.at[k])
    lax.fori_loop(1, heads, share_later, 0)
    lax.fori_loop(0, heads, share_q, 0)

    def await_bytes(ref, sem):
        pltpu.make_async_copy(ref, ref, sem).wait()

    def ring_copy(way, s, h):
        if way == 0:
            first, last, shift = max(0, REACH - s * frames_here), REACH - (s - 1) * frames_here, frames_here
        else:
            first = REACH + s * frames_here
            last, shift = min(frames_here + SLOTS, first + frames_here), -frames_here
        rows = (last - first) * FRAME
        return pltpu.make_async_remote_copy(
            src_ref=kv.at[h, :, pl.ds((first + shift) * FRAME, rows)],
            dst_ref=kv.at[h, :, pl.ds(first * FRAME, rows)],
            send_sem=ring_sent.at[way, s - 1, h], recv_sem=ring_in.at[way, s - 1, h],
            device_id=beside(1 if way == 0 else -1), device_id_type=MESH,
        )

    def sends(way, s):
        if way == 0:
            return (place >= s - 1) & has_right
        return (place + s <= places) & has_left

    def receives(way, s):
        return place >= s if way == 0 else place + s <= places - 1

    def ring_start(s, h):
        for way in (0, 1):
            @pl.when(sends(way, s))
            def _():
                ring_copy(way, s, h).start()

    def ring_arrived(s, h):
        for way in (0, 1):
            @pl.when(receives(way, s))
            def _():
                ring_copy(way, s, h).wait_recv()

    def attend(h):
        def one_frame(f, carry):
            own = pl.multiple_of((REACH + f) * FRAME, FRAME)
            ks[pl.ds(0, FRAME), :] = kv[h, 0, pl.ds(own, FRAME), :]
            vs[pl.ds(0, FRAME), :] = kv[h, 1, pl.ds(own, FRAME), :]

            def pick(i, carry):
                far = place * frames_here + f + i - REACH + i // REACH
                slot = jnp.minimum(jnp.maximum(far, 0), ctx - 1) - place * frames_here + REACH
                row = pl.multiple_of(slot * FRAME, FRAME)
                second = sel_ref[f, i] == 1
                to = pl.ds(pl.multiple_of(FRAME + i * BLK, BLK), BLK)
                for which, dst in ((0, ks), (1, vs)):
                    dst[to, :] = jnp.where(
                        second,
                        kv[h, which, pl.ds(row + BLK, BLK), :],
                        kv[h, which, pl.ds(row, BLK), :],
                    )
                return carry

            lax.fori_loop(0, SLOTS, pick, 0)

            def one_block(b, carry):
                rows = pl.ds(pl.multiple_of(f * FRAME + b * BLK, BLK), BLK)
                scores = lax.dot_general(
                    qb[h, rows, :], ks[...], (((1,), (1,)), ((), ())),
                    preferred_element_type=jnp.float32,
                )
                scores = scores * scale2 + bias_ref[f * BPF + b]
                weights = jnp.exp2(scores - jnp.max(scores, axis=1, keepdims=True))
                total = jnp.sum(weights, axis=1, keepdims=True)
                mixed = jnp.dot(
                    weights.astype(jnp.bfloat16), vs[...], preferred_element_type=jnp.float32
                )
                ob[h, rows, :] = (mixed / total).astype(jnp.bfloat16)
                return carry

            lax.fori_loop(0, BPF, one_block, 0)
            return carry

        lax.fori_loop(0, frames_here, one_frame, 0)

    def give_back(h):
        for k in range(1, GROUP):
            j = (me + k) % GROUP
            pltpu.make_async_remote_copy(
                src_ref=ob.at[h, pl.ds(pl.multiple_of(j * tokens, tokens), tokens)],
                dst_ref=out_ref.at[:, columns(me, h)],
                send_sem=out_sent.at[h], recv_sem=out_in.at[0],
                device_id=member(j), device_id_type=MESH,
            ).start()
        pltpu.make_async_copy(ob.at[h, q_rows], out_ref.at[:, columns(me, h)], out_in.at[0]).start()

    def step(t, carry):
        @pl.when((t >= 1) & (t < heads))
        def _():
            await_bytes(kv.at[t, :, pl.ds(REACH * FRAME, here)], kv_in.at[t])
            ring_start(1, t)

        for s in range(1, hops):
            @pl.when((t >= s) & (t < heads + s))
            def _():
                ring_arrived(s, t - s)
                ring_start(s + 1, t - s)

        @pl.when(t >= hops)
        def _():
            ring_arrived(hops, t - hops)
            await_bytes(qb.at[t - hops], q_in.at[t - hops])
            attend(t - hops)
            give_back(t - hops)

        return carry

    for k in range(GROUP):
        row = REACH * FRAME + (me + GROUP - k) % GROUP * tokens
        piece = kv.at[0, :, pl.ds(pl.multiple_of(row, tokens), tokens)]
        await_bytes(piece, first_in.at[k])
        for way in (0, 1):
            @pl.when(sends(way, 1))
            def _():
                to = row - here if way == 0 else row + here
                pltpu.make_async_remote_copy(
                    src_ref=piece, dst_ref=kv.at[0, :, pl.ds(pl.multiple_of(to, tokens), tokens)],
                    send_sem=ring_sent.at[way, 0, 0], recv_sem=ring_in.at[way, 0, 0],
                    device_id=beside(1 if way == 0 else -1), device_id_type=MESH,
                ).start()

    lax.fori_loop(0, heads + hops, step, 0)

    def finish(h, carry):
        others = (GROUP - 1) * tokens
        await_bytes(kv.at[h, :, pl.ds(0, others)], kv_sent.at[h])
        await_bytes(qb.at[h, pl.ds(0, others)], q_sent.at[h])
        await_bytes(ob.at[h, pl.ds(0, others)], out_sent.at[h])
        for s in range(1, hops + 1):
            for way in (0, 1):
                @pl.when(sends(way, s))
                def _():
                    ring_copy(way, s, h).wait_send()
        return carry

    lax.fori_loop(0, heads, finish, 0)
    await_bytes(out_ref, out_in.at[0])


def tables(kv_list, place, frames_here, frames):
    lists = lax.dynamic_slice_in_dim(kv_list, place * frames_here * BPF, frames_here * BPF, 0)
    lists = lists.reshape(frames_here, BPF, 1, -1)
    steps = jnp.array([d for d in range(-REACH, REACH + 1) if d != 0], jnp.int32)
    far = place * frames_here + jnp.arange(frames_here, dtype=jnp.int32)[:, None] + steps[None, :]
    inside = (far >= 0) & (far < frames)
    has = [jnp.any(lists == (far * BPF + b)[:, None, :, None], axis=3) for b in range(BPF)]
    listed = (has[0] | has[1]) & inside[:, None, :]
    sel = jnp.any(has[1], axis=1).astype(jnp.int32)
    bias = jnp.where(listed, 0.0, very_low).astype(jnp.float32)
    bias = jnp.concatenate([jnp.zeros((frames_here, BPF, BPF), jnp.float32), bias], axis=2)
    bias = jnp.repeat(bias.reshape(frames_here * BPF, BPF + SLOTS), BLK, axis=1)
    return sel, bias.reshape(frames_here * BPF, 1, KEYS)


def ring_attention(q_proj, k_proj, v_proj, kv_list):
    ctx, rep, uly = lax.axis_size("ctx"), lax.axis_size("rep"), lax.axis_size("uly")
    tokens, width = q_proj.shape
    heads = width // HD // GROUP
    inner = GROUP // (rep * uly)
    here = GROUP * tokens
    frames_here = here // FRAME
    hops = -(-REACH // frames_here)
    sel, bias = tables(kv_list, lax.axis_index("ctx") // inner, frames_here, ctx)
    window = (frames_here + SLOTS) * FRAME
    any_space = pl.BlockSpec(memory_space=pl.ANY)
    dma = pltpu.SemaphoreType.DMA
    return pl.pallas_call(
        functools.partial(ring_kernel, (ctx, rep, uly, tokens, heads)),
        out_shape=jax.ShapeDtypeStruct((tokens, width), jnp.bfloat16),
        in_specs=[
            pl.BlockSpec(memory_space=pltpu.SMEM),
            pl.BlockSpec(memory_space=pltpu.VMEM),
            any_space, any_space, any_space,
        ],
        out_specs=any_space,
        scratch_shapes=[
            pltpu.VMEM((heads, 2, window, HD), jnp.bfloat16),
            pltpu.VMEM((heads, here, HD), jnp.bfloat16),
            pltpu.VMEM((heads, here, HD), jnp.bfloat16),
            pltpu.VMEM((KEYS, HD), jnp.bfloat16),
            pltpu.VMEM((KEYS, HD), jnp.bfloat16),
            dma((GROUP,)), dma((heads,)), dma((heads,)), dma((heads,)), dma((heads,)),
            dma((2, hops, heads)), dma((2, hops, heads)), dma((1,)), dma((heads,)),
        ],
        compiler_params=pltpu.CompilerParams(
            collective_id=0, has_side_effects=True, vmem_limit_bytes=56 * 1024 * 1024
        ),
    )(sel, bias, q_proj, k_proj, v_proj)


PLANE = 4
NEAR = 3 * PLANE * FRAME
NEAR_KEYS = NEAR // 2 + BLK
FAR_SLOTS = 3
FAR = (2 * FAR_SLOTS - 1) * BLK
FAR_KEYS = FAR_SLOTS * BLK
STEPS = 2 * REACH + 1
PEERS = (2, 1, 3, 4, 6, 5, 7)


def plane_kernel(ctx, heads, list_ref, q_ref, k_ref, v_ref, out_ref,
                 lists, sel, listed, bias_near, bias_far, near, far, chosen, qb, ob, part, high, low, ks, vs,
                 list_in, beside_in, plane_in, q_in, ring_in, far_in, out_in,
                 plane_sent, q_sent, ring_sent, far_sent, out_sent):
    here = PLANE * FRAME
    places = ctx // PLANE
    c = lax.axis_index("ctx")
    u = lax.axis_index("uly")
    place = c // PLANE
    me = (c % PLANE) * BPF + u

    def member(j):
        return {"ctx": place * PLANE + j // BPF, "uly": j % BPF}

    def beside(way):
        return {"ctx": c + (PLANE if way == 0 else -PLANE)}

    def peer(k):
        bits = (me % 2, (me // 2) % 2, me // 4)
        return sum((1 - bit if (k >> n) & 1 else bit) << n for n, bit in enumerate(bits))

    has = (place <= places - 2, place >= 1)
    gets = (place >= 1, place <= places - 2)
    sends_far = ((place >= 1) & (place <= places - 2),) * 2
    gets_far = (place >= 2, place <= places - 3)

    barrier = pltpu.get_barrier_semaphore()
    for way in (0, 1):
        @pl.when(has[way])
        def _():
            pl.semaphore_signal(barrier, inc=1, device_id=beside(way), device_id_type=MESH)
    for k in PEERS:
        pl.semaphore_signal(barrier, inc=1, device_id=member(peer(k)), device_id_type=MESH)
    neighbours = jnp.minimum(place, 1) + jnp.minimum(places - 1 - place, 1)
    pl.semaphore_wait(barrier, GROUP - 1 + neighbours)

    def columns(owner, h):
        return pl.ds(pl.multiple_of((owner * heads + h) * HD, HD), HD)

    def rows_of(j, base=0):
        return pl.ds(pl.multiple_of(base + j * BLK, BLK), BLK)

    def await_bytes(ref, sem):
        pltpu.make_async_copy(ref, ref, sem).wait()

    lands = (0, 2 * here)

    def ring_own(h, carry):
        for way in (0, 1):
            @pl.when(has[way])
            def _():
                for which, src in enumerate((k_ref, v_ref)):
                    pltpu.make_async_remote_copy(
                        src_ref=src.at[:, columns(me, h)], dst_ref=near.at[h, which, rows_of(me, lands[way])],
                        send_sem=ring_sent.at[way, h], recv_sem=ring_in.at[way, h],
                        device_id=beside(way), device_id_type=MESH,
                    ).start()
        return carry

    def ring_piece(h, j):
        for way in (0, 1):
            @pl.when(has[way])
            def _():
                pltpu.make_async_remote_copy(
                    src_ref=near.at[h, :, rows_of(j, here)], dst_ref=near.at[h, :, rows_of(j, lands[way])],
                    send_sem=ring_sent.at[way, h], recv_sem=ring_in.at[way, h],
                    device_id=beside(way), device_id_type=MESH,
                ).start()

    def share_kv(h, carry):
        for k in PEERS:
            j = peer(k)
            for which, src in enumerate((k_ref, v_ref)):
                pltpu.make_async_remote_copy(
                    src_ref=src.at[:, columns(j, h)], dst_ref=near.at[h, which, rows_of(me, here)],
                    send_sem=plane_sent.at[h], recv_sem=(beside_in if k == 2 else plane_in).at[h],
                    device_id=member(j), device_id_type=MESH,
                ).start()
        for which, src in enumerate((k_ref, v_ref)):
            pltpu.make_async_copy(
                src.at[:, columns(me, h)], near.at[h, which, rows_of(me, here)], plane_in.at[h]
            ).start()
        return carry

    def share_q(h, carry):
        for k in PEERS:
            j = peer(k)
            pltpu.make_async_remote_copy(
                src_ref=q_ref.at[:, columns(j, h)], dst_ref=qb.at[h, rows_of(me)],
                send_sem=q_sent.at[h], recv_sem=q_in.at[h],
                device_id=member(j), device_id_type=MESH,
            ).start()
        pltpu.make_async_copy(q_ref.at[:, columns(me, h)], qb.at[h, rows_of(me)], q_in.at[h]).start()
        return carry

    lax.fori_loop(0, heads, ring_own, 0)
    lax.fori_loop(0, heads, share_kv, 0)
    lax.fori_loop(0, heads, share_q, 0)
    get_lists = pltpu.make_async_copy(list_ref, lists, list_in.at[0])
    get_lists.start()

    def ring_beside(h, carry):
        await_bytes(near.at[h, :, pl.ds(here, BLK)], beside_in.at[h])
        ring_piece(h, peer(2))
        return carry

    lax.fori_loop(0, heads, ring_beside, 0)

    for way in (0, 1):
        @pl.when(jnp.logical_not(gets[way]))
        def _():
            def clear(h, carry):
                for which in (0, 1):
                    near[h, which, pl.ds(lands[way], here), :] = jnp.zeros((here, HD), jnp.bfloat16)
                return carry

            lax.fori_loop(0, heads, clear, 0)

        @pl.when(jnp.logical_not(gets_far[way]))
        def _():
            def clear(h, carry):
                for which in (0, 1):
                    far[h, way, which] = jnp.zeros((FAR, HD), jnp.bfloat16)
                return carry

            lax.fori_loop(0, heads, clear, 0)

    get_lists.wait()

    def count(row, block):
        return sum((lists[j, row] == block).astype(jnp.int32) for j in range(lists.shape[0]))

    def tables(n, carry):
        a, d = n // STEPS, n % STEPS
        target = place * PLANE + a + d - REACH
        block = jnp.where(target < 0, -BLK, target * BPF)
        second = 0
        for b in range(BPF):
            row = (place * PLANE + a) * BPF + b
            one = count(row, block + 1)
            listed[a * BPF + b, d] = jnp.minimum(count(row, block) + one, 1)
            second = second + one
        sel[a, d] = jnp.minimum(second, 1)
        return carry

    lax.fori_loop(0, PLANE * STEPS, tables, 0)

    def fill(ref, r, slot, d):
        value = jnp.where(listed[r, d] == 1, 0.0, very_low)
        ref[r, :, pl.ds(pl.multiple_of(slot * BLK, BLK), BLK)] = jnp.full((1, BLK), value, jnp.float32)

    def biases(r, carry):
        a = r // BPF
        bias_near[r, :, pl.ds(0, FRAME)] = jnp.zeros((1, FRAME), jnp.float32)

        def one_near(i, carry):
            w = i + (i + REACH - PLANE - a) // REACH
            fill(bias_near, r, BPF + i, jnp.minimum(w + REACH - PLANE - a, STEPS - 1))
            return carry

        def one_far(i, carry):
            right = (i + a) // FAR_SLOTS
            fill(bias_far, r, i, i + right * (STEPS - FAR_SLOTS))
            return carry

        lax.fori_loop(0, 3 * PLANE - 1, one_near, 0)
        lax.fori_loop(0, FAR_SLOTS, one_far, 0)
        return carry

    lax.fori_loop(0, PLANE * BPF, biases, 0)

    def ring_rest(h, carry):
        await_bytes(near.at[h, :, pl.ds(here, here - BLK)], plane_in.at[h])
        for k in PEERS[1:]:
            ring_piece(h, peer(k))
        return carry

    lax.fori_loop(0, heads, ring_rest, 0)

    frames = ctx
    onward = (
        (jnp.minimum((place + 1) * PLANE, frames - 1), place * PLANE - PLANE + 1),
        (jnp.maximum((place - 1) * PLANE + PLANE - 1, 0), place * PLANE + PLANE + 2),
    )
    takes_second = [
        (count(f * BPF, g * BPF + 1) + count(f * BPF + 1, g * BPF + 1)) > 0 for f, g in onward
    ]

    def far_copy(way, n, h):
        b = 3 - n if way == 0 else 2 * PLANE + n
        whole = n < FAR_SLOTS - 1
        rows = FRAME if whole else BLK
        return pltpu.make_async_remote_copy(
            src_ref=near.at[h, :, pl.ds(b * FRAME, rows)] if whole else chosen.at[h, way],
            dst_ref=far.at[h, way, :, pl.ds(n * FRAME, rows)],
            send_sem=far_sent.at[way, n, h], recv_sem=far_in.at[way, n, h],
            device_id=beside(way), device_id_type=MESH,
        )

    def attend_near(h):
        def one_frame(a, carry):
            own = pl.multiple_of((PLANE + a) * FRAME, FRAME)
            ks[pl.ds(0, FRAME), :] = near[h, 0, pl.ds(own, FRAME), :]
            vs[pl.ds(0, FRAME), :] = near[h, 1, pl.ds(own, FRAME), :]

            def pick(i, carry):
                w = i + (i + REACH - PLANE - a) // REACH
                row = pl.multiple_of(w * FRAME, FRAME)
                second = sel[a, jnp.minimum(w + REACH - PLANE - a, STEPS - 1)] == 1
                to = pl.ds(pl.multiple_of(FRAME + i * BLK, BLK), BLK)
                for which, dst in ((0, ks), (1, vs)):
                    dst[to, :] = jnp.where(
                        second, near[h, which, pl.ds(row + BLK, BLK), :], near[h, which, pl.ds(row, BLK), :]
                    )
                return carry

            lax.fori_loop(0, 3 * PLANE - 1, pick, 0)
            rows = pl.ds(pl.multiple_of(a * FRAME, FRAME), FRAME)
            scores = lax.dot_general(
                qb[h, rows, :], ks[...], (((1,), (1,)), ((), ())), preferred_element_type=jnp.float32
            ).reshape(BPF, BLK, NEAR_KEYS)
            scores = scores * scale2 + bias_near[pl.ds(a * BPF, BPF)]
            top = jnp.max(scores, axis=2, keepdims=True)
            weights = jnp.exp2(scores - top)
            total = jnp.sum(weights, axis=2, keepdims=True)
            part[h, rows, :] = jnp.dot(
                weights.reshape(FRAME, NEAR_KEYS).astype(jnp.bfloat16), vs[...],
                preferred_element_type=jnp.float32,
            )
            high[h, rows, :] = jnp.broadcast_to(top, (BPF, BLK, HD)).reshape(FRAME, HD)
            low[h, rows, :] = jnp.broadcast_to(total, (BPF, BLK, HD)).reshape(FRAME, HD)
            return carry

        lax.fori_loop(0, PLANE, one_frame, 0)

    def attend_far(h, a):
        def pick(i, carry):
            right = (i + a) // FAR_SLOTS
            pair = (1 - right) * (FAR_SLOTS - 1 - a - i) + right * (i + a - FAR_SLOTS)
            whole = 1 - pair // (FAR_SLOTS - 1)
            row = pl.multiple_of(pair * FRAME, FRAME)
            row_b = pl.multiple_of(pair * FRAME + whole * BLK, BLK)
            second = sel[a, i + right * (STEPS - FAR_SLOTS)] == 1
            to = pl.ds(pl.multiple_of(i * BLK, BLK), BLK)
            for which, dst in ((0, ks), (1, vs)):
                dst[to, :] = jnp.where(
                    second, far[h, right, which, pl.ds(row_b, BLK), :], far[h, right, which, pl.ds(row, BLK), :]
                )
            return carry

        lax.fori_loop(0, FAR_SLOTS, pick, 0)
        rows = pl.ds(pl.multiple_of(a * FRAME, FRAME), FRAME)
        keys = pl.ds(0, FAR_KEYS)
        scores = lax.dot_general(
            qb[h, rows, :], ks[keys, :], (((1,), (1,)), ((), ())), preferred_element_type=jnp.float32
        ).reshape(BPF, BLK, FAR_KEYS)
        scores = (scores * scale2 + bias_far[pl.ds(a * BPF, BPF)]).reshape(FRAME, FAR_KEYS)
        before = high[h, rows, :]
        top = jnp.maximum(before, jnp.max(scores, axis=1, keepdims=True))
        weights = jnp.exp2(scores - jnp.concatenate([top] * FAR_SLOTS, axis=1))
        fade = jnp.exp2(before - top)
        total = fade * low[h, rows, :] + jnp.sum(weights, axis=1, keepdims=True)
        mixed = fade * part[h, rows, :] + jnp.dot(
            weights.astype(jnp.bfloat16), vs[keys, :], preferred_element_type=jnp.float32
        )
        ob[h, rows, :] = (mixed / total).astype(jnp.bfloat16)

    def give_back(h, a):
        for b in range(BPF):
            j = a * BPF + b

            @pl.when(j != me)
            def _():
                pltpu.make_async_remote_copy(
                    src_ref=ob.at[h, rows_of(j)], dst_ref=out_ref.at[:, columns(me, h)],
                    send_sem=out_sent.at[h], recv_sem=out_in.at[0],
                    device_id=member(j), device_id_type=MESH,
                ).start()

            @pl.when(j == me)
            def _():
                pltpu.make_async_copy(ob.at[h, rows_of(j)], out_ref.at[:, columns(me, h)], out_in.at[0]).start()

    def first_phase(h, carry):
        for way in (0, 1):
            @pl.when(gets[way])
            def _():
                await_bytes(near.at[h, :, pl.ds(lands[way], here)], ring_in.at[way, h])

        for way in (0, 1):
            @pl.when(sends_far[way])
            def _():
                frame = 1 if way == 0 else 2 * PLANE + 2
                for which in (0, 1):
                    chosen[h, way, which] = jnp.where(
                        takes_second[way],
                        near[h, which, pl.ds(frame * FRAME + BLK, BLK), :],
                        near[h, which, pl.ds(frame * FRAME, BLK), :],
                    )
                for n in range(FAR_SLOTS):
                    far_copy(way, n, h).start()

        await_bytes(qb.at[h], q_in.at[h])
        attend_near(h)
        return carry

    lax.fori_loop(0, heads, first_phase, 0)

    both = gets_far[0] & gets_far[1]
    falling = jnp.where(gets_far[0], 1, 0)

    def second_phase(h, carry):
        for way in (0, 1):
            @pl.when(both)
            def _():
                for n in range(FAR_SLOTS):
                    far_copy(way, n, h).wait_recv()

        for n in range(PLANE):
            if n >= 1:
                for way in (0, 1):
                    @pl.when(gets_far[way] & jnp.logical_not(both))
                    def _():
                        far_copy(way, n - 1, h).wait_recv()
            a = falling * (PLANE - 1 - n) + (1 - falling) * n
            attend_far(h, a)
            give_back(h, a)
        return carry

    lax.fori_loop(0, heads, second_phase, 0)

    def finish(h, carry):
        others = (GROUP - 1) * BLK
        await_bytes(near.at[h, :, pl.ds(0, others)], plane_sent.at[h])
        await_bytes(qb.at[h, pl.ds(0, others)], q_sent.at[h])
        await_bytes(ob.at[h, pl.ds(0, others)], out_sent.at[h])
        for way in (0, 1):
            @pl.when(has[way])
            def _():
                await_bytes(near.at[h, :, pl.ds(0, here)], ring_sent.at[way, h])

            @pl.when(sends_far[way])
            def _():
                for n in range(FAR_SLOTS):
                    far_copy(way, n, h).wait_send()
        return carry

    lax.fori_loop(0, heads, finish, 0)
    await_bytes(out_ref, out_in.at[0])


def plane_attention(q_proj, k_proj, v_proj, kv_list):
    ctx = lax.axis_size("ctx")
    tokens, width = q_proj.shape
    heads = width // HD // GROUP
    here = PLANE * FRAME
    lists = kv_list.T
    any_space = pl.BlockSpec(memory_space=pl.ANY)
    dma = pltpu.SemaphoreType.DMA
    bf16, f32 = jnp.bfloat16, jnp.float32
    return pl.pallas_call(
        functools.partial(plane_kernel, ctx, heads),
        out_shape=jax.ShapeDtypeStruct((tokens, width), bf16),
        in_specs=[any_space] * 4,
        out_specs=any_space,
        scratch_shapes=[
            pltpu.SMEM(lists.shape, jnp.int32),
            pltpu.SMEM((PLANE, STEPS), jnp.int32),
            pltpu.SMEM((PLANE * BPF, STEPS), jnp.int32),
            pltpu.VMEM((PLANE * BPF, 1, NEAR_KEYS), f32),
            pltpu.VMEM((PLANE * BPF, 1, FAR_KEYS), f32),
            pltpu.VMEM((heads, 2, NEAR, HD), bf16),
            pltpu.VMEM((heads, 2, 2, FAR, HD), bf16),
            pltpu.VMEM((heads, 2, 2, BLK, HD), bf16),
            pltpu.VMEM((heads, here, HD), bf16),
            pltpu.VMEM((heads, here, HD), bf16),
            pltpu.VMEM((heads, here, HD), f32),
            pltpu.VMEM((heads, here, HD), f32),
            pltpu.VMEM((heads, here, HD), f32),
            pltpu.VMEM((NEAR_KEYS, HD), bf16),
            pltpu.VMEM((NEAR_KEYS, HD), bf16),
            dma((1,)), dma((heads,)), dma((heads,)), dma((heads,)), dma((2, heads)),
            dma((2, FAR_SLOTS, heads)), dma((1,)),
            dma((heads,)), dma((heads,)), dma((2, heads)), dma((2, FAR_SLOTS, heads)), dma((heads,)),
        ],
        compiler_params=pltpu.CompilerParams(
            collective_id=0, has_side_effects=True, vmem_limit_bytes=56 * 1024 * 1024
        ),
    )(lists, q_proj, k_proj, v_proj)


def on_device(q_proj, k_proj, v_proj, kv_list):
    rep, uly = lax.axis_size("rep"), lax.axis_size("uly")
    if rep == 1 and uly == BPF and q_proj.shape[0] == BLK and lax.axis_size("ctx") % PLANE == 0:
        return plane_attention(q_proj, k_proj, v_proj, kv_list)
    return ring_attention(q_proj, k_proj, v_proj, kv_list)


def solution(mesh):
    rows = P(("groups", "ctx", "rep", "uly"), None)
    return jax.shard_map(
        on_device,
        mesh=mesh,
        in_specs=(rows, rows, rows, P("groups", None)),
        out_specs=rows,
        check_vma=False,
    )
```

```python
import functools
import math

import jax
import jax.numpy as jnp
from jax import lax
from jax.experimental import pallas as pl
from jax.experimental.pallas import tpu as pltpu
from jax.sharding import PartitionSpec as P

HD = 128
BLK = 128
BPF = 2
FRAME = BLK * BPF
REACH = 7
GROUP = 8
SLOTS = 2 * REACH
KEYS = (SLOTS + BPF) * BLK

very_low = -1e30
scale2 = math.log2(math.e) / math.sqrt(HD)
MESH = pl.DeviceIdType.MESH


def ring_kernel(sizes, sel_ref, bias_ref, q_ref, k_ref, v_ref, out_ref, kv, qb, ob, ks, vs,
           first_in, kv_in, q_in, kv_sent, q_sent, ring_in, ring_sent, out_in, out_sent):
    ctx, rep, uly, tokens, heads = sizes
    inner = GROUP // (rep * uly)
    here = GROUP * tokens
    frames_here = here // FRAME
    places = ctx // inner
    hops = -(-REACH // frames_here)
    c = lax.axis_index("ctx")
    r = lax.axis_index("rep")
    u = lax.axis_index("uly")
    place = c // inner
    me = (c % inner) * (rep * uly) + r * uly + u

    def member(j):
        return {"ctx": place * inner + j // (rep * uly), "rep": (j // uly) % rep, "uly": j % uly}

    def beside(step):
        return {"ctx": c + step * inner}

    has_left, has_right = place >= 1, place <= places - 2

    barrier = pltpu.get_barrier_semaphore()
    for k in range(1, GROUP):
        pl.semaphore_signal(barrier, inc=1, device_id=member((me + k) % GROUP), device_id_type=MESH)

    @pl.when(has_left)
    def _():
        pl.semaphore_signal(barrier, inc=1, device_id=beside(-1), device_id_type=MESH)

    @pl.when(has_right)
    def _():
        pl.semaphore_signal(barrier, inc=1, device_id=beside(1), device_id_type=MESH)

    neighbours = jnp.minimum(place, 1) + jnp.minimum(places - 1 - place, 1)
    pl.semaphore_wait(barrier, GROUP - 1 + neighbours)

    def columns(owner, h):
        return pl.ds(pl.multiple_of((owner * heads + h) * HD, HD), HD)

    own_rows = pl.ds(pl.multiple_of(REACH * FRAME + me * tokens, tokens), tokens)
    q_rows = pl.ds(pl.multiple_of(me * tokens, tokens), tokens)

    def share_kv(h, arrived):
        for k in range(1, GROUP):
            j = (me + k) % GROUP
            for which, src in enumerate((k_ref, v_ref)):
                pltpu.make_async_remote_copy(
                    src_ref=src.at[:, columns(j, h)], dst_ref=kv.at[h, which, own_rows],
                    send_sem=kv_sent.at[h], recv_sem=arrived(k),
                    device_id=member(j), device_id_type=MESH,
                ).start()
        for which, src in enumerate((k_ref, v_ref)):
            pltpu.make_async_copy(
                src.at[:, columns(me, h)], kv.at[h, which, own_rows], arrived(0)
            ).start()

    def share_later(h, carry):
        share_kv(h, lambda k: kv_in.at[h])
        return carry

    def share_q(h, carry):
        for k in range(1, GROUP):
            j = (me + k) % GROUP
            pltpu.make_async_remote_copy(
                src_ref=q_ref.at[:, columns(j, h)], dst_ref=qb.at[h, q_rows],
                send_sem=q_sent.at[h], recv_sem=q_in.at[h],
                device_id=member(j), device_id_type=MESH,
            ).start()
        pltpu.make_async_copy(q_ref.at[:, columns(me, h)], qb.at[h, q_rows], q_in.at[h]).start()
        return carry

    share_kv(0, lambda k: first_in.at[k])
    lax.fori_loop(1, heads, share_later, 0)
    lax.fori_loop(0, heads, share_q, 0)

    def await_bytes(ref, sem):
        pltpu.make_async_copy(ref, ref, sem).wait()

    def ring_copy(way, s, h):
        if way == 0:
            first, last, shift = max(0, REACH - s * frames_here), REACH - (s - 1) * frames_here, frames_here
        else:
            first = REACH + s * frames_here
            last, shift = min(frames_here + SLOTS, first + frames_here), -frames_here
        rows = (last - first) * FRAME
        return pltpu.make_async_remote_copy(
            src_ref=kv.at[h, :, pl.ds((first + shift) * FRAME, rows)],
            dst_ref=kv.at[h, :, pl.ds(first * FRAME, rows)],
            send_sem=ring_sent.at[way, s - 1, h], recv_sem=ring_in.at[way, s - 1, h],
            device_id=beside(1 if way == 0 else -1), device_id_type=MESH,
        )

    def sends(way, s):
        if way == 0:
            return (place >= s - 1) & has_right
        return (place + s <= places) & has_left

    def receives(way, s):
        return place >= s if way == 0 else place + s <= places - 1

    def ring_start(s, h):
        for way in (0, 1):
            @pl.when(sends(way, s))
            def _():
                ring_copy(way, s, h).start()

    def ring_arrived(s, h):
        for way in (0, 1):
            @pl.when(receives(way, s))
            def _():
                ring_copy(way, s, h).wait_recv()

    def attend(h):
        def one_frame(f, carry):
            own = pl.multiple_of((REACH + f) * FRAME, FRAME)
            ks[pl.ds(0, FRAME), :] = kv[h, 0, pl.ds(own, FRAME), :]
            vs[pl.ds(0, FRAME), :] = kv[h, 1, pl.ds(own, FRAME), :]

            def pick(i, carry):
                far = place * frames_here + f + i - REACH + i // REACH
                slot = jnp.minimum(jnp.maximum(far, 0), ctx - 1) - place * frames_here + REACH
                row = pl.multiple_of(slot * FRAME, FRAME)
                second = sel_ref[f, i] == 1
                to = pl.ds(pl.multiple_of(FRAME + i * BLK, BLK), BLK)
                for which, dst in ((0, ks), (1, vs)):
                    dst[to, :] = jnp.where(
                        second,
                        kv[h, which, pl.ds(row + BLK, BLK), :],
                        kv[h, which, pl.ds(row, BLK), :],
                    )
                return carry

            lax.fori_loop(0, SLOTS, pick, 0)

            def one_block(b, carry):
                rows = pl.ds(pl.multiple_of(f * FRAME + b * BLK, BLK), BLK)
                scores = lax.dot_general(
                    qb[h, rows, :], ks[...], (((1,), (1,)), ((), ())),
                    preferred_element_type=jnp.float32,
                )
                scores = scores * scale2 + bias_ref[f * BPF + b]
                weights = jnp.exp2(scores - jnp.max(scores, axis=1, keepdims=True))
                total = jnp.sum(weights, axis=1, keepdims=True)
                mixed = jnp.dot(
                    weights.astype(jnp.bfloat16), vs[...], preferred_element_type=jnp.float32
                )
                ob[h, rows, :] = (mixed / total).astype(jnp.bfloat16)
                return carry

            lax.fori_loop(0, BPF, one_block, 0)
            return carry

        lax.fori_loop(0, frames_here, one_frame, 0)

    def give_back(h):
        for k in range(1, GROUP):
            j = (me + k) % GROUP
            pltpu.make_async_remote_copy(
                src_ref=ob.at[h, pl.ds(pl.multiple_of(j * tokens, tokens), tokens)],
                dst_ref=out_ref.at[:, columns(me, h)],
                send_sem=out_sent.at[h], recv_sem=out_in.at[0],
                device_id=member(j), device_id_type=MESH,
            ).start()
        pltpu.make_async_copy(ob.at[h, q_rows], out_ref.at[:, columns(me, h)], out_in.at[0]).start()

    def step(t, carry):
        @pl.when((t >= 1) & (t < heads))
        def _():
            await_bytes(kv.at[t, :, pl.ds(REACH * FRAME, here)], kv_in.at[t])
            ring_start(1, t)

        for s in range(1, hops):
            @pl.when((t >= s) & (t < heads + s))
            def _():
                ring_arrived(s, t - s)
                ring_start(s + 1, t - s)

        @pl.when(t >= hops)
        def _():
            ring_arrived(hops, t - hops)
            await_bytes(qb.at[t - hops], q_in.at[t - hops])
            attend(t - hops)
            give_back(t - hops)

        return carry

    for k in range(GROUP):
        row = REACH * FRAME + (me + GROUP - k) % GROUP * tokens
        piece = kv.at[0, :, pl.ds(pl.multiple_of(row, tokens), tokens)]
        await_bytes(piece, first_in.at[k])
        for way in (0, 1):
            @pl.when(sends(way, 1))
            def _():
                to = row - here if way == 0 else row + here
                pltpu.make_async_remote_copy(
                    src_ref=piece, dst_ref=kv.at[0, :, pl.ds(pl.multiple_of(to, tokens), tokens)],
                    send_sem=ring_sent.at[way, 0, 0], recv_sem=ring_in.at[way, 0, 0],
                    device_id=beside(1 if way == 0 else -1), device_id_type=MESH,
                ).start()

    lax.fori_loop(0, heads + hops, step, 0)

    def finish(h, carry):
        others = (GROUP - 1) * tokens
        await_bytes(kv.at[h, :, pl.ds(0, others)], kv_sent.at[h])
        await_bytes(qb.at[h, pl.ds(0, others)], q_sent.at[h])
        await_bytes(ob.at[h, pl.ds(0, others)], out_sent.at[h])
        for s in range(1, hops + 1):
            for way in (0, 1):
                @pl.when(sends(way, s))
                def _():
                    ring_copy(way, s, h).wait_send()
        return carry

    lax.fori_loop(0, heads, finish, 0)
    await_bytes(out_ref, out_in.at[0])


def tables(kv_list, place, frames_here, frames):
    lists = lax.dynamic_slice_in_dim(kv_list, place * frames_here * BPF, frames_here * BPF, 0)
    lists = lists.reshape(frames_here, BPF, 1, -1)
    steps = jnp.array([d for d in range(-REACH, REACH + 1) if d != 0], jnp.int32)
    far = place * frames_here + jnp.arange(frames_here, dtype=jnp.int32)[:, None] + steps[None, :]
    inside = (far >= 0) & (far < frames)
    has = [jnp.any(lists == (far * BPF + b)[:, None, :, None], axis=3) for b in range(BPF)]
    listed = (has[0] | has[1]) & inside[:, None, :]
    sel = jnp.any(has[1], axis=1).astype(jnp.int32)
    bias = jnp.where(listed, 0.0, very_low).astype(jnp.float32)
    bias = jnp.concatenate([jnp.zeros((frames_here, BPF, BPF), jnp.float32), bias], axis=2)
    bias = jnp.repeat(bias.reshape(frames_here * BPF, BPF + SLOTS), BLK, axis=1)
    return sel, bias.reshape(frames_here * BPF, 1, KEYS)


def ring_attention(q_proj, k_proj, v_proj, kv_list):
    ctx, rep, uly = lax.axis_size("ctx"), lax.axis_size("rep"), lax.axis_size("uly")
    tokens, width = q_proj.shape
    heads = width // HD // GROUP
    inner = GROUP // (rep * uly)
    here = GROUP * tokens
    frames_here = here // FRAME
    hops = -(-REACH // frames_here)
    sel, bias = tables(kv_list, lax.axis_index("ctx") // inner, frames_here, ctx)
    window = (frames_here + SLOTS) * FRAME
    any_space = pl.BlockSpec(memory_space=pl.ANY)
    dma = pltpu.SemaphoreType.DMA
    return pl.pallas_call(
        functools.partial(ring_kernel, (ctx, rep, uly, tokens, heads)),
        out_shape=jax.ShapeDtypeStruct((tokens, width), jnp.bfloat16),
        in_specs=[
            pl.BlockSpec(memory_space=pltpu.SMEM),
            pl.BlockSpec(memory_space=pltpu.VMEM),
            any_space, any_space, any_space,
        ],
        out_specs=any_space,
        scratch_shapes=[
            pltpu.VMEM((heads, 2, window, HD), jnp.bfloat16),
            pltpu.VMEM((heads, here, HD), jnp.bfloat16),
            pltpu.VMEM((heads, here, HD), jnp.bfloat16),
            pltpu.VMEM((KEYS, HD), jnp.bfloat16),
            pltpu.VMEM((KEYS, HD), jnp.bfloat16),
            dma((GROUP,)), dma((heads,)), dma((heads,)), dma((heads,)), dma((heads,)),
            dma((2, hops, heads)), dma((2, hops, heads)), dma((1,)), dma((heads,)),
        ],
        compiler_params=pltpu.CompilerParams(
            collective_id=0, has_side_effects=True, vmem_limit_bytes=56 * 1024 * 1024
        ),
    )(sel, bias, q_proj, k_proj, v_proj)


PLANE = 4
NEAR = 3 * PLANE * FRAME
NEAR_KEYS = NEAR // 2 + BLK
FAR_SLOTS = 3
FAR = (2 * FAR_SLOTS - 1) * BLK
FAR_KEYS = FAR_SLOTS * BLK
STEPS = 2 * REACH + 1
PEERS = (2, 1, 3, 4, 6, 5, 7)


def plane_kernel(ctx, heads, list_ref, q_ref, k_ref, v_ref, out_ref,
                 lists, sel, listed, bias_near, bias_far, near, far, chosen, qb, ob, part, high, low, ks, vs,
                 list_in, beside_in, plane_in, q_in, ring_in, far_in, out_in,
                 plane_sent, q_sent, ring_sent, far_sent, out_sent):
    here = PLANE * FRAME
    places = ctx // PLANE
    c = lax.axis_index("ctx")
    u = lax.axis_index("uly")
    place = c // PLANE
    me = (c % PLANE) * BPF + u

    def member(j):
        return {"ctx": place * PLANE + j // BPF, "uly": j % BPF}

    def beside(way):
        return {"ctx": c + (PLANE if way == 0 else -PLANE)}

    def peer(k):
        bits = (me % 2, (me // 2) % 2, me // 4)
        return sum((1 - bit if (k >> n) & 1 else bit) << n for n, bit in enumerate(bits))

    has = (place <= places - 2, place >= 1)
    gets = (place >= 1, place <= places - 2)
    sends_far = ((place >= 1) & (place <= places - 2),) * 2
    gets_far = (place >= 2, place <= places - 3)

    barrier = pltpu.get_barrier_semaphore()
    for way in (0, 1):
        @pl.when(has[way])
        def _():
            pl.semaphore_signal(barrier, inc=1, device_id=beside(way), device_id_type=MESH)
    for k in PEERS:
        pl.semaphore_signal(barrier, inc=1, device_id=member(peer(k)), device_id_type=MESH)
    neighbours = jnp.minimum(place, 1) + jnp.minimum(places - 1 - place, 1)
    pl.semaphore_wait(barrier, GROUP - 1 + neighbours)

    def columns(owner, h):
        return pl.ds(pl.multiple_of((owner * heads + h) * HD, HD), HD)

    def rows_of(j, base=0):
        return pl.ds(pl.multiple_of(base + j * BLK, BLK), BLK)

    def await_bytes(ref, sem):
        pltpu.make_async_copy(ref, ref, sem).wait()

    lands = (0, 2 * here)

    def ring_own(h, carry):
        for way in (0, 1):
            @pl.when(has[way])
            def _():
                for which, src in enumerate((k_ref, v_ref)):
                    pltpu.make_async_remote_copy(
                        src_ref=src.at[:, columns(me, h)], dst_ref=near.at[h, which, rows_of(me, lands[way])],
                        send_sem=ring_sent.at[way, h], recv_sem=ring_in.at[way, h],
                        device_id=beside(way), device_id_type=MESH,
                    ).start()
        return carry

    def ring_piece(h, j):
        for way in (0, 1):
            @pl.when(has[way])
            def _():
                pltpu.make_async_remote_copy(
                    src_ref=near.at[h, :, rows_of(j, here)], dst_ref=near.at[h, :, rows_of(j, lands[way])],
                    send_sem=ring_sent.at[way, h], recv_sem=ring_in.at[way, h],
                    device_id=beside(way), device_id_type=MESH,
                ).start()

    def share_kv(h, carry):
        for k in PEERS:
            j = peer(k)
            for which, src in enumerate((k_ref, v_ref)):
                pltpu.make_async_remote_copy(
                    src_ref=src.at[:, columns(j, h)], dst_ref=near.at[h, which, rows_of(me, here)],
                    send_sem=plane_sent.at[h], recv_sem=(beside_in if k == 2 else plane_in).at[h],
                    device_id=member(j), device_id_type=MESH,
                ).start()
        for which, src in enumerate((k_ref, v_ref)):
            pltpu.make_async_copy(
                src.at[:, columns(me, h)], near.at[h, which, rows_of(me, here)], plane_in.at[h]
            ).start()
        return carry

    def share_q(h, carry):
        for k in PEERS:
            j = peer(k)
            pltpu.make_async_remote_copy(
                src_ref=q_ref.at[:, columns(j, h)], dst_ref=qb.at[h, rows_of(me)],
                send_sem=q_sent.at[h], recv_sem=q_in.at[h],
                device_id=member(j), device_id_type=MESH,
            ).start()
        pltpu.make_async_copy(q_ref.at[:, columns(me, h)], qb.at[h, rows_of(me)], q_in.at[h]).start()
        return carry

    lax.fori_loop(0, heads, ring_own, 0)
    lax.fori_loop(0, heads, share_kv, 0)
    lax.fori_loop(0, heads, share_q, 0)
    get_lists = pltpu.make_async_copy(list_ref, lists, list_in.at[0])
    get_lists.start()

    def ring_beside(h, carry):
        await_bytes(near.at[h, :, pl.ds(here, BLK)], beside_in.at[h])
        ring_piece(h, peer(2))
        return carry

    lax.fori_loop(0, heads, ring_beside, 0)

    for way in (0, 1):
        @pl.when(jnp.logical_not(gets[way]))
        def _():
            def clear(h, carry):
                for which in (0, 1):
                    near[h, which, pl.ds(lands[way], here), :] = jnp.zeros((here, HD), jnp.bfloat16)
                return carry

            lax.fori_loop(0, heads, clear, 0)

        @pl.when(jnp.logical_not(gets_far[way]))
        def _():
            def clear(h, carry):
                for which in (0, 1):
                    far[h, way, which] = jnp.zeros((FAR, HD), jnp.bfloat16)
                return carry

            lax.fori_loop(0, heads, clear, 0)

    get_lists.wait()

    def count(row, block):
        return sum((lists[j, row] == block).astype(jnp.int32) for j in range(lists.shape[0]))

    def tables(n, carry):
        a, d = n // STEPS, n % STEPS
        target = place * PLANE + a + d - REACH
        block = jnp.where(target < 0, -BLK, target * BPF)
        second = 0
        for b in range(BPF):
            row = (place * PLANE + a) * BPF + b
            one = count(row, block + 1)
            listed[a * BPF + b, d] = jnp.minimum(count(row, block) + one, 1)
            second = second + one
        sel[a, d] = jnp.minimum(second, 1)
        return carry

    lax.fori_loop(0, PLANE * STEPS, tables, 0)

    def fill(ref, r, slot, d):
        value = jnp.where(listed[r, d] == 1, 0.0, very_low)
        ref[r, :, pl.ds(pl.multiple_of(slot * BLK, BLK), BLK)] = jnp.full((1, BLK), value, jnp.float32)

    def biases(r, carry):
        a = r // BPF
        bias_near[r, :, pl.ds(0, FRAME)] = jnp.zeros((1, FRAME), jnp.float32)

        def one_near(i, carry):
            w = i + (i + REACH - PLANE - a) // REACH
            fill(bias_near, r, BPF + i, jnp.minimum(w + REACH - PLANE - a, STEPS - 1))
            return carry

        def one_far(i, carry):
            right = (i + a) // FAR_SLOTS
            fill(bias_far, r, i, i + right * (STEPS - FAR_SLOTS))
            return carry

        lax.fori_loop(0, 3 * PLANE - 1, one_near, 0)
        lax.fori_loop(0, FAR_SLOTS, one_far, 0)
        return carry

    lax.fori_loop(0, PLANE * BPF, biases, 0)

    def ring_rest(h, carry):
        await_bytes(near.at[h, :, pl.ds(here, here - BLK)], plane_in.at[h])
        for k in PEERS[1:]:
            ring_piece(h, peer(k))
        return carry

    lax.fori_loop(0, heads, ring_rest, 0)

    frames = ctx
    onward = (
        (jnp.minimum((place + 1) * PLANE, frames - 1), place * PLANE - PLANE + 1),
        (jnp.maximum((place - 1) * PLANE + PLANE - 1, 0), place * PLANE + PLANE + 2),
    )
    takes_second = [
        (count(f * BPF, g * BPF + 1) + count(f * BPF + 1, g * BPF + 1)) > 0 for f, g in onward
    ]

    def far_copy(way, n, h):
        b = 3 - n if way == 0 else 2 * PLANE + n
        whole = n < FAR_SLOTS - 1
        rows = FRAME if whole else BLK
        return pltpu.make_async_remote_copy(
            src_ref=near.at[h, :, pl.ds(b * FRAME, rows)] if whole else chosen.at[h, way],
            dst_ref=far.at[h, way, :, pl.ds(n * FRAME, rows)],
            send_sem=far_sent.at[way, n, h], recv_sem=far_in.at[way, n, h],
            device_id=beside(way), device_id_type=MESH,
        )

    def attend_near(h):
        def one_frame(a, carry):
            own = pl.multiple_of((PLANE + a) * FRAME, FRAME)
            ks[pl.ds(0, FRAME), :] = near[h, 0, pl.ds(own, FRAME), :]
            vs[pl.ds(0, FRAME), :] = near[h, 1, pl.ds(own, FRAME), :]

            def pick(i, carry):
                w = i + (i + REACH - PLANE - a) // REACH
                row = pl.multiple_of(w * FRAME, FRAME)
                second = sel[a, jnp.minimum(w + REACH - PLANE - a, STEPS - 1)] == 1
                to = pl.ds(pl.multiple_of(FRAME + i * BLK, BLK), BLK)
                for which, dst in ((0, ks), (1, vs)):
                    dst[to, :] = jnp.where(
                        second, near[h, which, pl.ds(row + BLK, BLK), :], near[h, which, pl.ds(row, BLK), :]
                    )
                return carry

            lax.fori_loop(0, 3 * PLANE - 1, pick, 0)
            rows = pl.ds(pl.multiple_of(a * FRAME, FRAME), FRAME)
            scores = lax.dot_general(
                qb[h, rows, :], ks[...], (((1,), (1,)), ((), ())), preferred_element_type=jnp.float32
            ).reshape(BPF, BLK, NEAR_KEYS)
            scores = scores * scale2 + bias_near[pl.ds(a * BPF, BPF)]
            top = jnp.max(scores, axis=2, keepdims=True)
            weights = jnp.exp2(scores - top)
            total = jnp.sum(weights, axis=2, keepdims=True)
            part[h, rows, :] = jnp.dot(
                weights.reshape(FRAME, NEAR_KEYS).astype(jnp.bfloat16), vs[...],
                preferred_element_type=jnp.float32,
            )
            high[h, rows, :] = jnp.broadcast_to(top, (BPF, BLK, HD)).reshape(FRAME, HD)
            low[h, rows, :] = jnp.broadcast_to(total, (BPF, BLK, HD)).reshape(FRAME, HD)
            return carry

        lax.fori_loop(0, PLANE, one_frame, 0)

    def attend_far(h, a):
        def pick(i, carry):
            right = (i + a) // FAR_SLOTS
            pair = (1 - right) * (FAR_SLOTS - 1 - a - i) + right * (i + a - FAR_SLOTS)
            whole = 1 - pair // (FAR_SLOTS - 1)
            row = pl.multiple_of(pair * FRAME, FRAME)
            row_b = pl.multiple_of(pair * FRAME + whole * BLK, BLK)
            second = sel[a, i + right * (STEPS - FAR_SLOTS)] == 1
            to = pl.ds(pl.multiple_of(i * BLK, BLK), BLK)
            for which, dst in ((0, ks), (1, vs)):
                dst[to, :] = jnp.where(
                    second, far[h, right, which, pl.ds(row_b, BLK), :], far[h, right, which, pl.ds(row, BLK), :]
                )
            return carry

        lax.fori_loop(0, FAR_SLOTS, pick, 0)
        rows = pl.ds(pl.multiple_of(a * FRAME, FRAME), FRAME)
        keys = pl.ds(0, FAR_KEYS)
        scores = lax.dot_general(
            qb[h, rows, :], ks[keys, :], (((1,), (1,)), ((), ())), preferred_element_type=jnp.float32
        ).reshape(BPF, BLK, FAR_KEYS)
        scores = (scores * scale2 + bias_far[pl.ds(a * BPF, BPF)]).reshape(FRAME, FAR_KEYS)
        before = high[h, rows, :]
        top = jnp.maximum(before, jnp.max(scores, axis=1, keepdims=True))
        weights = jnp.exp2(scores - jnp.concatenate([top] * FAR_SLOTS, axis=1))
        fade = jnp.exp2(before - top)
        total = fade * low[h, rows, :] + jnp.sum(weights, axis=1, keepdims=True)
        mixed = fade * part[h, rows, :] + jnp.dot(
            weights.astype(jnp.bfloat16), vs[keys, :], preferred_element_type=jnp.float32
        )
        ob[h, rows, :] = (mixed / total).astype(jnp.bfloat16)

    def give_back(h, a):
        for b in range(BPF):
            j = a * BPF + b

            @pl.when(j != me)
            def _():
                pltpu.make_async_remote_copy(
                    src_ref=ob.at[h, rows_of(j)], dst_ref=out_ref.at[:, columns(me, h)],
                    send_sem=out_sent.at[h], recv_sem=out_in.at[0],
                    device_id=member(j), device_id_type=MESH,
                ).start()

            @pl.when(j == me)
            def _():
                pltpu.make_async_copy(ob.at[h, rows_of(j)], out_ref.at[:, columns(me, h)], out_in.at[0]).start()

    def first_phase(h, carry):
        for way in (0, 1):
            @pl.when(gets[way])
            def _():
                await_bytes(near.at[h, :, pl.ds(lands[way], here)], ring_in.at[way, h])

        for way in (0, 1):
            @pl.when(sends_far[way])
            def _():
                frame = 1 if way == 0 else 2 * PLANE + 2
                for which in (0, 1):
                    chosen[h, way, which] = jnp.where(
                        takes_second[way],
                        near[h, which, pl.ds(frame * FRAME + BLK, BLK), :],
                        near[h, which, pl.ds(frame * FRAME, BLK), :],
                    )
                for n in range(FAR_SLOTS):
                    far_copy(way, n, h).start()

        await_bytes(qb.at[h], q_in.at[h])
        attend_near(h)
        return carry

    lax.fori_loop(0, heads, first_phase, 0)

    both = gets_far[0] & gets_far[1]
    falling = jnp.where(gets_far[0], 1, 0)

    def second_phase(h, carry):
        for way in (0, 1):
            @pl.when(both)
            def _():
                for n in range(FAR_SLOTS):
                    far_copy(way, n, h).wait_recv()

        for n in range(PLANE):
            if n >= 1:
                for way in (0, 1):
                    @pl.when(gets_far[way] & jnp.logical_not(both))
                    def _():
                        far_copy(way, n - 1, h).wait_recv()
            a = falling * (PLANE - 1 - n) + (1 - falling) * n
            attend_far(h, a)
            give_back(h, a)
        return carry

    lax.fori_loop(0, heads, second_phase, 0)

    def finish(h, carry):
        others = (GROUP - 1) * BLK
        await_bytes(near.at[h, :, pl.ds(0, others)], plane_sent.at[h])
        await_bytes(qb.at[h, pl.ds(0, others)], q_sent.at[h])
        await_bytes(ob.at[h, pl.ds(0, others)], out_sent.at[h])
        for way in (0, 1):
            @pl.when(has[way])
            def _():
                await_bytes(near.at[h, :, pl.ds(0, here)], ring_sent.at[way, h])

            @pl.when(sends_far[way])
            def _():
                for n in range(FAR_SLOTS):
                    far_copy(way, n, h).wait_send()
        return carry

    lax.fori_loop(0, heads, finish, 0)
    await_bytes(out_ref, out_in.at[0])


def plane_attention(q_proj, k_proj, v_proj, kv_list):
    ctx = lax.axis_size("ctx")
    tokens, width = q_proj.shape
    heads = width // HD // GROUP
    here = PLANE * FRAME
    lists = kv_list.T
    any_space = pl.BlockSpec(memory_space=pl.ANY)
    dma = pltpu.SemaphoreType.DMA
    bf16, f32 = jnp.bfloat16, jnp.float32
    return pl.pallas_call(
        functools.partial(plane_kernel, ctx, heads),
        out_shape=jax.ShapeDtypeStruct((tokens, width), bf16),
        in_specs=[any_space] * 4,
        out_specs=any_space,
        scratch_shapes=[
            pltpu.SMEM(lists.shape, jnp.int32),
            pltpu.SMEM((PLANE, STEPS), jnp.int32),
            pltpu.SMEM((PLANE * BPF, STEPS), jnp.int32),
            pltpu.VMEM((PLANE * BPF, 1, NEAR_KEYS), f32),
            pltpu.VMEM((PLANE * BPF, 1, FAR_KEYS), f32),
            pltpu.VMEM((heads, 2, NEAR, HD), bf16),
            pltpu.VMEM((heads, 2, 2, FAR, HD), bf16),
            pltpu.VMEM((heads, 2, 2, BLK, HD), bf16),
            pltpu.VMEM((heads, here, HD), bf16),
            pltpu.VMEM((heads, here, HD), bf16),
            pltpu.VMEM((heads, here, HD), f32),
            pltpu.VMEM((heads, here, HD), f32),
            pltpu.VMEM((heads, here, HD), f32),
            pltpu.VMEM((NEAR_KEYS, HD), bf16),
            pltpu.VMEM((NEAR_KEYS, HD), bf16),
            dma((1,)), dma((heads,)), dma((heads,)), dma((heads,)), dma((2, heads)),
            dma((2, FAR_SLOTS, heads)), dma((1,)),
            dma((heads,)), dma((heads,)), dma((2, heads)), dma((2, FAR_SLOTS, heads)), dma((heads,)),
        ],
        compiler_params=pltpu.CompilerParams(
            collective_id=0, has_side_effects=True, vmem_limit_bytes=30 * 1024 * 1024
        ),
    )(*[pltpu.with_memory_space_constraint(x, pltpu.HBM) for x in (lists, q_proj, k_proj, v_proj)])


def on_device(q_proj, k_proj, v_proj, kv_list):
    rep, uly = lax.axis_size("rep"), lax.axis_size("uly")
    if rep == 1 and uly == BPF and q_proj.shape[0] == BLK and lax.axis_size("ctx") % PLANE == 0:
        return plane_attention(q_proj, k_proj, v_proj, kv_list)
    return ring_attention(q_proj, k_proj, v_proj, kv_list)


def solution(mesh):
    rows = P(("groups", "ctx", "rep", "uly"), None)
    return jax.shard_map(
        on_device,
        mesh=mesh,
        in_specs=(rows, rows, rows, P("groups", None)),
        out_specs=rows,
        check_vma=False,
    )
```

```python
import functools
import math

import jax
import jax.numpy as jnp
from jax import lax
from jax.experimental import pallas as pl
from jax.experimental.pallas import tpu as pltpu
from jax.sharding import PartitionSpec as P

HD = 128
BLK = 128
BPF = 2
FRAME = BLK * BPF
REACH = 7
GROUP = 8
SLOTS = 2 * REACH
KEYS = (SLOTS + BPF) * BLK

very_low = -1e30
scale2 = math.log2(math.e) / math.sqrt(HD)
MESH = pl.DeviceIdType.MESH


def ring_kernel(sizes, sel_ref, bias_ref, q_ref, k_ref, v_ref, out_ref, kv, qb, ob, ks, vs,
           first_in, kv_in, q_in, kv_sent, q_sent, ring_in, ring_sent, out_in, out_sent):
    ctx, rep, uly, tokens, heads = sizes
    inner = GROUP // (rep * uly)
    here = GROUP * tokens
    frames_here = here // FRAME
    places = ctx // inner
    hops = -(-REACH // frames_here)
    c = lax.axis_index("ctx")
    r = lax.axis_index("rep")
    u = lax.axis_index("uly")
    place = c // inner
    me = (c % inner) * (rep * uly) + r * uly + u

    def member(j):
        return {"ctx": place * inner + j // (rep * uly), "rep": (j // uly) % rep, "uly": j % uly}

    def beside(step):
        return {"ctx": c + step * inner}

    has_left, has_right = place >= 1, place <= places - 2

    barrier = pltpu.get_barrier_semaphore()
    for k in range(1, GROUP):
        pl.semaphore_signal(barrier, inc=1, device_id=member((me + k) % GROUP), device_id_type=MESH)

    @pl.when(has_left)
    def _():
        pl.semaphore_signal(barrier, inc=1, device_id=beside(-1), device_id_type=MESH)

    @pl.when(has_right)
    def _():
        pl.semaphore_signal(barrier, inc=1, device_id=beside(1), device_id_type=MESH)

    neighbours = jnp.minimum(place, 1) + jnp.minimum(places - 1 - place, 1)
    pl.semaphore_wait(barrier, GROUP - 1 + neighbours)

    def columns(owner, h):
        return pl.ds(pl.multiple_of((owner * heads + h) * HD, HD), HD)

    own_rows = pl.ds(pl.multiple_of(REACH * FRAME + me * tokens, tokens), tokens)
    q_rows = pl.ds(pl.multiple_of(me * tokens, tokens), tokens)

    def share_kv(h, arrived):
        for k in range(1, GROUP):
            j = (me + k) % GROUP
            for which, src in enumerate((k_ref, v_ref)):
                pltpu.make_async_remote_copy(
                    src_ref=src.at[:, columns(j, h)], dst_ref=kv.at[h, which, own_rows],
                    send_sem=kv_sent.at[h], recv_sem=arrived(k),
                    device_id=member(j), device_id_type=MESH,
                ).start()
        for which, src in enumerate((k_ref, v_ref)):
            pltpu.make_async_copy(
                src.at[:, columns(me, h)], kv.at[h, which, own_rows], arrived(0)
            ).start()

    def share_later(h, carry):
        share_kv(h, lambda k: kv_in.at[h])
        return carry

    def share_q(h, carry):
        for k in range(1, GROUP):
            j = (me + k) % GROUP
            pltpu.make_async_remote_copy(
                src_ref=q_ref.at[:, columns(j, h)], dst_ref=qb.at[h, q_rows],
                send_sem=q_sent.at[h], recv_sem=q_in.at[h],
                device_id=member(j), device_id_type=MESH,
            ).start()
        pltpu.make_async_copy(q_ref.at[:, columns(me, h)], qb.at[h, q_rows], q_in.at[h]).start()
        return carry

    share_kv(0, lambda k: first_in.at[k])
    lax.fori_loop(1, heads, share_later, 0)
    lax.fori_loop(0, heads, share_q, 0)

    def await_bytes(ref, sem):
        pltpu.make_async_copy(ref, ref, sem).wait()

    def ring_copy(way, s, h):
        if way == 0:
            first, last, shift = max(0, REACH - s * frames_here), REACH - (s - 1) * frames_here, frames_here
        else:
            first = REACH + s * frames_here
            last, shift = min(frames_here + SLOTS, first + frames_here), -frames_here
        rows = (last - first) * FRAME
        return pltpu.make_async_remote_copy(
            src_ref=kv.at[h, :, pl.ds((first + shift) * FRAME, rows)],
            dst_ref=kv.at[h, :, pl.ds(first * FRAME, rows)],
            send_sem=ring_sent.at[way, s - 1, h], recv_sem=ring_in.at[way, s - 1, h],
            device_id=beside(1 if way == 0 else -1), device_id_type=MESH,
        )

    def sends(way, s):
        if way == 0:
            return (place >= s - 1) & has_right
        return (place + s <= places) & has_left

    def receives(way, s):
        return place >= s if way == 0 else place + s <= places - 1

    def ring_start(s, h):
        for way in (0, 1):
            @pl.when(sends(way, s))
            def _():
                ring_copy(way, s, h).start()

    def ring_arrived(s, h):
        for way in (0, 1):
            @pl.when(receives(way, s))
            def _():
                ring_copy(way, s, h).wait_recv()

    def attend(h):
        def one_frame(f, carry):
            own = pl.multiple_of((REACH + f) * FRAME, FRAME)
            ks[pl.ds(0, FRAME), :] = kv[h, 0, pl.ds(own, FRAME), :]
            vs[pl.ds(0, FRAME), :] = kv[h, 1, pl.ds(own, FRAME), :]

            def pick(i, carry):
                far = place * frames_here + f + i - REACH + i // REACH
                slot = jnp.minimum(jnp.maximum(far, 0), ctx - 1) - place * frames_here + REACH
                row = pl.multiple_of(slot * FRAME, FRAME)
                second = sel_ref[f, i] == 1
                to = pl.ds(pl.multiple_of(FRAME + i * BLK, BLK), BLK)
                for which, dst in ((0, ks), (1, vs)):
                    dst[to, :] = jnp.where(
                        second,
                        kv[h, which, pl.ds(row + BLK, BLK), :],
                        kv[h, which, pl.ds(row, BLK), :],
                    )
                return carry

            lax.fori_loop(0, SLOTS, pick, 0)

            def one_block(b, carry):
                rows = pl.ds(pl.multiple_of(f * FRAME + b * BLK, BLK), BLK)
                scores = lax.dot_general(
                    qb[h, rows, :], ks[...], (((1,), (1,)), ((), ())),
                    preferred_element_type=jnp.float32,
                )
                scores = scores * scale2 + bias_ref[f * BPF + b]
                weights = jnp.exp2(scores - jnp.max(scores, axis=1, keepdims=True))
                total = jnp.sum(weights, axis=1, keepdims=True)
                mixed = jnp.dot(
                    weights.astype(jnp.bfloat16), vs[...], preferred_element_type=jnp.float32
                )
                ob[h, rows, :] = (mixed / total).astype(jnp.bfloat16)
                return carry

            lax.fori_loop(0, BPF, one_block, 0)
            return carry

        lax.fori_loop(0, frames_here, one_frame, 0)

    def give_back(h):
        for k in range(1, GROUP):
            j = (me + k) % GROUP
            pltpu.make_async_remote_copy(
                src_ref=ob.at[h, pl.ds(pl.multiple_of(j * tokens, tokens), tokens)],
                dst_ref=out_ref.at[:, columns(me, h)],
                send_sem=out_sent.at[h], recv_sem=out_in.at[0],
                device_id=member(j), device_id_type=MESH,
            ).start()
        pltpu.make_async_copy(ob.at[h, q_rows], out_ref.at[:, columns(me, h)], out_in.at[0]).start()

    def step(t, carry):
        @pl.when((t >= 1) & (t < heads))
        def _():
            await_bytes(kv.at[t, :, pl.ds(REACH * FRAME, here)], kv_in.at[t])
            ring_start(1, t)

        for s in range(1, hops):
            @pl.when((t >= s) & (t < heads + s))
            def _():
                ring_arrived(s, t - s)
                ring_start(s + 1, t - s)

        @pl.when(t >= hops)
        def _():
            ring_arrived(hops, t - hops)
            await_bytes(qb.at[t - hops], q_in.at[t - hops])
            attend(t - hops)
            give_back(t - hops)

        return carry

    for k in range(GROUP):
        row = REACH * FRAME + (me + GROUP - k) % GROUP * tokens
        piece = kv.at[0, :, pl.ds(pl.multiple_of(row, tokens), tokens)]
        await_bytes(piece, first_in.at[k])
        for way in (0, 1):
            @pl.when(sends(way, 1))
            def _():
                to = row - here if way == 0 else row + here
                pltpu.make_async_remote_copy(
                    src_ref=piece, dst_ref=kv.at[0, :, pl.ds(pl.multiple_of(to, tokens), tokens)],
                    send_sem=ring_sent.at[way, 0, 0], recv_sem=ring_in.at[way, 0, 0],
                    device_id=beside(1 if way == 0 else -1), device_id_type=MESH,
                ).start()

    lax.fori_loop(0, heads + hops, step, 0)

    def finish(h, carry):
        others = (GROUP - 1) * tokens
        await_bytes(kv.at[h, :, pl.ds(0, others)], kv_sent.at[h])
        await_bytes(qb.at[h, pl.ds(0, others)], q_sent.at[h])
        await_bytes(ob.at[h, pl.ds(0, others)], out_sent.at[h])
        for s in range(1, hops + 1):
            for way in (0, 1):
                @pl.when(sends(way, s))
                def _():
                    ring_copy(way, s, h).wait_send()
        return carry

    lax.fori_loop(0, heads, finish, 0)
    await_bytes(out_ref, out_in.at[0])


def tables(kv_list, place, frames_here, frames):
    lists = lax.dynamic_slice_in_dim(kv_list, place * frames_here * BPF, frames_here * BPF, 0)
    lists = lists.reshape(frames_here, BPF, 1, -1)
    steps = jnp.array([d for d in range(-REACH, REACH + 1) if d != 0], jnp.int32)
    far = place * frames_here + jnp.arange(frames_here, dtype=jnp.int32)[:, None] + steps[None, :]
    inside = (far >= 0) & (far < frames)
    has = [jnp.any(lists == (far * BPF + b)[:, None, :, None], axis=3) for b in range(BPF)]
    listed = (has[0] | has[1]) & inside[:, None, :]
    sel = jnp.any(has[1], axis=1).astype(jnp.int32)
    bias = jnp.where(listed, 0.0, very_low).astype(jnp.float32)
    bias = jnp.concatenate([jnp.zeros((frames_here, BPF, BPF), jnp.float32), bias], axis=2)
    bias = jnp.repeat(bias.reshape(frames_here * BPF, BPF + SLOTS), BLK, axis=1)
    return sel, bias.reshape(frames_here * BPF, 1, KEYS)


def ring_attention(q_proj, k_proj, v_proj, kv_list):
    ctx, rep, uly = lax.axis_size("ctx"), lax.axis_size("rep"), lax.axis_size("uly")
    tokens, width = q_proj.shape
    heads = width // HD // GROUP
    inner = GROUP // (rep * uly)
    here = GROUP * tokens
    frames_here = here // FRAME
    hops = -(-REACH // frames_here)
    sel, bias = tables(kv_list, lax.axis_index("ctx") // inner, frames_here, ctx)
    window = (frames_here + SLOTS) * FRAME
    any_space = pl.BlockSpec(memory_space=pl.ANY)
    dma = pltpu.SemaphoreType.DMA
    return pl.pallas_call(
        functools.partial(ring_kernel, (ctx, rep, uly, tokens, heads)),
        out_shape=jax.ShapeDtypeStruct((tokens, width), jnp.bfloat16),
        in_specs=[
            pl.BlockSpec(memory_space=pltpu.SMEM),
            pl.BlockSpec(memory_space=pltpu.VMEM),
            any_space, any_space, any_space,
        ],
        out_specs=any_space,
        scratch_shapes=[
            pltpu.VMEM((heads, 2, window, HD), jnp.bfloat16),
            pltpu.VMEM((heads, here, HD), jnp.bfloat16),
            pltpu.VMEM((heads, here, HD), jnp.bfloat16),
            pltpu.VMEM((KEYS, HD), jnp.bfloat16),
            pltpu.VMEM((KEYS, HD), jnp.bfloat16),
            dma((GROUP,)), dma((heads,)), dma((heads,)), dma((heads,)), dma((heads,)),
            dma((2, hops, heads)), dma((2, hops, heads)), dma((1,)), dma((heads,)),
        ],
        compiler_params=pltpu.CompilerParams(
            collective_id=0, has_side_effects=True, vmem_limit_bytes=56 * 1024 * 1024
        ),
    )(sel, bias, q_proj, k_proj, v_proj)


PLANE = 4
NEAR = 3 * PLANE * FRAME
NEAR_KEYS = NEAR // 2 + BLK
FAR_SLOTS = 3
FAR = (2 * FAR_SLOTS - 1) * BLK
FAR_KEYS = FAR_SLOTS * BLK
STEPS = 2 * REACH + 1
PEERS = (2, 1, 3, 4, 6, 5, 7)


def plane_kernel(ctx, heads, list_ref, q_ref, k_ref, v_ref, out_ref,
                 lists, sel, listed, bias_near, bias_far, near, far, chosen, qb, ob, part, high, low, ks, vs,
                 list_in, own_in, beside_in, plane_in, q_in, ring_in, far_in, out_in,
                 plane_sent, q_sent, ring_sent, far_sent, out_sent):
    here = PLANE * FRAME
    places = ctx // PLANE
    c = lax.axis_index("ctx")
    u = lax.axis_index("uly")
    place = c // PLANE
    me = (c % PLANE) * BPF + u

    def member(j):
        return {"ctx": place * PLANE + j // BPF, "uly": j % BPF}

    def beside(way):
        return {"ctx": c + (PLANE if way == 0 else -PLANE)}

    def peer(k):
        bits = (me % 2, (me // 2) % 2, me // 4)
        return sum((1 - bit if (k >> n) & 1 else bit) << n for n, bit in enumerate(bits))

    has = (place <= places - 2, place >= 1)
    gets = (place >= 1, place <= places - 2)
    sends_far = ((place >= 1) & (place <= places - 2),) * 2
    gets_far = (place >= 2, place <= places - 3)

    def columns(owner, h):
        return pl.ds(pl.multiple_of((owner * heads + h) * HD, HD), HD)

    def rows_of(j, base=0):
        return pl.ds(pl.multiple_of(base + j * BLK, BLK), BLK)

    def await_bytes(ref, sem):
        pltpu.make_async_copy(ref, ref, sem).wait()

    def fetch_own(h, carry):
        for which, src in enumerate((k_ref, v_ref)):
            pltpu.make_async_copy(
                src.at[:, columns(me, h)], near.at[h, which, rows_of(me, here)], own_in.at[h]
            ).start()
        return carry

    barrier = pltpu.get_barrier_semaphore()
    for way in (0, 1):
        @pl.when(has[way])
        def _():
            pl.semaphore_signal(barrier, inc=1, device_id=beside(way), device_id_type=MESH)
    for k in PEERS:
        pl.semaphore_signal(barrier, inc=1, device_id=member(peer(k)), device_id_type=MESH)
    lax.fori_loop(0, heads, fetch_own, 0)
    neighbours = jnp.minimum(place, 1) + jnp.minimum(places - 1 - place, 1)
    pl.semaphore_wait(barrier, GROUP - 1 + neighbours)

    lands = (0, 2 * here)

    def ring_piece(h, j):
        for way in (0, 1):
            @pl.when(has[way])
            def _():
                pltpu.make_async_remote_copy(
                    src_ref=near.at[h, :, rows_of(j, here)], dst_ref=near.at[h, :, rows_of(j, lands[way])],
                    send_sem=ring_sent.at[way, h], recv_sem=ring_in.at[way, h],
                    device_id=beside(way), device_id_type=MESH,
                ).start()

    def share_kv(h, carry):
        for k in PEERS:
            j = peer(k)
            for which, src in enumerate((k_ref, v_ref)):
                pltpu.make_async_remote_copy(
                    src_ref=src.at[:, columns(j, h)], dst_ref=near.at[h, which, rows_of(me, here)],
                    send_sem=plane_sent.at[h], recv_sem=(beside_in if k == 2 else plane_in).at[h],
                    device_id=member(j), device_id_type=MESH,
                ).start()
        return carry

    def share_q(h, carry):
        for k in PEERS:
            j = peer(k)
            pltpu.make_async_remote_copy(
                src_ref=q_ref.at[:, columns(j, h)], dst_ref=qb.at[h, rows_of(me)],
                send_sem=q_sent.at[h], recv_sem=q_in.at[h],
                device_id=member(j), device_id_type=MESH,
            ).start()
        pltpu.make_async_copy(q_ref.at[:, columns(me, h)], qb.at[h, rows_of(me)], q_in.at[h]).start()
        return carry

    def ring_own(h, carry):
        await_bytes(near.at[h, :, pl.ds(here, BLK)], own_in.at[h])
        ring_piece(h, me)
        return carry

    lax.fori_loop(0, heads, ring_own, 0)
    lax.fori_loop(0, heads, share_kv, 0)
    lax.fori_loop(0, heads, share_q, 0)
    get_lists = pltpu.make_async_copy(list_ref, lists, list_in.at[0])
    get_lists.start()

    def ring_beside(h, carry):
        await_bytes(near.at[h, :, pl.ds(here, BLK)], beside_in.at[h])
        ring_piece(h, peer(2))
        return carry

    lax.fori_loop(0, heads, ring_beside, 0)

    for way in (0, 1):
        @pl.when(jnp.logical_not(gets[way]))
        def _():
            def clear(h, carry):
                for which in (0, 1):
                    near[h, which, pl.ds(lands[way], here), :] = jnp.zeros((here, HD), jnp.bfloat16)
                return carry

            lax.fori_loop(0, heads, clear, 0)

        @pl.when(jnp.logical_not(gets_far[way]))
        def _():
            def clear(h, carry):
                for which in (0, 1):
                    far[h, way, which] = jnp.zeros((FAR, HD), jnp.bfloat16)
                return carry

            lax.fori_loop(0, heads, clear, 0)

    get_lists.wait()

    def count(row, block):
        return sum((lists[j, row] == block).astype(jnp.int32) for j in range(lists.shape[0]))

    def tables(n, carry):
        a, d = n // STEPS, n % STEPS
        target = place * PLANE + a + d - REACH
        block = jnp.where(target < 0, -BLK, target * BPF)
        second = 0
        for b in range(BPF):
            row = (place * PLANE + a) * BPF + b
            one = count(row, block + 1)
            listed[a * BPF + b, d] = jnp.minimum(count(row, block) + one, 1)
            second = second + one
        sel[a, d] = jnp.minimum(second, 1)
        return carry

    lax.fori_loop(0, PLANE * STEPS, tables, 0)

    def fill(ref, r, slot, d):
        value = jnp.where(listed[r, d] == 1, 0.0, very_low)
        ref[r, :, pl.ds(pl.multiple_of(slot * BLK, BLK), BLK)] = jnp.full((1, BLK), value, jnp.float32)

    def biases(r, carry):
        a = r // BPF
        bias_near[r, :, pl.ds(0, FRAME)] = jnp.zeros((1, FRAME), jnp.float32)

        def one_near(i, carry):
            w = i + (i + REACH - PLANE - a) // REACH
            fill(bias_near, r, BPF + i, jnp.minimum(w + REACH - PLANE - a, STEPS - 1))
            return carry

        def one_far(i, carry):
            right = (i + a) // FAR_SLOTS
            fill(bias_far, r, i, i + right * (STEPS - FAR_SLOTS))
            return carry

        lax.fori_loop(0, 3 * PLANE - 1, one_near, 0)
        lax.fori_loop(0, FAR_SLOTS, one_far, 0)
        return carry

    lax.fori_loop(0, PLANE * BPF, biases, 0)

    def ring_rest(h, carry):
        await_bytes(near.at[h, :, pl.ds(here, here - BPF * BLK)], plane_in.at[h])
        for k in PEERS[1:]:
            ring_piece(h, peer(k))
        return carry

    lax.fori_loop(0, heads, ring_rest, 0)

    frames = ctx
    onward = (
        (jnp.minimum((place + 1) * PLANE, frames - 1), place * PLANE - PLANE + 1),
        (jnp.maximum((place - 1) * PLANE + PLANE - 1, 0), place * PLANE + PLANE + 2),
    )
    takes_second = [
        (count(f * BPF, g * BPF + 1) + count(f * BPF + 1, g * BPF + 1)) > 0 for f, g in onward
    ]

    def far_copy(way, n, h):
        b = 3 - n if way == 0 else 2 * PLANE + n
        whole = n < FAR_SLOTS - 1
        rows = FRAME if whole else BLK
        return pltpu.make_async_remote_copy(
            src_ref=near.at[h, :, pl.ds(b * FRAME, rows)] if whole else chosen.at[h, way],
            dst_ref=far.at[h, way, :, pl.ds(n * FRAME, rows)],
            send_sem=far_sent.at[way, n, h], recv_sem=far_in.at[way, n, h],
            device_id=beside(way), device_id_type=MESH,
        )

    def attend_near(h):
        def one_frame(a, carry):
            own = pl.multiple_of((PLANE + a) * FRAME, FRAME)
            ks[pl.ds(0, FRAME), :] = near[h, 0, pl.ds(own, FRAME), :]
            vs[pl.ds(0, FRAME), :] = near[h, 1, pl.ds(own, FRAME), :]

            def pick(i, carry):
                w = i + (i + REACH - PLANE - a) // REACH
                row = pl.multiple_of(w * FRAME, FRAME)
                second = sel[a, jnp.minimum(w + REACH - PLANE - a, STEPS - 1)] == 1
                to = pl.ds(pl.multiple_of(FRAME + i * BLK, BLK), BLK)
                for which, dst in ((0, ks), (1, vs)):
                    dst[to, :] = jnp.where(
                        second, near[h, which, pl.ds(row + BLK, BLK), :], near[h, which, pl.ds(row, BLK), :]
                    )
                return carry

            lax.fori_loop(0, 3 * PLANE - 1, pick, 0)
            rows = pl.ds(pl.multiple_of(a * FRAME, FRAME), FRAME)
            scores = lax.dot_general(
                qb[h, rows, :], ks[...], (((1,), (1,)), ((), ())), preferred_element_type=jnp.float32
            ).reshape(BPF, BLK, NEAR_KEYS)
            scores = scores * scale2 + bias_near[pl.ds(a * BPF, BPF)]
            top = jnp.max(scores, axis=2, keepdims=True)
            weights = jnp.exp2(scores - top)
            total = jnp.sum(weights, axis=2, keepdims=True)
            part[h, rows, :] = jnp.dot(
                weights.reshape(FRAME, NEAR_KEYS).astype(jnp.bfloat16), vs[...],
                preferred_element_type=jnp.float32,
            )
            high[h, rows, :] = jnp.broadcast_to(top, (BPF, BLK, HD)).reshape(FRAME, HD)
            low[h, rows, :] = jnp.broadcast_to(total, (BPF, BLK, HD)).reshape(FRAME, HD)
            return carry

        lax.fori_loop(0, PLANE, one_frame, 0)

    def attend_far(h, a):
        def pick(i, carry):
            right = (i + a) // FAR_SLOTS
            pair = (1 - right) * (FAR_SLOTS - 1 - a - i) + right * (i + a - FAR_SLOTS)
            whole = 1 - pair // (FAR_SLOTS - 1)
            row = pl.multiple_of(pair * FRAME, FRAME)
            row_b = pl.multiple_of(pair * FRAME + whole * BLK, BLK)
            second = sel[a, i + right * (STEPS - FAR_SLOTS)] == 1
            to = pl.ds(pl.multiple_of(i * BLK, BLK), BLK)
            for which, dst in ((0, ks), (1, vs)):
                dst[to, :] = jnp.where(
                    second, far[h, right, which, pl.ds(row_b, BLK), :], far[h, right, which, pl.ds(row, BLK), :]
                )
            return carry

        lax.fori_loop(0, FAR_SLOTS, pick, 0)
        rows = pl.ds(pl.multiple_of(a * FRAME, FRAME), FRAME)
        keys = pl.ds(0, FAR_KEYS)
        scores = lax.dot_general(
            qb[h, rows, :], ks[keys, :], (((1,), (1,)), ((), ())), preferred_element_type=jnp.float32
        ).reshape(BPF, BLK, FAR_KEYS)
        scores = (scores * scale2 + bias_far[pl.ds(a * BPF, BPF)]).reshape(FRAME, FAR_KEYS)
        before = high[h, rows, :]
        top = jnp.maximum(before, jnp.max(scores, axis=1, keepdims=True))
        weights = jnp.exp2(scores - jnp.concatenate([top] * FAR_SLOTS, axis=1))
        fade = jnp.exp2(before - top)
        total = fade * low[h, rows, :] + jnp.sum(weights, axis=1, keepdims=True)
        mixed = fade * part[h, rows, :] + jnp.dot(
            weights.astype(jnp.bfloat16), vs[keys, :], preferred_element_type=jnp.float32
        )
        ob[h, rows, :] = (mixed / total).astype(jnp.bfloat16)

    def give_back(h, a):
        for b in range(BPF):
            j = a * BPF + b

            @pl.when(j != me)
            def _():
                pltpu.make_async_remote_copy(
                    src_ref=ob.at[h, rows_of(j)], dst_ref=out_ref.at[:, columns(me, h)],
                    send_sem=out_sent.at[h], recv_sem=out_in.at[0],
                    device_id=member(j), device_id_type=MESH,
                ).start()

            @pl.when(j == me)
            def _():
                pltpu.make_async_copy(ob.at[h, rows_of(j)], out_ref.at[:, columns(me, h)], out_in.at[0]).start()

    def first_phase(h, carry):
        for way in (0, 1):
            @pl.when(gets[way])
            def _():
                await_bytes(near.at[h, :, pl.ds(lands[way], here)], ring_in.at[way, h])

        for way in (0, 1):
            @pl.when(sends_far[way])
            def _():
                frame = 1 if way == 0 else 2 * PLANE + 2
                for which in (0, 1):
                    chosen[h, way, which] = jnp.where(
                        takes_second[way],
                        near[h, which, pl.ds(frame * FRAME + BLK, BLK), :],
                        near[h, which, pl.ds(frame * FRAME, BLK), :],
                    )
                for n in range(FAR_SLOTS):
                    far_copy(way, n, h).start()

        await_bytes(qb.at[h], q_in.at[h])
        attend_near(h)
        return carry

    lax.fori_loop(0, heads, first_phase, 0)

    both = gets_far[0] & gets_far[1]
    falling = jnp.where(gets_far[0], 1, 0)

    others = (GROUP - 1) * BLK

    def await_far_sent(h):
        for way in (0, 1):
            @pl.when(sends_far[way])
            def _():
                for n in range(FAR_SLOTS):
                    far_copy(way, n, h).wait_send()

    def await_out_sent(h):
        await_bytes(ob.at[h, pl.ds(0, others)], out_sent.at[h])

    def second_phase(h, carry):
        await_bytes(near.at[h, :, pl.ds(0, others)], plane_sent.at[h])
        await_bytes(qb.at[h, pl.ds(0, others)], q_sent.at[h])
        for way in (0, 1):
            @pl.when(has[way])
            def _():
                await_bytes(near.at[h, :, pl.ds(0, here)], ring_sent.at[way, h])

        @pl.when(h >= 1)
        def _():
            await_far_sent(h - 1)
            await_out_sent(h - 1)

        for way in (0, 1):
            @pl.when(both)
            def _():
                for n in range(FAR_SLOTS):
                    far_copy(way, n, h).wait_recv()

        for n in range(PLANE):
            if n >= 1:
                for way in (0, 1):
                    @pl.when(gets_far[way] & jnp.logical_not(both))
                    def _():
                        far_copy(way, n - 1, h).wait_recv()
            a = falling * (PLANE - 1 - n) + (1 - falling) * n
            attend_far(h, a)
            give_back(h, a)
        return carry

    lax.fori_loop(0, heads, second_phase, 0)

    await_far_sent(heads - 1)
    await_out_sent(heads - 1)
    await_bytes(out_ref, out_in.at[0])


def plane_attention(q_proj, k_proj, v_proj, kv_list):
    ctx = lax.axis_size("ctx")
    tokens, width = q_proj.shape
    heads = width // HD // GROUP
    here = PLANE * FRAME
    lists = kv_list.T
    any_space = pl.BlockSpec(memory_space=pl.ANY)
    dma = pltpu.SemaphoreType.DMA
    bf16, f32 = jnp.bfloat16, jnp.float32
    return pl.pallas_call(
        functools.partial(plane_kernel, ctx, heads),
        out_shape=jax.ShapeDtypeStruct((tokens, width), bf16),
        in_specs=[any_space] * 4,
        out_specs=any_space,
        scratch_shapes=[
            pltpu.SMEM(lists.shape, jnp.int32),
            pltpu.SMEM((PLANE, STEPS), jnp.int32),
            pltpu.SMEM((PLANE * BPF, STEPS), jnp.int32),
            pltpu.VMEM((PLANE * BPF, 1, NEAR_KEYS), f32),
            pltpu.VMEM((PLANE * BPF, 1, FAR_KEYS), f32),
            pltpu.VMEM((heads, 2, NEAR, HD), bf16),
            pltpu.VMEM((heads, 2, 2, FAR, HD), bf16),
            pltpu.VMEM((heads, 2, 2, BLK, HD), bf16),
            pltpu.VMEM((heads, here, HD), bf16),
            pltpu.VMEM((heads, here, HD), bf16),
            pltpu.VMEM((heads, here, HD), f32),
            pltpu.VMEM((heads, here, HD), f32),
            pltpu.VMEM((heads, here, HD), f32),
            pltpu.VMEM((NEAR_KEYS, HD), bf16),
            pltpu.VMEM((NEAR_KEYS, HD), bf16),
            dma((1,)), dma((heads,)), dma((heads,)), dma((heads,)), dma((heads,)), dma((2, heads)),
            dma((2, FAR_SLOTS, heads)), dma((1,)),
            dma((heads,)), dma((heads,)), dma((2, heads)), dma((2, FAR_SLOTS, heads)), dma((heads,)),
        ],
        compiler_params=pltpu.CompilerParams(
            collective_id=0, has_side_effects=True, vmem_limit_bytes=30 * 1024 * 1024
        ),
    )(*[pltpu.with_memory_space_constraint(x, pltpu.HBM) for x in (lists, q_proj, k_proj, v_proj)])


def on_device(q_proj, k_proj, v_proj, kv_list):
    rep, uly = lax.axis_size("rep"), lax.axis_size("uly")
    if rep == 1 and uly == BPF and q_proj.shape[0] == BLK and lax.axis_size("ctx") % PLANE == 0:
        return plane_attention(q_proj, k_proj, v_proj, kv_list)
    return ring_attention(q_proj, k_proj, v_proj, kv_list)


def solution(mesh):
    rows = P(("groups", "ctx", "rep", "uly"), None)
    return jax.shard_map(
        on_device,
        mesh=mesh,
        in_specs=(rows, rows, rows, P("groups", None)),
        out_specs=rows,
        check_vma=False,
    )
```

```python
import functools
import math

import jax
import jax.numpy as jnp
from jax import lax
from jax.experimental import pallas as pl
from jax.experimental.pallas import tpu as pltpu
from jax.sharding import PartitionSpec as P

HD = 128
BLK = 128
BPF = 2
FRAME = BLK * BPF
REACH = 7
GROUP = 8
SLOTS = 2 * REACH
KEYS = (SLOTS + BPF) * BLK

very_low = -1e30
scale2 = math.log2(math.e) / math.sqrt(HD)
MESH = pl.DeviceIdType.MESH


def ring_kernel(sizes, sel_ref, bias_ref, q_ref, k_ref, v_ref, out_ref, kv, qb, ob, ks, vs,
           first_in, kv_in, q_in, kv_sent, q_sent, ring_in, ring_sent, out_in, out_sent):
    ctx, rep, uly, tokens, heads = sizes
    inner = GROUP // (rep * uly)
    here = GROUP * tokens
    frames_here = here // FRAME
    places = ctx // inner
    hops = -(-REACH // frames_here)
    c = lax.axis_index("ctx")
    r = lax.axis_index("rep")
    u = lax.axis_index("uly")
    place = c // inner
    me = (c % inner) * (rep * uly) + r * uly + u

    def member(j):
        return {"ctx": place * inner + j // (rep * uly), "rep": (j // uly) % rep, "uly": j % uly}

    def beside(step):
        return {"ctx": c + step * inner}

    has_left, has_right = place >= 1, place <= places - 2

    barrier = pltpu.get_barrier_semaphore()
    for k in range(1, GROUP):
        pl.semaphore_signal(barrier, inc=1, device_id=member((me + k) % GROUP), device_id_type=MESH)

    @pl.when(has_left)
    def _():
        pl.semaphore_signal(barrier, inc=1, device_id=beside(-1), device_id_type=MESH)

    @pl.when(has_right)
    def _():
        pl.semaphore_signal(barrier, inc=1, device_id=beside(1), device_id_type=MESH)

    neighbours = jnp.minimum(place, 1) + jnp.minimum(places - 1 - place, 1)
    pl.semaphore_wait(barrier, GROUP - 1 + neighbours)

    def columns(owner, h):
        return pl.ds(pl.multiple_of((owner * heads + h) * HD, HD), HD)

    own_rows = pl.ds(pl.multiple_of(REACH * FRAME + me * tokens, tokens), tokens)
    q_rows = pl.ds(pl.multiple_of(me * tokens, tokens), tokens)

    def share_kv(h, arrived):
        for k in range(1, GROUP):
            j = (me + k) % GROUP
            for which, src in enumerate((k_ref, v_ref)):
                pltpu.make_async_remote_copy(
                    src_ref=src.at[:, columns(j, h)], dst_ref=kv.at[h, which, own_rows],
                    send_sem=kv_sent.at[h], recv_sem=arrived(k),
                    device_id=member(j), device_id_type=MESH,
                ).start()
        for which, src in enumerate((k_ref, v_ref)):
            pltpu.make_async_copy(
                src.at[:, columns(me, h)], kv.at[h, which, own_rows], arrived(0)
            ).start()

    def share_later(h, carry):
        share_kv(h, lambda k: kv_in.at[h])
        return carry

    def share_q(h, carry):
        for k in range(1, GROUP):
            j = (me + k) % GROUP
            pltpu.make_async_remote_copy(
                src_ref=q_ref.at[:, columns(j, h)], dst_ref=qb.at[h, q_rows],
                send_sem=q_sent.at[h], recv_sem=q_in.at[h],
                device_id=member(j), device_id_type=MESH,
            ).start()
        pltpu.make_async_copy(q_ref.at[:, columns(me, h)], qb.at[h, q_rows], q_in.at[h]).start()
        return carry

    share_kv(0, lambda k: first_in.at[k])
    lax.fori_loop(1, heads, share_later, 0)
    lax.fori_loop(0, heads, share_q, 0)

    def await_bytes(ref, sem):
        pltpu.make_async_copy(ref, ref, sem).wait()

    def ring_copy(way, s, h):
        if way == 0:
            first, last, shift = max(0, REACH - s * frames_here), REACH - (s - 1) * frames_here, frames_here
        else:
            first = REACH + s * frames_here
            last, shift = min(frames_here + SLOTS, first + frames_here), -frames_here
        rows = (last - first) * FRAME
        return pltpu.make_async_remote_copy(
            src_ref=kv.at[h, :, pl.ds((first + shift) * FRAME, rows)],
            dst_ref=kv.at[h, :, pl.ds(first * FRAME, rows)],
            send_sem=ring_sent.at[way, s - 1, h], recv_sem=ring_in.at[way, s - 1, h],
            device_id=beside(1 if way == 0 else -1), device_id_type=MESH,
        )

    def sends(way, s):
        if way == 0:
            return (place >= s - 1) & has_right
        return (place + s <= places) & has_left

    def receives(way, s):
        return place >= s if way == 0 else place + s <= places - 1

    def ring_start(s, h):
        for way in (0, 1):
            @pl.when(sends(way, s))
            def _():
                ring_copy(way, s, h).start()

    def ring_arrived(s, h):
        for way in (0, 1):
            @pl.when(receives(way, s))
            def _():
                ring_copy(way, s, h).wait_recv()

    def attend(h):
        def one_frame(f, carry):
            own = pl.multiple_of((REACH + f) * FRAME, FRAME)
            ks[pl.ds(0, FRAME), :] = kv[h, 0, pl.ds(own, FRAME), :]
            vs[pl.ds(0, FRAME), :] = kv[h, 1, pl.ds(own, FRAME), :]

            def pick(i, carry):
                far = place * frames_here + f + i - REACH + i // REACH
                slot = jnp.minimum(jnp.maximum(far, 0), ctx - 1) - place * frames_here + REACH
                row = pl.multiple_of(slot * FRAME, FRAME)
                second = sel_ref[f, i] == 1
                to = pl.ds(pl.multiple_of(FRAME + i * BLK, BLK), BLK)
                for which, dst in ((0, ks), (1, vs)):
                    dst[to, :] = jnp.where(
                        second,
                        kv[h, which, pl.ds(row + BLK, BLK), :],
                        kv[h, which, pl.ds(row, BLK), :],
                    )
                return carry

            lax.fori_loop(0, SLOTS, pick, 0)

            def one_block(b, carry):
                rows = pl.ds(pl.multiple_of(f * FRAME + b * BLK, BLK), BLK)
                scores = lax.dot_general(
                    qb[h, rows, :], ks[...], (((1,), (1,)), ((), ())),
                    preferred_element_type=jnp.float32,
                )
                scores = scores * scale2 + bias_ref[f * BPF + b]
                weights = jnp.exp2(scores - jnp.max(scores, axis=1, keepdims=True))
                total = jnp.sum(weights, axis=1, keepdims=True)
                mixed = jnp.dot(
                    weights.astype(jnp.bfloat16), vs[...], preferred_element_type=jnp.float32
                )
                ob[h, rows, :] = (mixed / total).astype(jnp.bfloat16)
                return carry

            lax.fori_loop(0, BPF, one_block, 0)
            return carry

        lax.fori_loop(0, frames_here, one_frame, 0)

    def give_back(h):
        for k in range(1, GROUP):
            j = (me + k) % GROUP
            pltpu.make_async_remote_copy(
                src_ref=ob.at[h, pl.ds(pl.multiple_of(j * tokens, tokens), tokens)],
                dst_ref=out_ref.at[:, columns(me, h)],
                send_sem=out_sent.at[h], recv_sem=out_in.at[0],
                device_id=member(j), device_id_type=MESH,
            ).start()
        pltpu.make_async_copy(ob.at[h, q_rows], out_ref.at[:, columns(me, h)], out_in.at[0]).start()

    def step(t, carry):
        @pl.when((t >= 1) & (t < heads))
        def _():
            await_bytes(kv.at[t, :, pl.ds(REACH * FRAME, here)], kv_in.at[t])
            ring_start(1, t)

        for s in range(1, hops):
            @pl.when((t >= s) & (t < heads + s))
            def _():
                ring_arrived(s, t - s)
                ring_start(s + 1, t - s)

        @pl.when(t >= hops)
        def _():
            ring_arrived(hops, t - hops)
            await_bytes(qb.at[t - hops], q_in.at[t - hops])
            attend(t - hops)
            give_back(t - hops)

        return carry

    for k in range(GROUP):
        row = REACH * FRAME + (me + GROUP - k) % GROUP * tokens
        piece = kv.at[0, :, pl.ds(pl.multiple_of(row, tokens), tokens)]
        await_bytes(piece, first_in.at[k])
        for way in (0, 1):
            @pl.when(sends(way, 1))
            def _():
                to = row - here if way == 0 else row + here
                pltpu.make_async_remote_copy(
                    src_ref=piece, dst_ref=kv.at[0, :, pl.ds(pl.multiple_of(to, tokens), tokens)],
                    send_sem=ring_sent.at[way, 0, 0], recv_sem=ring_in.at[way, 0, 0],
                    device_id=beside(1 if way == 0 else -1), device_id_type=MESH,
                ).start()

    lax.fori_loop(0, heads + hops, step, 0)

    def finish(h, carry):
        others = (GROUP - 1) * tokens
        await_bytes(kv.at[h, :, pl.ds(0, others)], kv_sent.at[h])
        await_bytes(qb.at[h, pl.ds(0, others)], q_sent.at[h])
        await_bytes(ob.at[h, pl.ds(0, others)], out_sent.at[h])
        for s in range(1, hops + 1):
            for way in (0, 1):
                @pl.when(sends(way, s))
                def _():
                    ring_copy(way, s, h).wait_send()
        return carry

    lax.fori_loop(0, heads, finish, 0)
    await_bytes(out_ref, out_in.at[0])


def tables(kv_list, place, frames_here, frames):
    lists = lax.dynamic_slice_in_dim(kv_list, place * frames_here * BPF, frames_here * BPF, 0)
    lists = lists.reshape(frames_here, BPF, 1, -1)
    steps = jnp.array([d for d in range(-REACH, REACH + 1) if d != 0], jnp.int32)
    far = place * frames_here + jnp.arange(frames_here, dtype=jnp.int32)[:, None] + steps[None, :]
    inside = (far >= 0) & (far < frames)
    has = [jnp.any(lists == (far * BPF + b)[:, None, :, None], axis=3) for b in range(BPF)]
    listed = (has[0] | has[1]) & inside[:, None, :]
    sel = jnp.any(has[1], axis=1).astype(jnp.int32)
    bias = jnp.where(listed, 0.0, very_low).astype(jnp.float32)
    bias = jnp.concatenate([jnp.zeros((frames_here, BPF, BPF), jnp.float32), bias], axis=2)
    bias = jnp.repeat(bias.reshape(frames_here * BPF, BPF + SLOTS), BLK, axis=1)
    return sel, bias.reshape(frames_here * BPF, 1, KEYS)


def ring_attention(q_proj, k_proj, v_proj, kv_list):
    ctx, rep, uly = lax.axis_size("ctx"), lax.axis_size("rep"), lax.axis_size("uly")
    tokens, width = q_proj.shape
    heads = width // HD // GROUP
    inner = GROUP // (rep * uly)
    here = GROUP * tokens
    frames_here = here // FRAME
    hops = -(-REACH // frames_here)
    sel, bias = tables(kv_list, lax.axis_index("ctx") // inner, frames_here, ctx)
    window = (frames_here + SLOTS) * FRAME
    any_space = pl.BlockSpec(memory_space=pl.ANY)
    dma = pltpu.SemaphoreType.DMA
    return pl.pallas_call(
        functools.partial(ring_kernel, (ctx, rep, uly, tokens, heads)),
        out_shape=jax.ShapeDtypeStruct((tokens, width), jnp.bfloat16),
        in_specs=[
            pl.BlockSpec(memory_space=pltpu.SMEM),
            pl.BlockSpec(memory_space=pltpu.VMEM),
            any_space, any_space, any_space,
        ],
        out_specs=any_space,
        scratch_shapes=[
            pltpu.VMEM((heads, 2, window, HD), jnp.bfloat16),
            pltpu.VMEM((heads, here, HD), jnp.bfloat16),
            pltpu.VMEM((heads, here, HD), jnp.bfloat16),
            pltpu.VMEM((KEYS, HD), jnp.bfloat16),
            pltpu.VMEM((KEYS, HD), jnp.bfloat16),
            dma((GROUP,)), dma((heads,)), dma((heads,)), dma((heads,)), dma((heads,)),
            dma((2, hops, heads)), dma((2, hops, heads)), dma((1,)), dma((heads,)),
        ],
        compiler_params=pltpu.CompilerParams(
            collective_id=0, has_side_effects=True, vmem_limit_bytes=56 * 1024 * 1024
        ),
    )(sel, bias, q_proj, k_proj, v_proj)


PLANE = 4
NEAR = 3 * PLANE * FRAME
NEAR_KEYS = NEAR // 2 + BLK
FAR_SLOTS = 3
FAR = (2 * FAR_SLOTS - 1) * BLK
FAR_KEYS = FAR_SLOTS * BLK
STEPS = 2 * REACH + 1
PEERS = (2, 1, 3, 4, 6, 5, 7)


def plane_kernel(ctx, heads, list_ref, q_ref, k_ref, v_ref, out_ref,
                 lists, sel, listed, bias_near, bias_far, near, far, chosen, qb, ob, part, high, low, ks, vs,
                 list_in, own_in, beside_in, plane_in, q_in, ring_in, far_in, out_in,
                 plane_sent, q_sent, ring_sent, far_sent, out_sent):
    here = PLANE * FRAME
    places = ctx // PLANE
    c = lax.axis_index("ctx")
    u = lax.axis_index("uly")
    place = c // PLANE
    me = (c % PLANE) * BPF + u

    def member(j):
        return {"ctx": place * PLANE + j // BPF, "uly": j % BPF}

    def beside(way):
        return {"ctx": c + (PLANE if way == 0 else -PLANE)}

    def peer(k):
        bits = (me % 2, (me // 2) % 2, me // 4)
        return sum((1 - bit if (k >> n) & 1 else bit) << n for n, bit in enumerate(bits))

    has = (place <= places - 2, place >= 1)
    gets = (place >= 1, place <= places - 2)
    sends_far = ((place >= 1) & (place <= places - 2),) * 2
    gets_far = (place >= 2, place <= places - 3)

    def columns(owner, h):
        return pl.ds(pl.multiple_of((owner * heads + h) * HD, HD), HD)

    def rows_of(j, base=0):
        return pl.ds(pl.multiple_of(base + j * BLK, BLK), BLK)

    def await_bytes(ref, sem):
        pltpu.make_async_copy(ref, ref, sem).wait()

    def fetch_own(h, carry):
        for which, src in enumerate((k_ref, v_ref)):
            pltpu.make_async_copy(
                src.at[:, columns(me, h)], near.at[h, which, rows_of(me, here)], own_in.at[h]
            ).start()
        return carry

    barrier = pltpu.get_barrier_semaphore()
    for way in (0, 1):
        @pl.when(has[way])
        def _():
            pl.semaphore_signal(barrier, inc=1, device_id=beside(way), device_id_type=MESH)
    for k in PEERS:
        pl.semaphore_signal(barrier, inc=1, device_id=member(peer(k)), device_id_type=MESH)
    lax.fori_loop(0, heads, fetch_own, 0)
    neighbours = jnp.minimum(place, 1) + jnp.minimum(places - 1 - place, 1)
    pl.semaphore_wait(barrier, GROUP - 1 + neighbours)

    lands = (0, 2 * here)

    def ring_piece(h, j):
        for way in (0, 1):
            @pl.when(has[way])
            def _():
                pltpu.make_async_remote_copy(
                    src_ref=near.at[h, :, rows_of(j, here)], dst_ref=near.at[h, :, rows_of(j, lands[way])],
                    send_sem=ring_sent.at[way, h], recv_sem=ring_in.at[way, h],
                    device_id=beside(way), device_id_type=MESH,
                ).start()

    def share_kv(h, carry):
        for k in PEERS:
            j = peer(k)
            for which, src in enumerate((k_ref, v_ref)):
                pltpu.make_async_remote_copy(
                    src_ref=src.at[:, columns(j, h)], dst_ref=near.at[h, which, rows_of(me, here)],
                    send_sem=plane_sent.at[h], recv_sem=(beside_in if k == 2 else plane_in).at[h],
                    device_id=member(j), device_id_type=MESH,
                ).start()
        return carry

    def share_q(h, carry):
        for k in PEERS:
            j = peer(k)
            pltpu.make_async_remote_copy(
                src_ref=q_ref.at[:, columns(j, h)], dst_ref=qb.at[h, rows_of(me)],
                send_sem=q_sent.at[h], recv_sem=q_in.at[h],
                device_id=member(j), device_id_type=MESH,
            ).start()
        pltpu.make_async_copy(q_ref.at[:, columns(me, h)], qb.at[h, rows_of(me)], q_in.at[h]).start()
        return carry

    def ring_own(h, carry):
        await_bytes(near.at[h, :, pl.ds(here, BLK)], own_in.at[h])
        ring_piece(h, me)
        return carry

    lax.fori_loop(0, heads, ring_own, 0)
    lax.fori_loop(0, heads, share_kv, 0)
    lax.fori_loop(0, heads, share_q, 0)
    get_lists = pltpu.make_async_copy(list_ref, lists, list_in.at[0])
    get_lists.start()

    def ring_beside(h, carry):
        await_bytes(near.at[h, :, pl.ds(here, BLK)], beside_in.at[h])
        ring_piece(h, peer(2))
        return carry

    lax.fori_loop(0, heads, ring_beside, 0)

    for way in (0, 1):
        @pl.when(jnp.logical_not(gets[way]))
        def _():
            def clear(h, carry):
                for which in (0, 1):
                    near[h, which, pl.ds(lands[way], here), :] = jnp.zeros((here, HD), jnp.bfloat16)
                return carry

            lax.fori_loop(0, heads, clear, 0)

        @pl.when(jnp.logical_not(gets_far[way]))
        def _():
            def clear(h, carry):
                for which in (0, 1):
                    far[h, way, which] = jnp.zeros((FAR, HD), jnp.bfloat16)
                return carry

            lax.fori_loop(0, heads, clear, 0)

    get_lists.wait()

    def count(row, block):
        return sum((lists[j, row] == block).astype(jnp.int32) for j in range(lists.shape[0]))

    def tables(n, carry):
        a, d = n // STEPS, n % STEPS
        target = place * PLANE + a + d - REACH
        block = jnp.where(target < 0, -BLK, target * BPF)
        second = 0
        for b in range(BPF):
            row = (place * PLANE + a) * BPF + b
            one = count(row, block + 1)
            listed[a * BPF + b, d] = jnp.minimum(count(row, block) + one, 1)
            second = second + one
        sel[a, d] = jnp.minimum(second, 1)
        return carry

    lax.fori_loop(0, PLANE * STEPS, tables, 0)

    def fill(ref, r, slot, d):
        value = jnp.where(listed[r, d] == 1, 0.0, very_low)
        ref[r, :, pl.ds(pl.multiple_of(slot * BLK, BLK), BLK)] = jnp.full((1, BLK), value, jnp.float32)

    def biases(r, carry):
        a = r // BPF
        bias_near[r, :, pl.ds(0, FRAME)] = jnp.zeros((1, FRAME), jnp.float32)

        def one_near(i, carry):
            w = i + (i + REACH - PLANE - a) // REACH
            fill(bias_near, r, BPF + i, jnp.minimum(w + REACH - PLANE - a, STEPS - 1))
            return carry

        def one_far(i, carry):
            right = (i + a) // FAR_SLOTS
            fill(bias_far, r, i, i + right * (STEPS - FAR_SLOTS))
            return carry

        lax.fori_loop(0, 3 * PLANE - 1, one_near, 0)
        lax.fori_loop(0, FAR_SLOTS, one_far, 0)
        return carry

    lax.fori_loop(0, PLANE * BPF, biases, 0)

    def ring_rest(h, carry):
        await_bytes(near.at[h, :, pl.ds(here, here - BPF * BLK)], plane_in.at[h])
        for k in PEERS[1:]:
            ring_piece(h, peer(k))
        return carry

    lax.fori_loop(0, heads, ring_rest, 0)

    frames = ctx
    onward = (
        (jnp.minimum((place + 1) * PLANE, frames - 1), place * PLANE - PLANE + 1),
        (jnp.maximum((place - 1) * PLANE + PLANE - 1, 0), place * PLANE + PLANE + 2),
    )
    takes_second = [
        (count(f * BPF, g * BPF + 1) + count(f * BPF + 1, g * BPF + 1)) > 0 for f, g in onward
    ]

    def far_copy(way, n, h):
        b = 3 - n if way == 0 else 2 * PLANE + n
        whole = n < FAR_SLOTS - 1
        rows = FRAME if whole else BLK
        return pltpu.make_async_remote_copy(
            src_ref=near.at[h, :, pl.ds(b * FRAME, rows)] if whole else chosen.at[h, way],
            dst_ref=far.at[h, way, :, pl.ds(n * FRAME, rows)],
            send_sem=far_sent.at[way, n, h], recv_sem=far_in.at[way, n, h],
            device_id=beside(way), device_id_type=MESH,
        )

    def attend_near(h):
        def one_frame(a, carry):
            own = pl.multiple_of((PLANE + a) * FRAME, FRAME)
            ks[pl.ds(0, FRAME), :] = near[h, 0, pl.ds(own, FRAME), :]
            vs[pl.ds(0, FRAME), :] = near[h, 1, pl.ds(own, FRAME), :]

            def pick(i, carry):
                w = i + (i + REACH - PLANE - a) // REACH
                row = pl.multiple_of(w * FRAME, FRAME)
                second = sel[a, jnp.minimum(w + REACH - PLANE - a, STEPS - 1)] == 1
                to = pl.ds(pl.multiple_of(FRAME + i * BLK, BLK), BLK)
                for which, dst in ((0, ks), (1, vs)):
                    dst[to, :] = jnp.where(
                        second, near[h, which, pl.ds(row + BLK, BLK), :], near[h, which, pl.ds(row, BLK), :]
                    )
                return carry

            lax.fori_loop(0, 3 * PLANE - 1, pick, 0)
            rows = pl.ds(pl.multiple_of(a * FRAME, FRAME), FRAME)
            scores = lax.dot_general(
                qb[h, rows, :], ks[...], (((1,), (1,)), ((), ())), preferred_element_type=jnp.float32
            ).reshape(BPF, BLK, NEAR_KEYS)
            scores = scores * scale2 + bias_near[pl.ds(a * BPF, BPF)]
            top = jnp.max(scores, axis=2, keepdims=True)
            weights = jnp.exp2(scores - top)
            total = jnp.sum(weights, axis=2, keepdims=True)
            part[h, rows, :] = jnp.dot(
                weights.reshape(FRAME, NEAR_KEYS).astype(jnp.bfloat16), vs[...],
                preferred_element_type=jnp.float32,
            )
            high[h, rows, :] = jnp.broadcast_to(top, (BPF, BLK, HD)).reshape(FRAME, HD)
            low[h, rows, :] = jnp.broadcast_to(total, (BPF, BLK, HD)).reshape(FRAME, HD)
            return carry

        lax.fori_loop(0, PLANE, one_frame, 0)

    def attend_far(h, a):
        def pick(i, carry):
            right = (i + a) // FAR_SLOTS
            pair = (1 - right) * (FAR_SLOTS - 1 - a - i) + right * (i + a - FAR_SLOTS)
            whole = 1 - pair // (FAR_SLOTS - 1)
            row = pl.multiple_of(pair * FRAME, FRAME)
            row_b = pl.multiple_of(pair * FRAME + whole * BLK, BLK)
            second = sel[a, i + right * (STEPS - FAR_SLOTS)] == 1
            to = pl.ds(pl.multiple_of(i * BLK, BLK), BLK)
            for which, dst in ((0, ks), (1, vs)):
                dst[to, :] = jnp.where(
                    second, far[h, right, which, pl.ds(row_b, BLK), :], far[h, right, which, pl.ds(row, BLK), :]
                )
            return carry

        lax.fori_loop(0, FAR_SLOTS, pick, 0)
        rows = pl.ds(pl.multiple_of(a * FRAME, FRAME), FRAME)
        keys = pl.ds(0, FAR_KEYS)
        scores = lax.dot_general(
            qb[h, rows, :], ks[keys, :], (((1,), (1,)), ((), ())), preferred_element_type=jnp.float32
        ).reshape(BPF, BLK, FAR_KEYS)
        scores = (scores * scale2 + bias_far[pl.ds(a * BPF, BPF)]).reshape(FRAME, FAR_KEYS)
        before = high[h, rows, :]
        top = jnp.maximum(before, jnp.max(scores, axis=1, keepdims=True))
        weights = jnp.exp2(scores - jnp.concatenate([top] * FAR_SLOTS, axis=1))
        fade = jnp.exp2(before - top)
        total = fade * low[h, rows, :] + jnp.sum(weights, axis=1, keepdims=True)
        mixed = fade * part[h, rows, :] + jnp.dot(
            weights.astype(jnp.bfloat16), vs[keys, :], preferred_element_type=jnp.float32
        )
        ob[h, rows, :] = (mixed / total).astype(jnp.bfloat16)

    def fold(h, a, n, last):
        right = 1 - falling
        i = falling * (FAR_SLOTS - 1 - a - n) + right * (n + FAR_SLOTS - a)
        second = sel[a, i + right * (STEPS - FAR_SLOTS)] == 1
        keys, values = [
            far[h, right, which, pl.ds(n * FRAME, BLK), :] if n == FAR_SLOTS - 1 else jnp.where(
                second, far[h, right, which, pl.ds(n * FRAME + BLK, BLK), :], far[h, right, which, pl.ds(n * FRAME, BLK), :]
            )
            for which in (0, 1)
        ]
        slot = pl.ds(pl.multiple_of(i * BLK, BLK), BLK)
        rows = pl.ds(pl.multiple_of(a * FRAME, FRAME), FRAME)
        scores = lax.dot_general(
            qb[h, rows, :], keys, (((1,), (1,)), ((), ())), preferred_element_type=jnp.float32
        ).reshape(BPF, BLK, BLK)
        scores = (scores * scale2 + bias_far[pl.ds(a * BPF, BPF), :, slot]).reshape(FRAME, BLK)
        before = high[h, rows, :]
        top = jnp.maximum(before, jnp.max(scores, axis=1, keepdims=True))
        weights = jnp.exp2(scores - top)
        fade = jnp.exp2(before - top)
        total = fade * low[h, rows, :] + jnp.sum(weights, axis=1, keepdims=True)
        mixed = fade * part[h, rows, :] + jnp.dot(
            weights.astype(jnp.bfloat16), values, preferred_element_type=jnp.float32
        )
        if last:
            ob[h, rows, :] = (mixed / total).astype(jnp.bfloat16)
        else:
            high[h, rows, :] = top
            low[h, rows, :] = total
            part[h, rows, :] = mixed

    def give_back(h, a):
        for b in range(BPF):
            j = a * BPF + (b + 1 - u) % BPF

            @pl.when(j != me)
            def _():
                pltpu.make_async_remote_copy(
                    src_ref=ob.at[h, rows_of(j)], dst_ref=out_ref.at[:, columns(me, h)],
                    send_sem=out_sent.at[h], recv_sem=out_in.at[0],
                    device_id=member(j), device_id_type=MESH,
                ).start()

            @pl.when(j == me)
            def _():
                pltpu.make_async_copy(ob.at[h, rows_of(j)], out_ref.at[:, columns(me, h)], out_in.at[0]).start()

    def first_phase(h, carry):
        for way in (0, 1):
            @pl.when(gets[way])
            def _():
                await_bytes(near.at[h, :, pl.ds(lands[way], here)], ring_in.at[way, h])

        for way in (0, 1):
            @pl.when(sends_far[way])
            def _():
                frame = 1 if way == 0 else 2 * PLANE + 2
                for which in (0, 1):
                    chosen[h, way, which] = jnp.where(
                        takes_second[way],
                        near[h, which, pl.ds(frame * FRAME + BLK, BLK), :],
                        near[h, which, pl.ds(frame * FRAME, BLK), :],
                    )
                for n in range(FAR_SLOTS):
                    far_copy(way, n, h).start()

        await_bytes(qb.at[h], q_in.at[h])
        attend_near(h)
        return carry

    lax.fori_loop(0, heads, first_phase, 0)

    both = gets_far[0] & gets_far[1]
    neither = jnp.logical_not(gets_far[0] | gets_far[1])
    falling = jnp.where(gets_far[0], 1, 0)

    others = (GROUP - 1) * BLK

    def await_far_sent(h):
        for way in (0, 1):
            @pl.when(sends_far[way])
            def _():
                for n in range(FAR_SLOTS):
                    far_copy(way, n, h).wait_send()

    def await_out_sent(h):
        await_bytes(ob.at[h, pl.ds(0, others)], out_sent.at[h])

    def second_phase(h, carry):
        await_bytes(near.at[h, :, pl.ds(0, others)], plane_sent.at[h])
        await_bytes(qb.at[h, pl.ds(0, others)], q_sent.at[h])
        for way in (0, 1):
            @pl.when(has[way])
            def _():
                await_bytes(near.at[h, :, pl.ds(0, here)], ring_sent.at[way, h])

        @pl.when(h >= 1)
        def _():
            await_far_sent(h - 1)
            await_out_sent(h - 1)

        @pl.when(both | neither)
        def _():
            for way in (0, 1):
                @pl.when(both)
                def _():
                    for n in range(FAR_SLOTS):
                        far_copy(way, n, h).wait_recv()

            def one(a, carry):
                attend_far(h, a)
                give_back(h, a)
                return carry

            lax.fori_loop(0, PLANE, one, 0)

        @pl.when(jnp.logical_not(both | neither))
        def _():
            free = falling * (PLANE - 1)
            rows = pl.ds(pl.multiple_of(free * FRAME, FRAME), FRAME)
            ob[h, rows, :] = (part[h, rows, :] / low[h, rows, :]).astype(jnp.bfloat16)
            give_back(h, free)
            for n in range(FAR_SLOTS):
                for way in (0, 1):
                    @pl.when(gets_far[way])
                    def _():
                        far_copy(way, n, h).wait_recv()

                done = falling * (FAR_SLOTS - 1 - n) + (1 - falling) * (n + 1)
                fold(h, done, n, True)
                give_back(h, done)
                for j in range(1, FAR_SLOTS - n):
                    fold(h, done + (1 - 2 * falling) * j, n, False)

        return carry

    lax.fori_loop(0, heads, second_phase, 0)

    await_far_sent(heads - 1)
    await_out_sent(heads - 1)
    await_bytes(out_ref, out_in.at[0])


def plane_attention(q_proj, k_proj, v_proj, kv_list):
    ctx = lax.axis_size("ctx")
    tokens, width = q_proj.shape
    heads = width // HD // GROUP
    here = PLANE * FRAME
    lists = kv_list.T
    any_space = pl.BlockSpec(memory_space=pl.ANY)
    dma = pltpu.SemaphoreType.DMA
    bf16, f32 = jnp.bfloat16, jnp.float32
    return pl.pallas_call(
        functools.partial(plane_kernel, ctx, heads),
        out_shape=jax.ShapeDtypeStruct((tokens, width), bf16),
        in_specs=[any_space] * 4,
        out_specs=any_space,
        scratch_shapes=[
            pltpu.SMEM(lists.shape, jnp.int32),
            pltpu.SMEM((PLANE, STEPS), jnp.int32),
            pltpu.SMEM((PLANE * BPF, STEPS), jnp.int32),
            pltpu.VMEM((PLANE * BPF, 1, NEAR_KEYS), f32),
            pltpu.VMEM((PLANE * BPF, 1, FAR_KEYS), f32),
            pltpu.VMEM((heads, 2, NEAR, HD), bf16),
            pltpu.VMEM((heads, 2, 2, FAR, HD), bf16),
            pltpu.VMEM((heads, 2, 2, BLK, HD), bf16),
            pltpu.VMEM((heads, here, HD), bf16),
            pltpu.VMEM((heads, here, HD), bf16),
            pltpu.VMEM((heads, here, HD), f32),
            pltpu.VMEM((heads, here, HD), f32),
            pltpu.VMEM((heads, here, HD), f32),
            pltpu.VMEM((NEAR_KEYS, HD), bf16),
            pltpu.VMEM((NEAR_KEYS, HD), bf16),
            dma((1,)), dma((heads,)), dma((heads,)), dma((heads,)), dma((heads,)), dma((2, heads)),
            dma((2, FAR_SLOTS, heads)), dma((1,)),
            dma((heads,)), dma((heads,)), dma((2, heads)), dma((2, FAR_SLOTS, heads)), dma((heads,)),
        ],
        compiler_params=pltpu.CompilerParams(
            collective_id=0, has_side_effects=True, vmem_limit_bytes=30 * 1024 * 1024
        ),
    )(*[pltpu.with_memory_space_constraint(x, pltpu.HBM) for x in (lists, q_proj, k_proj, v_proj)])


def on_device(q_proj, k_proj, v_proj, kv_list):
    rep, uly = lax.axis_size("rep"), lax.axis_size("uly")
    if rep == 1 and uly == BPF and q_proj.shape[0] == BLK and lax.axis_size("ctx") % PLANE == 0:
        return plane_attention(q_proj, k_proj, v_proj, kv_list)
    return ring_attention(q_proj, k_proj, v_proj, kv_list)


def solution(mesh):
    rows = P(("groups", "ctx", "rep", "uly"), None)
    return jax.shard_map(
        on_device,
        mesh=mesh,
        in_specs=(rows, rows, rows, P("groups", None)),
        out_specs=rows,
        check_vma=False,
    )
```

```python
import functools
import math

import jax
import jax.numpy as jnp
from jax import lax
from jax.experimental import pallas as pl
from jax.experimental.pallas import tpu as pltpu
from jax.sharding import PartitionSpec as P

HD = 128
BLK = 128
BPF = 2
FRAME = BLK * BPF
REACH = 7
GROUP = 8
SLOTS = 2 * REACH
KEYS = (SLOTS + BPF) * BLK

very_low = -1e30
scale2 = math.log2(math.e) / math.sqrt(HD)
MESH = pl.DeviceIdType.MESH


def ring_kernel(sizes, sel_ref, bias_ref, q_ref, k_ref, v_ref, out_ref, kv, qb, ob, ks, vs,
           first_in, kv_in, q_in, kv_sent, q_sent, ring_in, ring_sent, out_in, out_sent):
    ctx, rep, uly, tokens, heads = sizes
    inner = GROUP // (rep * uly)
    here = GROUP * tokens
    frames_here = here // FRAME
    places = ctx // inner
    hops = -(-REACH // frames_here)
    c = lax.axis_index("ctx")
    r = lax.axis_index("rep")
    u = lax.axis_index("uly")
    place = c // inner
    me = (c % inner) * (rep * uly) + r * uly + u

    def member(j):
        return {"ctx": place * inner + j // (rep * uly), "rep": (j // uly) % rep, "uly": j % uly}

    def beside(step):
        return {"ctx": c + step * inner}

    has_left, has_right = place >= 1, place <= places - 2

    barrier = pltpu.get_barrier_semaphore()
    for k in range(1, GROUP):
        pl.semaphore_signal(barrier, inc=1, device_id=member((me + k) % GROUP), device_id_type=MESH)

    @pl.when(has_left)
    def _():
        pl.semaphore_signal(barrier, inc=1, device_id=beside(-1), device_id_type=MESH)

    @pl.when(has_right)
    def _():
        pl.semaphore_signal(barrier, inc=1, device_id=beside(1), device_id_type=MESH)

    neighbours = jnp.minimum(place, 1) + jnp.minimum(places - 1 - place, 1)
    pl.semaphore_wait(barrier, GROUP - 1 + neighbours)

    def columns(owner, h):
        return pl.ds(pl.multiple_of((owner * heads + h) * HD, HD), HD)

    own_rows = pl.ds(pl.multiple_of(REACH * FRAME + me * tokens, tokens), tokens)
    q_rows = pl.ds(pl.multiple_of(me * tokens, tokens), tokens)

    def share_kv(h, arrived):
        for k in range(1, GROUP):
            j = (me + k) % GROUP
            for which, src in enumerate((k_ref, v_ref)):
                pltpu.make_async_remote_copy(
                    src_ref=src.at[:, columns(j, h)], dst_ref=kv.at[h, which, own_rows],
                    send_sem=kv_sent.at[h], recv_sem=arrived(k),
                    device_id=member(j), device_id_type=MESH,
                ).start()
        for which, src in enumerate((k_ref, v_ref)):
            pltpu.make_async_copy(
                src.at[:, columns(me, h)], kv.at[h, which, own_rows], arrived(0)
            ).start()

    def share_later(h, carry):
        share_kv(h, lambda k: kv_in.at[h])
        return carry

    def share_q(h, carry):
        for k in range(1, GROUP):
            j = (me + k) % GROUP
            pltpu.make_async_remote_copy(
                src_ref=q_ref.at[:, columns(j, h)], dst_ref=qb.at[h, q_rows],
                send_sem=q_sent.at[h], recv_sem=q_in.at[h],
                device_id=member(j), device_id_type=MESH,
            ).start()
        pltpu.make_async_copy(q_ref.at[:, columns(me, h)], qb.at[h, q_rows], q_in.at[h]).start()
        return carry

    share_kv(0, lambda k: first_in.at[k])
    lax.fori_loop(1, heads, share_later, 0)
    lax.fori_loop(0, heads, share_q, 0)

    def await_bytes(ref, sem):
        pltpu.make_async_copy(ref, ref, sem).wait()

    def ring_copy(way, s, h):
        if way == 0:
            first, last, shift = max(0, REACH - s * frames_here), REACH - (s - 1) * frames_here, frames_here
        else:
            first = REACH + s * frames_here
            last, shift = min(frames_here + SLOTS, first + frames_here), -frames_here
        rows = (last - first) * FRAME
        return pltpu.make_async_remote_copy(
            src_ref=kv.at[h, :, pl.ds((first + shift) * FRAME, rows)],
            dst_ref=kv.at[h, :, pl.ds(first * FRAME, rows)],
            send_sem=ring_sent.at[way, s - 1, h], recv_sem=ring_in.at[way, s - 1, h],
            device_id=beside(1 if way == 0 else -1), device_id_type=MESH,
        )

    def sends(way, s):
        if way == 0:
            return (place >= s - 1) & has_right
        return (place + s <= places) & has_left

    def receives(way, s):
        return place >= s if way == 0 else place + s <= places - 1

    def ring_start(s, h):
        for way in (0, 1):
            @pl.when(sends(way, s))
            def _():
                ring_copy(way, s, h).start()

    def ring_arrived(s, h):
        for way in (0, 1):
            @pl.when(receives(way, s))
            def _():
                ring_copy(way, s, h).wait_recv()

    def attend(h):
        def one_frame(f, carry):
            own = pl.multiple_of((REACH + f) * FRAME, FRAME)
            ks[pl.ds(0, FRAME), :] = kv[h, 0, pl.ds(own, FRAME), :]
            vs[pl.ds(0, FRAME), :] = kv[h, 1, pl.ds(own, FRAME), :]

            def pick(i, carry):
                far = place * frames_here + f + i - REACH + i // REACH
                slot = jnp.minimum(jnp.maximum(far, 0), ctx - 1) - place * frames_here + REACH
                row = pl.multiple_of(slot * FRAME, FRAME)
                second = sel_ref[f, i] == 1
                to = pl.ds(pl.multiple_of(FRAME + i * BLK, BLK), BLK)
                for which, dst in ((0, ks), (1, vs)):
                    dst[to, :] = jnp.where(
                        second,
                        kv[h, which, pl.ds(row + BLK, BLK), :],
                        kv[h, which, pl.ds(row, BLK), :],
                    )
                return carry

            lax.fori_loop(0, SLOTS, pick, 0)

            def one_block(b, carry):
                rows = pl.ds(pl.multiple_of(f * FRAME + b * BLK, BLK), BLK)
                scores = lax.dot_general(
                    qb[h, rows, :], ks[...], (((1,), (1,)), ((), ())),
                    preferred_element_type=jnp.float32,
                )
                scores = scores * scale2 + bias_ref[f * BPF + b]
                weights = jnp.exp2(scores - jnp.max(scores, axis=1, keepdims=True))
                total = jnp.sum(weights, axis=1, keepdims=True)
                mixed = jnp.dot(
                    weights.astype(jnp.bfloat16), vs[...], preferred_element_type=jnp.float32
                )
                ob[h, rows, :] = (mixed / total).astype(jnp.bfloat16)
                return carry

            lax.fori_loop(0, BPF, one_block, 0)
            return carry

        lax.fori_loop(0, frames_here, one_frame, 0)

    def give_back(h):
        for k in range(1, GROUP):
            j = (me + k) % GROUP
            pltpu.make_async_remote_copy(
                src_ref=ob.at[h, pl.ds(pl.multiple_of(j * tokens, tokens), tokens)],
                dst_ref=out_ref.at[:, columns(me, h)],
                send_sem=out_sent.at[h], recv_sem=out_in.at[0],
                device_id=member(j), device_id_type=MESH,
            ).start()
        pltpu.make_async_copy(ob.at[h, q_rows], out_ref.at[:, columns(me, h)], out_in.at[0]).start()

    def step(t, carry):
        @pl.when((t >= 1) & (t < heads))
        def _():
            await_bytes(kv.at[t, :, pl.ds(REACH * FRAME, here)], kv_in.at[t])
            ring_start(1, t)

        for s in range(1, hops):
            @pl.when((t >= s) & (t < heads + s))
            def _():
                ring_arrived(s, t - s)
                ring_start(s + 1, t - s)

        @pl.when(t >= hops)
        def _():
            ring_arrived(hops, t - hops)
            await_bytes(qb.at[t - hops], q_in.at[t - hops])
            attend(t - hops)
            give_back(t - hops)

        return carry

    for k in range(GROUP):
        row = REACH * FRAME + (me + GROUP - k) % GROUP * tokens
        piece = kv.at[0, :, pl.ds(pl.multiple_of(row, tokens), tokens)]
        await_bytes(piece, first_in.at[k])
        for way in (0, 1):
            @pl.when(sends(way, 1))
            def _():
                to = row - here if way == 0 else row + here
                pltpu.make_async_remote_copy(
                    src_ref=piece, dst_ref=kv.at[0, :, pl.ds(pl.multiple_of(to, tokens), tokens)],
                    send_sem=ring_sent.at[way, 0, 0], recv_sem=ring_in.at[way, 0, 0],
                    device_id=beside(1 if way == 0 else -1), device_id_type=MESH,
                ).start()

    lax.fori_loop(0, heads + hops, step, 0)

    def finish(h, carry):
        others = (GROUP - 1) * tokens
        await_bytes(kv.at[h, :, pl.ds(0, others)], kv_sent.at[h])
        await_bytes(qb.at[h, pl.ds(0, others)], q_sent.at[h])
        await_bytes(ob.at[h, pl.ds(0, others)], out_sent.at[h])
        for s in range(1, hops + 1):
            for way in (0, 1):
                @pl.when(sends(way, s))
                def _():
                    ring_copy(way, s, h).wait_send()
        return carry

    lax.fori_loop(0, heads, finish, 0)
    await_bytes(out_ref, out_in.at[0])


def tables(kv_list, place, frames_here, frames):
    lists = lax.dynamic_slice_in_dim(kv_list, place * frames_here * BPF, frames_here * BPF, 0)
    lists = lists.reshape(frames_here, BPF, 1, -1)
    steps = jnp.array([d for d in range(-REACH, REACH + 1) if d != 0], jnp.int32)
    far = place * frames_here + jnp.arange(frames_here, dtype=jnp.int32)[:, None] + steps[None, :]
    inside = (far >= 0) & (far < frames)
    has = [jnp.any(lists == (far * BPF + b)[:, None, :, None], axis=3) for b in range(BPF)]
    listed = (has[0] | has[1]) & inside[:, None, :]
    sel = jnp.any(has[1], axis=1).astype(jnp.int32)
    bias = jnp.where(listed, 0.0, very_low).astype(jnp.float32)
    bias = jnp.concatenate([jnp.zeros((frames_here, BPF, BPF), jnp.float32), bias], axis=2)
    bias = jnp.repeat(bias.reshape(frames_here * BPF, BPF + SLOTS), BLK, axis=1)
    return sel, bias.reshape(frames_here * BPF, 1, KEYS)


def ring_attention(q_proj, k_proj, v_proj, kv_list):
    ctx, rep, uly = lax.axis_size("ctx"), lax.axis_size("rep"), lax.axis_size("uly")
    tokens, width = q_proj.shape
    heads = width // HD // GROUP
    inner = GROUP // (rep * uly)
    here = GROUP * tokens
    frames_here = here // FRAME
    hops = -(-REACH // frames_here)
    sel, bias = tables(kv_list, lax.axis_index("ctx") // inner, frames_here, ctx)
    window = (frames_here + SLOTS) * FRAME
    any_space = pl.BlockSpec(memory_space=pl.ANY)
    dma = pltpu.SemaphoreType.DMA
    return pl.pallas_call(
        functools.partial(ring_kernel, (ctx, rep, uly, tokens, heads)),
        out_shape=jax.ShapeDtypeStruct((tokens, width), jnp.bfloat16),
        in_specs=[
            pl.BlockSpec(memory_space=pltpu.SMEM),
            pl.BlockSpec(memory_space=pltpu.VMEM),
            any_space, any_space, any_space,
        ],
        out_specs=any_space,
        scratch_shapes=[
            pltpu.VMEM((heads, 2, window, HD), jnp.bfloat16),
            pltpu.VMEM((heads, here, HD), jnp.bfloat16),
            pltpu.VMEM((heads, here, HD), jnp.bfloat16),
            pltpu.VMEM((KEYS, HD), jnp.bfloat16),
            pltpu.VMEM((KEYS, HD), jnp.bfloat16),
            dma((GROUP,)), dma((heads,)), dma((heads,)), dma((heads,)), dma((heads,)),
            dma((2, hops, heads)), dma((2, hops, heads)), dma((1,)), dma((heads,)),
        ],
        compiler_params=pltpu.CompilerParams(
            collective_id=0, has_side_effects=True, vmem_limit_bytes=56 * 1024 * 1024
        ),
    )(sel, bias, q_proj, k_proj, v_proj)


PLANE = 4
NEAR = 3 * PLANE * FRAME
NEAR_KEYS = NEAR // 2 + BLK
FAR_SLOTS = 3
FAR = (2 * FAR_SLOTS - 1) * BLK
FAR_KEYS = FAR_SLOTS * BLK
STEPS = 2 * REACH + 1
PEERS = (2, 1, 3, 4, 6, 5, 7)


def plane_kernel(ctx, heads, list_ref, q_ref, k_ref, v_ref, out_ref,
                 lists, sel, listed, bias_near, bias_far, near, far, chosen, qb, ob, part, high, low, ks, vs,
                 list_in, own_in, beside_in, plane_in, q_in, ring_in, far_in, out_in,
                 plane_sent, q_sent, ring_sent, far_sent, out_sent):
    here = PLANE * FRAME
    places = ctx // PLANE
    c = lax.axis_index("ctx")
    u = lax.axis_index("uly")
    place = c // PLANE
    me = (c % PLANE) * BPF + u

    def member(j):
        return {"ctx": place * PLANE + j // BPF, "uly": j % BPF}

    def beside(way):
        return {"ctx": c + (PLANE if way == 0 else -PLANE)}

    def peer(k):
        bits = (me % 2, (me // 2) % 2, me // 4)
        return sum((1 - bit if (k >> n) & 1 else bit) << n for n, bit in enumerate(bits))

    has = (place <= places - 2, place >= 1)
    gets = (place >= 1, place <= places - 2)
    sends_far = ((place >= 1) & (place <= places - 2),) * 2
    gets_far = (place >= 2, place <= places - 3)

    def columns(owner, h):
        return pl.ds(pl.multiple_of((owner * heads + h) * HD, HD), HD)

    def rows_of(j, base=0):
        return pl.ds(pl.multiple_of(base + j * BLK, BLK), BLK)

    def await_bytes(ref, sem):
        pltpu.make_async_copy(ref, ref, sem).wait()

    def fetch_own(h, carry):
        for which, src in enumerate((k_ref, v_ref)):
            pltpu.make_async_copy(
                src.at[:, columns(me, h)], near.at[h, which, rows_of(me, here)], own_in.at[h]
            ).start()
        return carry

    barrier = pltpu.get_barrier_semaphore()
    for way in (0, 1):
        @pl.when(has[way])
        def _():
            pl.semaphore_signal(barrier, inc=1, device_id=beside(way), device_id_type=MESH)
    for k in PEERS:
        pl.semaphore_signal(barrier, inc=1, device_id=member(peer(k)), device_id_type=MESH)
    lax.fori_loop(0, heads, fetch_own, 0)
    neighbours = jnp.minimum(place, 1) + jnp.minimum(places - 1 - place, 1)
    pl.semaphore_wait(barrier, GROUP - 1 + neighbours)

    lands = (0, 2 * here)

    def ring_piece(h, j):
        for way in (0, 1):
            @pl.when(has[way])
            def _():
                pltpu.make_async_remote_copy(
                    src_ref=near.at[h, :, rows_of(j, here)], dst_ref=near.at[h, :, rows_of(j, lands[way])],
                    send_sem=ring_sent.at[way, h], recv_sem=ring_in.at[way, h],
                    device_id=beside(way), device_id_type=MESH,
                ).start()

    def share_kv(h, carry):
        for k in PEERS:
            j = peer(k)
            for which, src in enumerate((k_ref, v_ref)):
                pltpu.make_async_remote_copy(
                    src_ref=src.at[:, columns(j, h)], dst_ref=near.at[h, which, rows_of(me, here)],
                    send_sem=plane_sent.at[h], recv_sem=(beside_in if k == 2 else plane_in).at[h],
                    device_id=member(j), device_id_type=MESH,
                ).start()
        return carry

    def share_q(h, carry):
        for k in PEERS:
            j = peer(k)
            pltpu.make_async_remote_copy(
                src_ref=q_ref.at[:, columns(j, h)], dst_ref=qb.at[h, rows_of(me)],
                send_sem=q_sent.at[h], recv_sem=q_in.at[h],
                device_id=member(j), device_id_type=MESH,
            ).start()
        pltpu.make_async_copy(q_ref.at[:, columns(me, h)], qb.at[h, rows_of(me)], q_in.at[h]).start()
        return carry

    def ring_own(h, carry):
        await_bytes(near.at[h, :, pl.ds(here, BLK)], own_in.at[h])
        ring_piece(h, me)
        return carry

    lax.fori_loop(0, heads, ring_own, 0)
    lax.fori_loop(0, heads, share_kv, 0)
    lax.fori_loop(0, heads, share_q, 0)
    get_lists = pltpu.make_async_copy(list_ref, lists, list_in.at[0])
    get_lists.start()

    def ring_beside(h, carry):
        await_bytes(near.at[h, :, pl.ds(here, BLK)], beside_in.at[h])
        ring_piece(h, peer(2))
        return carry

    lax.fori_loop(0, heads, ring_beside, 0)

    for way in (0, 1):
        @pl.when(jnp.logical_not(gets[way]))
        def _():
            def clear(h, carry):
                for which in (0, 1):
                    near[h, which, pl.ds(lands[way], here), :] = jnp.zeros((here, HD), jnp.bfloat16)
                return carry

            lax.fori_loop(0, heads, clear, 0)

        @pl.when(jnp.logical_not(gets_far[way]))
        def _():
            def clear(h, carry):
                for which in (0, 1):
                    far[h, way, which] = jnp.zeros((FAR, HD), jnp.bfloat16)
                return carry

            lax.fori_loop(0, heads, clear, 0)

    get_lists.wait()

    def count(row, block):
        return sum((lists[j, row] == block).astype(jnp.int32) for j in range(lists.shape[0]))

    def tables(n, carry):
        a, d = n // STEPS, n % STEPS
        target = place * PLANE + a + d - REACH
        block = jnp.where(target < 0, -BLK, target * BPF)
        second = 0
        for b in range(BPF):
            row = (place * PLANE + a) * BPF + b
            one = count(row, block + 1)
            listed[a * BPF + b, d] = jnp.minimum(count(row, block) + one, 1)
            second = second + one
        sel[a, d] = jnp.minimum(second, 1)
        return carry

    lax.fori_loop(0, PLANE * STEPS, tables, 0)

    def fill(ref, r, slot, d):
        value = jnp.where(listed[r, d] == 1, 0.0, very_low)
        ref[r, :, pl.ds(pl.multiple_of(slot * BLK, BLK), BLK)] = jnp.full((1, BLK), value, jnp.float32)

    def biases(r, carry):
        a = r // BPF
        bias_near[r, :, pl.ds(0, FRAME)] = jnp.zeros((1, FRAME), jnp.float32)

        def one_near(i, carry):
            w = i + (i + REACH - PLANE - a) // REACH
            fill(bias_near, r, BPF + i, jnp.minimum(w + REACH - PLANE - a, STEPS - 1))
            return carry

        def one_far(i, carry):
            right = (i + a) // FAR_SLOTS
            fill(bias_far, r, i, i + right * (STEPS - FAR_SLOTS))
            return carry

        lax.fori_loop(0, 3 * PLANE - 1, one_near, 0)
        lax.fori_loop(0, FAR_SLOTS, one_far, 0)
        return carry

    lax.fori_loop(0, PLANE * BPF, biases, 0)

    def ring_rest(h, carry):
        await_bytes(near.at[h, :, pl.ds(here, here - BPF * BLK)], plane_in.at[h])
        for k in PEERS[1:]:
            ring_piece(h, peer(k))
        return carry

    lax.fori_loop(0, heads, ring_rest, 0)

    frames = ctx
    onward = (
        (jnp.minimum((place + 1) * PLANE, frames - 1), place * PLANE - PLANE + 1),
        (jnp.maximum((place - 1) * PLANE + PLANE - 1, 0), place * PLANE + PLANE + 2),
    )
    takes_second = [
        (count(f * BPF, g * BPF + 1) + count(f * BPF + 1, g * BPF + 1)) > 0 for f, g in onward
    ]

    def far_copy(way, n, h):
        b = 3 - n if way == 0 else 2 * PLANE + n
        whole = n < FAR_SLOTS - 1
        rows = FRAME if whole else BLK
        return pltpu.make_async_remote_copy(
            src_ref=near.at[h, :, pl.ds(b * FRAME, rows)] if whole else chosen.at[h, way],
            dst_ref=far.at[h, way, :, pl.ds(n * FRAME, rows)],
            send_sem=far_sent.at[way, n, h], recv_sem=far_in.at[way, n, h],
            device_id=beside(way), device_id_type=MESH,
        )

    def attend_near(h):
        def one_frame(a, carry):
            own = pl.multiple_of((PLANE + a) * FRAME, FRAME)
            ks[pl.ds(0, FRAME), :] = near[h, 0, pl.ds(own, FRAME), :]
            vs[pl.ds(0, FRAME), :] = near[h, 1, pl.ds(own, FRAME), :]

            def pick(i, carry):
                w = i + (i + REACH - PLANE - a) // REACH
                row = pl.multiple_of(w * FRAME, FRAME)
                second = sel[a, jnp.minimum(w + REACH - PLANE - a, STEPS - 1)] == 1
                to = pl.ds(pl.multiple_of(FRAME + i * BLK, BLK), BLK)
                for which, dst in ((0, ks), (1, vs)):
                    dst[to, :] = jnp.where(
                        second, near[h, which, pl.ds(row + BLK, BLK), :], near[h, which, pl.ds(row, BLK), :]
                    )
                return carry

            lax.fori_loop(0, 3 * PLANE - 1, pick, 0)
            rows = pl.ds(pl.multiple_of(a * FRAME, FRAME), FRAME)
            scores = lax.dot_general(
                qb[h, rows, :], ks[...], (((1,), (1,)), ((), ())), preferred_element_type=jnp.float32
            ).reshape(BPF, BLK, NEAR_KEYS)
            scores = scores * scale2 + bias_near[pl.ds(a * BPF, BPF)]
            top = jnp.max(scores, axis=2, keepdims=True)
            weights = jnp.exp2(scores - top)
            total = jnp.sum(weights, axis=2, keepdims=True)
            part[h, rows, :] = jnp.dot(
                weights.reshape(FRAME, NEAR_KEYS).astype(jnp.bfloat16), vs[...],
                preferred_element_type=jnp.float32,
            )
            high[h, rows, :] = jnp.broadcast_to(top, (BPF, BLK, HD)).reshape(FRAME, HD)
            low[h, rows, :] = jnp.broadcast_to(total, (BPF, BLK, HD)).reshape(FRAME, HD)
            return carry

        lax.fori_loop(0, PLANE, one_frame, 0)

    def attend_far(h, a):
        def pick(i, carry):
            right = (i + a) // FAR_SLOTS
            pair = (1 - right) * (FAR_SLOTS - 1 - a - i) + right * (i + a - FAR_SLOTS)
            whole = 1 - pair // (FAR_SLOTS - 1)
            row = pl.multiple_of(pair * FRAME, FRAME)
            row_b = pl.multiple_of(pair * FRAME + whole * BLK, BLK)
            second = sel[a, i + right * (STEPS - FAR_SLOTS)] == 1
            to = pl.ds(pl.multiple_of(i * BLK, BLK), BLK)
            for which, dst in ((0, ks), (1, vs)):
                dst[to, :] = jnp.where(
                    second, far[h, right, which, pl.ds(row_b, BLK), :], far[h, right, which, pl.ds(row, BLK), :]
                )
            return carry

        lax.fori_loop(0, FAR_SLOTS, pick, 0)
        keys = pl.ds(0, FAR_KEYS)
        for b in range(BPF):
            j = a * BPF + (b + 1 - u) % BPF
            rows = rows_of(j)
            scores = lax.dot_general(
                qb[h, rows, :], ks[keys, :], (((1,), (1,)), ((), ())), preferred_element_type=jnp.float32
            )
            scores = scores * scale2 + bias_far[j]
            before = high[h, rows, :]
            top = jnp.maximum(before, jnp.max(scores, axis=1, keepdims=True))
            weights = jnp.exp2(scores - jnp.concatenate([top] * FAR_SLOTS, axis=1))
            fade = jnp.exp2(before - top)
            total = fade * low[h, rows, :] + jnp.sum(weights, axis=1, keepdims=True)
            mixed = fade * part[h, rows, :] + jnp.dot(
                weights.astype(jnp.bfloat16), vs[keys, :], preferred_element_type=jnp.float32
            )
            ob[h, rows, :] = (mixed / total).astype(jnp.bfloat16)
            give_back(h, j)

    def give_back(h, j):
        @pl.when(j != me)
        def _():
            pltpu.make_async_remote_copy(
                src_ref=ob.at[h, rows_of(j)], dst_ref=out_ref.at[:, columns(me, h)],
                send_sem=out_sent.at[h], recv_sem=out_in.at[0],
                device_id=member(j), device_id_type=MESH,
            ).start()

        @pl.when(j == me)
        def _():
            pltpu.make_async_copy(ob.at[h, rows_of(j)], out_ref.at[:, columns(me, h)], out_in.at[0]).start()

    def first_phase(h, carry):
        for way in (0, 1):
            @pl.when(gets[way])
            def _():
                await_bytes(near.at[h, :, pl.ds(lands[way], here)], ring_in.at[way, h])

        for way in (0, 1):
            @pl.when(sends_far[way])
            def _():
                frame = 1 if way == 0 else 2 * PLANE + 2
                for which in (0, 1):
                    chosen[h, way, which] = jnp.where(
                        takes_second[way],
                        near[h, which, pl.ds(frame * FRAME + BLK, BLK), :],
                        near[h, which, pl.ds(frame * FRAME, BLK), :],
                    )
                for n in range(FAR_SLOTS):
                    far_copy(way, n, h).start()

        await_bytes(qb.at[h], q_in.at[h])
        attend_near(h)
        return carry

    lax.fori_loop(0, heads, first_phase, 0)

    both = gets_far[0] & gets_far[1]
    falling = jnp.where(gets_far[0], 1, 0)

    others = (GROUP - 1) * BLK

    def await_far_sent(h):
        for way in (0, 1):
            @pl.when(sends_far[way])
            def _():
                for n in range(FAR_SLOTS):
                    far_copy(way, n, h).wait_send()

    def await_out_sent(h):
        await_bytes(ob.at[h, pl.ds(0, others)], out_sent.at[h])

    def second_phase(h, carry):
        await_bytes(near.at[h, :, pl.ds(0, others)], plane_sent.at[h])
        await_bytes(qb.at[h, pl.ds(0, others)], q_sent.at[h])
        for way in (0, 1):
            @pl.when(has[way])
            def _():
                await_bytes(near.at[h, :, pl.ds(0, here)], ring_sent.at[way, h])

        @pl.when(h >= 1)
        def _():
            await_far_sent(h - 1)
            await_out_sent(h - 1)

        for way in (0, 1):
            @pl.when(both)
            def _():
                for n in range(FAR_SLOTS):
                    far_copy(way, n, h).wait_recv()

        for n in range(PLANE):
            if n >= 1:
                for way in (0, 1):
                    @pl.when(gets_far[way] & jnp.logical_not(both))
                    def _():
                        far_copy(way, n - 1, h).wait_recv()
            a = falling * (PLANE - 1 - n) + (1 - falling) * n
            attend_far(h, a)
        return carry

    lax.fori_loop(0, heads, second_phase, 0)

    await_far_sent(heads - 1)
    await_out_sent(heads - 1)
    await_bytes(out_ref, out_in.at[0])


def plane_attention(q_proj, k_proj, v_proj, kv_list):
    ctx = lax.axis_size("ctx")
    tokens, width = q_proj.shape
    heads = width // HD // GROUP
    here = PLANE * FRAME
    lists = kv_list.T
    any_space = pl.BlockSpec(memory_space=pl.ANY)
    dma = pltpu.SemaphoreType.DMA
    bf16, f32 = jnp.bfloat16, jnp.float32
    return pl.pallas_call(
        functools.partial(plane_kernel, ctx, heads),
        out_shape=jax.ShapeDtypeStruct((tokens, width), bf16),
        in_specs=[any_space] * 4,
        out_specs=any_space,
        scratch_shapes=[
            pltpu.SMEM(lists.shape, jnp.int32),
            pltpu.SMEM((PLANE, STEPS), jnp.int32),
            pltpu.SMEM((PLANE * BPF, STEPS), jnp.int32),
            pltpu.VMEM((PLANE * BPF, 1, NEAR_KEYS), f32),
            pltpu.VMEM((PLANE * BPF, 1, FAR_KEYS), f32),
            pltpu.VMEM((heads, 2, NEAR, HD), bf16),
            pltpu.VMEM((heads, 2, 2, FAR, HD), bf16),
            pltpu.VMEM((heads, 2, 2, BLK, HD), bf16),
            pltpu.VMEM((heads, here, HD), bf16),
            pltpu.VMEM((heads, here, HD), bf16),
            pltpu.VMEM((heads, here, HD), f32),
            pltpu.VMEM((heads, here, HD), f32),
            pltpu.VMEM((heads, here, HD), f32),
            pltpu.VMEM((NEAR_KEYS, HD), bf16),
            pltpu.VMEM((NEAR_KEYS, HD), bf16),
            dma((1,)), dma((heads,)), dma((heads,)), dma((heads,)), dma((heads,)), dma((2, heads)),
            dma((2, FAR_SLOTS, heads)), dma((1,)),
            dma((heads,)), dma((heads,)), dma((2, heads)), dma((2, FAR_SLOTS, heads)), dma((heads,)),
        ],
        compiler_params=pltpu.CompilerParams(
            collective_id=0, has_side_effects=True, vmem_limit_bytes=30 * 1024 * 1024
        ),
    )(*[pltpu.with_memory_space_constraint(x, pltpu.HBM) for x in (lists, q_proj, k_proj, v_proj)])


def on_device(q_proj, k_proj, v_proj, kv_list):
    rep, uly = lax.axis_size("rep"), lax.axis_size("uly")
    if rep == 1 and uly == BPF and q_proj.shape[0] == BLK and lax.axis_size("ctx") % PLANE == 0:
        return plane_attention(q_proj, k_proj, v_proj, kv_list)
    return ring_attention(q_proj, k_proj, v_proj, kv_list)


def solution(mesh):
    rows = P(("groups", "ctx", "rep", "uly"), None)
    return jax.shard_map(
        on_device,
        mesh=mesh,
        in_specs=(rows, rows, rows, P("groups", None)),
        out_specs=rows,
        check_vma=False,
    )
```

```python
import functools
import math

import jax
import jax.numpy as jnp
from jax import lax
from jax.experimental import pallas as pl
from jax.experimental.pallas import tpu as pltpu
from jax.sharding import PartitionSpec as P

HD = 128
BLK = 128
BPF = 2
FRAME = BLK * BPF
REACH = 7
GROUP = 8
SLOTS = 2 * REACH
KEYS = (SLOTS + BPF) * BLK

very_low = -1e30
scale2 = math.log2(math.e) / math.sqrt(HD)
MESH = pl.DeviceIdType.MESH


def ring_kernel(sizes, sel_ref, bias_ref, q_ref, k_ref, v_ref, out_ref, kv, qb, ob, ks, vs,
           first_in, kv_in, q_in, kv_sent, q_sent, ring_in, ring_sent, out_in, out_sent):
    ctx, rep, uly, tokens, heads = sizes
    inner = GROUP // (rep * uly)
    here = GROUP * tokens
    frames_here = here // FRAME
    places = ctx // inner
    hops = -(-REACH // frames_here)
    c = lax.axis_index("ctx")
    r = lax.axis_index("rep")
    u = lax.axis_index("uly")
    place = c // inner
    me = (c % inner) * (rep * uly) + r * uly + u

    def member(j):
        return {"ctx": place * inner + j // (rep * uly), "rep": (j // uly) % rep, "uly": j % uly}

    def beside(step):
        return {"ctx": c + step * inner}

    has_left, has_right = place >= 1, place <= places - 2

    barrier = pltpu.get_barrier_semaphore()
    for k in range(1, GROUP):
        pl.semaphore_signal(barrier, inc=1, device_id=member((me + k) % GROUP), device_id_type=MESH)

    @pl.when(has_left)
    def _():
        pl.semaphore_signal(barrier, inc=1, device_id=beside(-1), device_id_type=MESH)

    @pl.when(has_right)
    def _():
        pl.semaphore_signal(barrier, inc=1, device_id=beside(1), device_id_type=MESH)

    neighbours = jnp.minimum(place, 1) + jnp.minimum(places - 1 - place, 1)
    pl.semaphore_wait(barrier, GROUP - 1 + neighbours)

    def columns(owner, h):
        return pl.ds(pl.multiple_of((owner * heads + h) * HD, HD), HD)

    own_rows = pl.ds(pl.multiple_of(REACH * FRAME + me * tokens, tokens), tokens)
    q_rows = pl.ds(pl.multiple_of(me * tokens, tokens), tokens)

    def share_kv(h, arrived):
        for k in range(1, GROUP):
            j = (me + k) % GROUP
            for which, src in enumerate((k_ref, v_ref)):
                pltpu.make_async_remote_copy(
                    src_ref=src.at[:, columns(j, h)], dst_ref=kv.at[h, which, own_rows],
                    send_sem=kv_sent.at[h], recv_sem=arrived(k),
                    device_id=member(j), device_id_type=MESH,
                ).start()
        for which, src in enumerate((k_ref, v_ref)):
            pltpu.make_async_copy(
                src.at[:, columns(me, h)], kv.at[h, which, own_rows], arrived(0)
            ).start()

    def share_later(h, carry):
        share_kv(h, lambda k: kv_in.at[h])
        return carry

    def share_q(h, carry):
        for k in range(1, GROUP):
            j = (me + k) % GROUP
            pltpu.make_async_remote_copy(
                src_ref=q_ref.at[:, columns(j, h)], dst_ref=qb.at[h, q_rows],
                send_sem=q_sent.at[h], recv_sem=q_in.at[h],
                device_id=member(j), device_id_type=MESH,
            ).start()
        pltpu.make_async_copy(q_ref.at[:, columns(me, h)], qb.at[h, q_rows], q_in.at[h]).start()
        return carry

    share_kv(0, lambda k: first_in.at[k])
    lax.fori_loop(1, heads, share_later, 0)
    lax.fori_loop(0, heads, share_q, 0)

    def await_bytes(ref, sem):
        pltpu.make_async_copy(ref, ref, sem).wait()

    def ring_copy(way, s, h):
        if way == 0:
            first, last, shift = max(0, REACH - s * frames_here), REACH - (s - 1) * frames_here, frames_here
        else:
            first = REACH + s * frames_here
            last, shift = min(frames_here + SLOTS, first + frames_here), -frames_here
        rows = (last - first) * FRAME
        return pltpu.make_async_remote_copy(
            src_ref=kv.at[h, :, pl.ds((first + shift) * FRAME, rows)],
            dst_ref=kv.at[h, :, pl.ds(first * FRAME, rows)],
            send_sem=ring_sent.at[way, s - 1, h], recv_sem=ring_in.at[way, s - 1, h],
            device_id=beside(1 if way == 0 else -1), device_id_type=MESH,
        )

    def sends(way, s):
        if way == 0:
            return (place >= s - 1) & has_right
        return (place + s <= places) & has_left

    def receives(way, s):
        return place >= s if way == 0 else place + s <= places - 1

    def ring_start(s, h):
        for way in (0, 1):
            @pl.when(sends(way, s))
            def _():
                ring_copy(way, s, h).start()

    def ring_arrived(s, h):
        for way in (0, 1):
            @pl.when(receives(way, s))
            def _():
                ring_copy(way, s, h).wait_recv()

    def attend(h):
        def one_frame(f, carry):
            own = pl.multiple_of((REACH + f) * FRAME, FRAME)
            ks[pl.ds(0, FRAME), :] = kv[h, 0, pl.ds(own, FRAME), :]
            vs[pl.ds(0, FRAME), :] = kv[h, 1, pl.ds(own, FRAME), :]

            def pick(i, carry):
                far = place * frames_here + f + i - REACH + i // REACH
                slot = jnp.minimum(jnp.maximum(far, 0), ctx - 1) - place * frames_here + REACH
                row = pl.multiple_of(slot * FRAME, FRAME)
                second = sel_ref[f, i] == 1
                to = pl.ds(pl.multiple_of(FRAME + i * BLK, BLK), BLK)
                for which, dst in ((0, ks), (1, vs)):
                    dst[to, :] = jnp.where(
                        second,
                        kv[h, which, pl.ds(row + BLK, BLK), :],
                        kv[h, which, pl.ds(row, BLK), :],
                    )
                return carry

            lax.fori_loop(0, SLOTS, pick, 0)

            def one_block(b, carry):
                rows = pl.ds(pl.multiple_of(f * FRAME + b * BLK, BLK), BLK)
                scores = lax.dot_general(
                    qb[h, rows, :], ks[...], (((1,), (1,)), ((), ())),
                    preferred_element_type=jnp.float32,
                )
                scores = scores * scale2 + bias_ref[f * BPF + b]
                weights = jnp.exp2(scores - jnp.max(scores, axis=1, keepdims=True))
                total = jnp.sum(weights, axis=1, keepdims=True)
                mixed = jnp.dot(
                    weights.astype(jnp.bfloat16), vs[...], preferred_element_type=jnp.float32
                )
                ob[h, rows, :] = (mixed / total).astype(jnp.bfloat16)
                return carry

            lax.fori_loop(0, BPF, one_block, 0)
            return carry

        lax.fori_loop(0, frames_here, one_frame, 0)

    def give_back(h):
        for k in range(1, GROUP):
            j = (me + k) % GROUP
            pltpu.make_async_remote_copy(
                src_ref=ob.at[h, pl.ds(pl.multiple_of(j * tokens, tokens), tokens)],
                dst_ref=out_ref.at[:, columns(me, h)],
                send_sem=out_sent.at[h], recv_sem=out_in.at[0],
                device_id=member(j), device_id_type=MESH,
            ).start()
        pltpu.make_async_copy(ob.at[h, q_rows], out_ref.at[:, columns(me, h)], out_in.at[0]).start()

    def step(t, carry):
        @pl.when((t >= 1) & (t < heads))
        def _():
            await_bytes(kv.at[t, :, pl.ds(REACH * FRAME, here)], kv_in.at[t])
            ring_start(1, t)

        for s in range(1, hops):
            @pl.when((t >= s) & (t < heads + s))
            def _():
                ring_arrived(s, t - s)
                ring_start(s + 1, t - s)

        @pl.when(t >= hops)
        def _():
            ring_arrived(hops, t - hops)
            await_bytes(qb.at[t - hops], q_in.at[t - hops])
            attend(t - hops)
            give_back(t - hops)

        return carry

    for k in range(GROUP):
        row = REACH * FRAME + (me + GROUP - k) % GROUP * tokens
        piece = kv.at[0, :, pl.ds(pl.multiple_of(row, tokens), tokens)]
        await_bytes(piece, first_in.at[k])
        for way in (0, 1):
            @pl.when(sends(way, 1))
            def _():
                to = row - here if way == 0 else row + here
                pltpu.make_async_remote_copy(
                    src_ref=piece, dst_ref=kv.at[0, :, pl.ds(pl.multiple_of(to, tokens), tokens)],
                    send_sem=ring_sent.at[way, 0, 0], recv_sem=ring_in.at[way, 0, 0],
                    device_id=beside(1 if way == 0 else -1), device_id_type=MESH,
                ).start()

    lax.fori_loop(0, heads + hops, step, 0)

    def finish(h, carry):
        others = (GROUP - 1) * tokens
        await_bytes(kv.at[h, :, pl.ds(0, others)], kv_sent.at[h])
        await_bytes(qb.at[h, pl.ds(0, others)], q_sent.at[h])
        await_bytes(ob.at[h, pl.ds(0, others)], out_sent.at[h])
        for s in range(1, hops + 1):
            for way in (0, 1):
                @pl.when(sends(way, s))
                def _():
                    ring_copy(way, s, h).wait_send()
        return carry

    lax.fori_loop(0, heads, finish, 0)
    await_bytes(out_ref, out_in.at[0])


def tables(kv_list, place, frames_here, frames):
    lists = lax.dynamic_slice_in_dim(kv_list, place * frames_here * BPF, frames_here * BPF, 0)
    lists = lists.reshape(frames_here, BPF, 1, -1)
    steps = jnp.array([d for d in range(-REACH, REACH + 1) if d != 0], jnp.int32)
    far = place * frames_here + jnp.arange(frames_here, dtype=jnp.int32)[:, None] + steps[None, :]
    inside = (far >= 0) & (far < frames)
    has = [jnp.any(lists == (far * BPF + b)[:, None, :, None], axis=3) for b in range(BPF)]
    listed = (has[0] | has[1]) & inside[:, None, :]
    sel = jnp.any(has[1], axis=1).astype(jnp.int32)
    bias = jnp.where(listed, 0.0, very_low).astype(jnp.float32)
    bias = jnp.concatenate([jnp.zeros((frames_here, BPF, BPF), jnp.float32), bias], axis=2)
    bias = jnp.repeat(bias.reshape(frames_here * BPF, BPF + SLOTS), BLK, axis=1)
    return sel, bias.reshape(frames_here * BPF, 1, KEYS)


def ring_attention(q_proj, k_proj, v_proj, kv_list):
    ctx, rep, uly = lax.axis_size("ctx"), lax.axis_size("rep"), lax.axis_size("uly")
    tokens, width = q_proj.shape
    heads = width // HD // GROUP
    inner = GROUP // (rep * uly)
    here = GROUP * tokens
    frames_here = here // FRAME
    hops = -(-REACH // frames_here)
    sel, bias = tables(kv_list, lax.axis_index("ctx") // inner, frames_here, ctx)
    window = (frames_here + SLOTS) * FRAME
    any_space = pl.BlockSpec(memory_space=pl.ANY)
    dma = pltpu.SemaphoreType.DMA
    return pl.pallas_call(
        functools.partial(ring_kernel, (ctx, rep, uly, tokens, heads)),
        out_shape=jax.ShapeDtypeStruct((tokens, width), jnp.bfloat16),
        in_specs=[
            pl.BlockSpec(memory_space=pltpu.SMEM),
            pl.BlockSpec(memory_space=pltpu.VMEM),
            any_space, any_space, any_space,
        ],
        out_specs=any_space,
        scratch_shapes=[
            pltpu.VMEM((heads, 2, window, HD), jnp.bfloat16),
            pltpu.VMEM((heads, here, HD), jnp.bfloat16),
            pltpu.VMEM((heads, here, HD), jnp.bfloat16),
            pltpu.VMEM((KEYS, HD), jnp.bfloat16),
            pltpu.VMEM((KEYS, HD), jnp.bfloat16),
            dma((GROUP,)), dma((heads,)), dma((heads,)), dma((heads,)), dma((heads,)),
            dma((2, hops, heads)), dma((2, hops, heads)), dma((1,)), dma((heads,)),
        ],
        compiler_params=pltpu.CompilerParams(
            collective_id=0, has_side_effects=True, vmem_limit_bytes=56 * 1024 * 1024
        ),
    )(sel, bias, q_proj, k_proj, v_proj)


PLANE = 4
NEAR = 3 * PLANE * FRAME
NEAR_KEYS = NEAR // 2 + BLK
FAR_SLOTS = 3
FAR = (2 * FAR_SLOTS - 1) * BLK
FAR_KEYS = FAR_SLOTS * BLK
STEPS = 2 * REACH + 1
PEERS = (2, 1, 3, 4, 6, 5, 7)


def plane_kernel(ctx, heads, list_ref, q_ref, k_ref, v_ref, out_ref,
                 lists, sel, listed, bias_near, bias_far, near, far, chosen, qb, ob, part, high, low, ks, vs,
                 list_in, own_in, beside_in, plane_in, q_in, ring_in, far_in, out_in,
                 plane_sent, q_sent, ring_sent, far_sent, out_sent):
    here = PLANE * FRAME
    places = ctx // PLANE
    c = lax.axis_index("ctx")
    u = lax.axis_index("uly")
    place = c // PLANE
    me = (c % PLANE) * BPF + u

    def member(j):
        return {"ctx": place * PLANE + j // BPF, "uly": j % BPF}

    def beside(way):
        return {"ctx": c + (PLANE if way == 0 else -PLANE)}

    def peer(k):
        bits = (me % 2, (me // 2) % 2, me // 4)
        return sum((1 - bit if (k >> n) & 1 else bit) << n for n, bit in enumerate(bits))

    has = (place <= places - 2, place >= 1)
    gets = (place >= 1, place <= places - 2)
    sends_far = ((place >= 1) & (place <= places - 2),) * 2
    gets_far = (place >= 2, place <= places - 3)

    def columns(owner, h):
        return pl.ds(pl.multiple_of((owner * heads + h) * HD, HD), HD)

    def rows_of(j, base=0):
        return pl.ds(pl.multiple_of(base + j * BLK, BLK), BLK)

    def await_bytes(ref, sem):
        pltpu.make_async_copy(ref, ref, sem).wait()

    def fetch_own(h, carry):
        for which, src in enumerate((k_ref, v_ref)):
            pltpu.make_async_copy(
                src.at[:, columns(me, h)], near.at[h, which, rows_of(me, here)], own_in.at[h]
            ).start()
        return carry

    barrier = pltpu.get_barrier_semaphore()
    for way in (0, 1):
        @pl.when(has[way])
        def _():
            pl.semaphore_signal(barrier, inc=1, device_id=beside(way), device_id_type=MESH)
    for k in PEERS:
        pl.semaphore_signal(barrier, inc=1, device_id=member(peer(k)), device_id_type=MESH)
    lax.fori_loop(0, heads, fetch_own, 0)
    neighbours = jnp.minimum(place, 1) + jnp.minimum(places - 1 - place, 1)
    pl.semaphore_wait(barrier, GROUP - 1 + neighbours)

    lands = (0, 2 * here)

    def ring_piece(h, j):
        for way in (1, 0):
            @pl.when(has[way])
            def _():
                pltpu.make_async_remote_copy(
                    src_ref=near.at[h, :, rows_of(j, here)], dst_ref=near.at[h, :, rows_of(j, lands[way])],
                    send_sem=ring_sent.at[way, h], recv_sem=ring_in.at[way, h],
                    device_id=beside(way), device_id_type=MESH,
                ).start()

    def share_kv(h, carry):
        for k in PEERS:
            j = peer(k)
            for which, src in enumerate((k_ref, v_ref)):
                pltpu.make_async_remote_copy(
                    src_ref=src.at[:, columns(j, h)], dst_ref=near.at[h, which, rows_of(me, here)],
                    send_sem=plane_sent.at[h], recv_sem=(beside_in if k == 2 else plane_in).at[h],
                    device_id=member(j), device_id_type=MESH,
                ).start()
        return carry

    def share_q(h, carry):
        for k in PEERS:
            j = peer(k)
            pltpu.make_async_remote_copy(
                src_ref=q_ref.at[:, columns(j, h)], dst_ref=qb.at[h, rows_of(me)],
                send_sem=q_sent.at[h], recv_sem=q_in.at[h],
                device_id=member(j), device_id_type=MESH,
            ).start()
        pltpu.make_async_copy(q_ref.at[:, columns(me, h)], qb.at[h, rows_of(me)], q_in.at[h]).start()
        return carry

    def ring_own(h, carry):
        await_bytes(near.at[h, :, pl.ds(here, BLK)], own_in.at[h])
        ring_piece(h, me)
        return carry

    lax.fori_loop(0, heads, ring_own, 0)
    lax.fori_loop(0, heads, share_kv, 0)
    lax.fori_loop(0, heads, share_q, 0)
    get_lists = pltpu.make_async_copy(list_ref, lists, list_in.at[0])
    get_lists.start()

    def ring_beside(h, carry):
        await_bytes(near.at[h, :, pl.ds(here, BLK)], beside_in.at[h])
        ring_piece(h, peer(2))
        return carry

    lax.fori_loop(0, heads, ring_beside, 0)

    for way in (0, 1):
        @pl.when(jnp.logical_not(gets[way]))
        def _():
            def clear(h, carry):
                for which in (0, 1):
                    near[h, which, pl.ds(lands[way], here), :] = jnp.zeros((here, HD), jnp.bfloat16)
                return carry

            lax.fori_loop(0, heads, clear, 0)

        @pl.when(jnp.logical_not(gets_far[way]))
        def _():
            def clear(h, carry):
                for which in (0, 1):
                    far[h, way, which] = jnp.zeros((FAR, HD), jnp.bfloat16)
                return carry

            lax.fori_loop(0, heads, clear, 0)

    get_lists.wait()

    def count(row, block):
        return sum((lists[j, row] == block).astype(jnp.int32) for j in range(lists.shape[0]))

    def tables(n, carry):
        a, d = n // STEPS, n % STEPS
        target = place * PLANE + a + d - REACH
        block = jnp.where(target < 0, -BLK, target * BPF)
        second = 0
        for b in range(BPF):
            row = (place * PLANE + a) * BPF + b
            one = count(row, block + 1)
            listed[a * BPF + b, d] = jnp.minimum(count(row, block) + one, 1)
            second = second + one
        sel[a, d] = jnp.minimum(second, 1)
        return carry

    lax.fori_loop(0, PLANE * STEPS, tables, 0)

    def fill(ref, r, slot, d):
        value = jnp.where(listed[r, d] == 1, 0.0, very_low)
        ref[r, :, pl.ds(pl.multiple_of(slot * BLK, BLK), BLK)] = jnp.full((1, BLK), value, jnp.float32)

    def biases(r, carry):
        a = r // BPF
        bias_near[r, :, pl.ds(0, FRAME)] = jnp.zeros((1, FRAME), jnp.float32)

        def one_near(i, carry):
            w = i + (i + REACH - PLANE - a) // REACH
            fill(bias_near, r, BPF + i, jnp.minimum(w + REACH - PLANE - a, STEPS - 1))
            return carry

        def one_far(i, carry):
            right = (i + a) // FAR_SLOTS
            fill(bias_far, r, i, i + right * (STEPS - FAR_SLOTS))
            return carry

        lax.fori_loop(0, 3 * PLANE - 1, one_near, 0)
        lax.fori_loop(0, FAR_SLOTS, one_far, 0)
        return carry

    lax.fori_loop(0, PLANE * BPF, biases, 0)

    def ring_rest(h, carry):
        await_bytes(near.at[h, :, pl.ds(here, here - BPF * BLK)], plane_in.at[h])
        for k in PEERS[1:]:
            ring_piece(h, peer(k))
        return carry

    lax.fori_loop(0, heads, ring_rest, 0)

    frames = ctx
    onward = (
        (jnp.minimum((place + 1) * PLANE, frames - 1), place * PLANE - PLANE + 1),
        (jnp.maximum((place - 1) * PLANE + PLANE - 1, 0), place * PLANE + PLANE + 2),
    )
    takes_second = [
        (count(f * BPF, g * BPF + 1) + count(f * BPF + 1, g * BPF + 1)) > 0 for f, g in onward
    ]

    def far_copy(way, n, h):
        b = 3 - n if way == 0 else 2 * PLANE + n
        whole = n < FAR_SLOTS - 1
        rows = FRAME if whole else BLK
        return pltpu.make_async_remote_copy(
            src_ref=near.at[h, :, pl.ds(b * FRAME, rows)] if whole else chosen.at[h, way],
            dst_ref=far.at[h, way, :, pl.ds(n * FRAME, rows)],
            send_sem=far_sent.at[way, n, h], recv_sem=far_in.at[way, n, h],
            device_id=beside(way), device_id_type=MESH,
        )

    def attend_near(h):
        def one_frame(a, carry):
            own = pl.multiple_of((PLANE + a) * FRAME, FRAME)
            ks[pl.ds(0, FRAME), :] = near[h, 0, pl.ds(own, FRAME), :]
            vs[pl.ds(0, FRAME), :] = near[h, 1, pl.ds(own, FRAME), :]

            def pick(i, carry):
                w = i + (i + REACH - PLANE - a) // REACH
                row = pl.multiple_of(w * FRAME, FRAME)
                second = sel[a, jnp.minimum(w + REACH - PLANE - a, STEPS - 1)] == 1
                to = pl.ds(pl.multiple_of(FRAME + i * BLK, BLK), BLK)
                for which, dst in ((0, ks), (1, vs)):
                    dst[to, :] = jnp.where(
                        second, near[h, which, pl.ds(row + BLK, BLK), :], near[h, which, pl.ds(row, BLK), :]
                    )
                return carry

            lax.fori_loop(0, 3 * PLANE - 1, pick, 0)
            rows = pl.ds(pl.multiple_of(a * FRAME, FRAME), FRAME)
            scores = lax.dot_general(
                qb[h, rows, :], ks[...], (((1,), (1,)), ((), ())), preferred_element_type=jnp.float32
            ).reshape(BPF, BLK, NEAR_KEYS)
            scores = scores * scale2 + bias_near[pl.ds(a * BPF, BPF)]
            top = jnp.max(scores, axis=2, keepdims=True)
            weights = jnp.exp2(scores - top)
            total = jnp.sum(weights, axis=2, keepdims=True)
            part[h, rows, :] = jnp.dot(
                weights.reshape(FRAME, NEAR_KEYS).astype(jnp.bfloat16), vs[...],
                preferred_element_type=jnp.float32,
            )
            high[h, rows, :] = jnp.broadcast_to(top, (BPF, BLK, HD)).reshape(FRAME, HD)
            low[h, rows, :] = jnp.broadcast_to(total, (BPF, BLK, HD)).reshape(FRAME, HD)
            return carry

        lax.fori_loop(0, PLANE, one_frame, 0)

    def attend_far(h, a):
        def pick(i, carry):
            right = (i + a) // FAR_SLOTS
            pair = (1 - right) * (FAR_SLOTS - 1 - a - i) + right * (i + a - FAR_SLOTS)
            whole = 1 - pair // (FAR_SLOTS - 1)
            row = pl.multiple_of(pair * FRAME, FRAME)
            row_b = pl.multiple_of(pair * FRAME + whole * BLK, BLK)
            second = sel[a, i + right * (STEPS - FAR_SLOTS)] == 1
            to = pl.ds(pl.multiple_of(i * BLK, BLK), BLK)
            for which, dst in ((0, ks), (1, vs)):
                dst[to, :] = jnp.where(
                    second, far[h, right, which, pl.ds(row_b, BLK), :], far[h, right, which, pl.ds(row, BLK), :]
                )
            return carry

        lax.fori_loop(0, FAR_SLOTS, pick, 0)
        rows = pl.ds(pl.multiple_of(a * FRAME, FRAME), FRAME)
        keys = pl.ds(0, FAR_KEYS)
        scores = lax.dot_general(
            qb[h, rows, :], ks[keys, :], (((1,), (1,)), ((), ())), preferred_element_type=jnp.float32
        ).reshape(BPF, BLK, FAR_KEYS)
        scores = (scores * scale2 + bias_far[pl.ds(a * BPF, BPF)]).reshape(FRAME, FAR_KEYS)
        before = high[h, rows, :]
        top = jnp.maximum(before, jnp.max(scores, axis=1, keepdims=True))
        weights = jnp.exp2(scores - jnp.concatenate([top] * FAR_SLOTS, axis=1))
        fade = jnp.exp2(before - top)
        total = fade * low[h, rows, :] + jnp.sum(weights, axis=1, keepdims=True)
        mixed = fade * part[h, rows, :] + jnp.dot(
            weights.astype(jnp.bfloat16), vs[keys, :], preferred_element_type=jnp.float32
        )
        ob[h, rows, :] = (mixed / total).astype(jnp.bfloat16)

    def give_back(h, a):
        for b in range(BPF):
            j = a * BPF + b

            @pl.when(j != me)
            def _():
                pltpu.make_async_remote_copy(
                    src_ref=ob.at[h, rows_of(j)], dst_ref=out_ref.at[:, columns(me, h)],
                    send_sem=out_sent.at[h], recv_sem=out_in.at[0],
                    device_id=member(j), device_id_type=MESH,
                ).start()

            @pl.when(j == me)
            def _():
                pltpu.make_async_copy(ob.at[h, rows_of(j)], out_ref.at[:, columns(me, h)], out_in.at[0]).start()

    def first_phase(h, carry):
        for way in (0, 1):
            @pl.when(gets[way])
            def _():
                await_bytes(near.at[h, :, pl.ds(lands[way], here)], ring_in.at[way, h])

        for way in (1, 0):
            @pl.when(sends_far[way])
            def _():
                frame = 1 if way == 0 else 2 * PLANE + 2
                for which in (0, 1):
                    chosen[h, way, which] = jnp.where(
                        takes_second[way],
                        near[h, which, pl.ds(frame * FRAME + BLK, BLK), :],
                        near[h, which, pl.ds(frame * FRAME, BLK), :],
                    )
                for n in range(FAR_SLOTS):
                    far_copy(way, n, h).start()

        await_bytes(qb.at[h], q_in.at[h])
        attend_near(h)
        return carry

    lax.fori_loop(0, heads, first_phase, 0)

    both = gets_far[0] & gets_far[1]
    falling = jnp.where(gets_far[0], 1, 0)

    others = (GROUP - 1) * BLK

    def await_far_sent(h):
        for way in (0, 1):
            @pl.when(sends_far[way])
            def _():
                for n in range(FAR_SLOTS):
                    far_copy(way, n, h).wait_send()

    def await_out_sent(h):
        await_bytes(ob.at[h, pl.ds(0, others)], out_sent.at[h])

    def second_phase(h, carry):
        await_bytes(near.at[h, :, pl.ds(0, others)], plane_sent.at[h])
        await_bytes(qb.at[h, pl.ds(0, others)], q_sent.at[h])
        for way in (0, 1):
            @pl.when(has[way])
            def _():
                await_bytes(near.at[h, :, pl.ds(0, here)], ring_sent.at[way, h])

        @pl.when(h >= 1)
        def _():
            await_far_sent(h - 1)
            await_out_sent(h - 1)

        for way in (0, 1):
            @pl.when(both)
            def _():
                for n in range(FAR_SLOTS):
                    far_copy(way, n, h).wait_recv()

        for n in range(PLANE):
            if n >= 1:
                for way in (0, 1):
                    @pl.when(gets_far[way] & jnp.logical_not(both))
                    def _():
                        far_copy(way, n - 1, h).wait_recv()
            a = falling * (PLANE - 1 - n) + (1 - falling) * n
            attend_far(h, a)
            give_back(h, a)
        return carry

    lax.fori_loop(0, heads, second_phase, 0)

    await_far_sent(heads - 1)
    await_out_sent(heads - 1)
    await_bytes(out_ref, out_in.at[0])


def plane_attention(q_proj, k_proj, v_proj, kv_list):
    ctx = lax.axis_size("ctx")
    tokens, width = q_proj.shape
    heads = width // HD // GROUP
    here = PLANE * FRAME
    lists = kv_list.T
    any_space = pl.BlockSpec(memory_space=pl.ANY)
    dma = pltpu.SemaphoreType.DMA
    bf16, f32 = jnp.bfloat16, jnp.float32
    return pl.pallas_call(
        functools.partial(plane_kernel, ctx, heads),
        out_shape=jax.ShapeDtypeStruct((tokens, width), bf16),
        in_specs=[any_space] * 4,
        out_specs=any_space,
        scratch_shapes=[
            pltpu.SMEM(lists.shape, jnp.int32),
            pltpu.SMEM((PLANE, STEPS), jnp.int32),
            pltpu.SMEM((PLANE * BPF, STEPS), jnp.int32),
            pltpu.VMEM((PLANE * BPF, 1, NEAR_KEYS), f32),
            pltpu.VMEM((PLANE * BPF, 1, FAR_KEYS), f32),
            pltpu.VMEM((heads, 2, NEAR, HD), bf16),
            pltpu.VMEM((heads, 2, 2, FAR, HD), bf16),
            pltpu.VMEM((heads, 2, 2, BLK, HD), bf16),
            pltpu.VMEM((heads, here, HD), bf16),
            pltpu.VMEM((heads, here, HD), bf16),
            pltpu.VMEM((heads, here, HD), f32),
            pltpu.VMEM((heads, here, HD), f32),
            pltpu.VMEM((heads, here, HD), f32),
            pltpu.VMEM((NEAR_KEYS, HD), bf16),
            pltpu.VMEM((NEAR_KEYS, HD), bf16),
            dma((1,)), dma((heads,)), dma((heads,)), dma((heads,)), dma((heads,)), dma((2, heads)),
            dma((2, FAR_SLOTS, heads)), dma((1,)),
            dma((heads,)), dma((heads,)), dma((2, heads)), dma((2, FAR_SLOTS, heads)), dma((heads,)),
        ],
        compiler_params=pltpu.CompilerParams(
            collective_id=0, has_side_effects=True, vmem_limit_bytes=30 * 1024 * 1024
        ),
    )(*[pltpu.with_memory_space_constraint(x, pltpu.HBM) for x in (lists, q_proj, k_proj, v_proj)])


def on_device(q_proj, k_proj, v_proj, kv_list):
    rep, uly = lax.axis_size("rep"), lax.axis_size("uly")
    if rep == 1 and uly == BPF and q_proj.shape[0] == BLK and lax.axis_size("ctx") % PLANE == 0:
        return plane_attention(q_proj, k_proj, v_proj, kv_list)
    return ring_attention(q_proj, k_proj, v_proj, kv_list)


def solution(mesh):
    rows = P(("groups", "ctx", "rep", "uly"), None)
    return jax.shard_map(
        on_device,
        mesh=mesh,
        in_specs=(rows, rows, rows, P("groups", None)),
        out_specs=rows,
        check_vma=False,
    )
```

```python
import functools
import math

import jax
import jax.numpy as jnp
from jax import lax
from jax.experimental import pallas as pl
from jax.experimental.pallas import tpu as pltpu
from jax.sharding import PartitionSpec as P

HD = 128
BLK = 128
BPF = 2
FRAME = BLK * BPF
REACH = 7
GROUP = 8
SLOTS = 2 * REACH
KEYS = (SLOTS + BPF) * BLK

very_low = -1e30
scale2 = math.log2(math.e) / math.sqrt(HD)
MESH = pl.DeviceIdType.MESH


def ring_kernel(sizes, sel_ref, bias_ref, q_ref, k_ref, v_ref, out_ref, kv, qb, ob, ks, vs,
           first_in, kv_in, q_in, kv_sent, q_sent, ring_in, ring_sent, out_in, out_sent):
    ctx, rep, uly, tokens, heads = sizes
    inner = GROUP // (rep * uly)
    here = GROUP * tokens
    frames_here = here // FRAME
    places = ctx // inner
    hops = -(-REACH // frames_here)
    c = lax.axis_index("ctx")
    r = lax.axis_index("rep")
    u = lax.axis_index("uly")
    place = c // inner
    me = (c % inner) * (rep * uly) + r * uly + u

    def member(j):
        return {"ctx": place * inner + j // (rep * uly), "rep": (j // uly) % rep, "uly": j % uly}

    def beside(step):
        return {"ctx": c + step * inner}

    has_left, has_right = place >= 1, place <= places - 2

    barrier = pltpu.get_barrier_semaphore()
    for k in range(1, GROUP):
        pl.semaphore_signal(barrier, inc=1, device_id=member((me + k) % GROUP), device_id_type=MESH)

    @pl.when(has_left)
    def _():
        pl.semaphore_signal(barrier, inc=1, device_id=beside(-1), device_id_type=MESH)

    @pl.when(has_right)
    def _():
        pl.semaphore_signal(barrier, inc=1, device_id=beside(1), device_id_type=MESH)

    neighbours = jnp.minimum(place, 1) + jnp.minimum(places - 1 - place, 1)
    pl.semaphore_wait(barrier, GROUP - 1 + neighbours)

    def columns(owner, h):
        return pl.ds(pl.multiple_of((owner * heads + h) * HD, HD), HD)

    own_rows = pl.ds(pl.multiple_of(REACH * FRAME + me * tokens, tokens), tokens)
    q_rows = pl.ds(pl.multiple_of(me * tokens, tokens), tokens)

    def share_kv(h, arrived):
        for k in range(1, GROUP):
            j = (me + k) % GROUP
            for which, src in enumerate((k_ref, v_ref)):
                pltpu.make_async_remote_copy(
                    src_ref=src.at[:, columns(j, h)], dst_ref=kv.at[h, which, own_rows],
                    send_sem=kv_sent.at[h], recv_sem=arrived(k),
                    device_id=member(j), device_id_type=MESH,
                ).start()
        for which, src in enumerate((k_ref, v_ref)):
            pltpu.make_async_copy(
                src.at[:, columns(me, h)], kv.at[h, which, own_rows], arrived(0)
            ).start()

    def share_later(h, carry):
        share_kv(h, lambda k: kv_in.at[h])
        return carry

    def share_q(h, carry):
        for k in range(1, GROUP):
            j = (me + k) % GROUP
            pltpu.make_async_remote_copy(
                src_ref=q_ref.at[:, columns(j, h)], dst_ref=qb.at[h, q_rows],
                send_sem=q_sent.at[h], recv_sem=q_in.at[h],
                device_id=member(j), device_id_type=MESH,
            ).start()
        pltpu.make_async_copy(q_ref.at[:, columns(me, h)], qb.at[h, q_rows], q_in.at[h]).start()
        return carry

    share_kv(0, lambda k: first_in.at[k])
    lax.fori_loop(1, heads, share_later, 0)
    lax.fori_loop(0, heads, share_q, 0)

    def await_bytes(ref, sem):
        pltpu.make_async_copy(ref, ref, sem).wait()

    def ring_copy(way, s, h):
        if way == 0:
            first, last, shift = max(0, REACH - s * frames_here), REACH - (s - 1) * frames_here, frames_here
        else:
            first = REACH + s * frames_here
            last, shift = min(frames_here + SLOTS, first + frames_here), -frames_here
        rows = (last - first) * FRAME
        return pltpu.make_async_remote_copy(
            src_ref=kv.at[h, :, pl.ds((first + shift) * FRAME, rows)],
            dst_ref=kv.at[h, :, pl.ds(first * FRAME, rows)],
            send_sem=ring_sent.at[way, s - 1, h], recv_sem=ring_in.at[way, s - 1, h],
            device_id=beside(1 if way == 0 else -1), device_id_type=MESH,
        )

    def sends(way, s):
        if way == 0:
            return (place >= s - 1) & has_right
        return (place + s <= places) & has_left

    def receives(way, s):
        return place >= s if way == 0 else place + s <= places - 1

    def ring_start(s, h):
        for way in (0, 1):
            @pl.when(sends(way, s))
            def _():
                ring_copy(way, s, h).start()

    def ring_arrived(s, h):
        for way in (0, 1):
            @pl.when(receives(way, s))
            def _():
                ring_copy(way, s, h).wait_recv()

    def attend(h):
        def one_frame(f, carry):
            own = pl.multiple_of((REACH + f) * FRAME, FRAME)
            ks[pl.ds(0, FRAME), :] = kv[h, 0, pl.ds(own, FRAME), :]
            vs[pl.ds(0, FRAME), :] = kv[h, 1, pl.ds(own, FRAME), :]

            def pick(i, carry):
                far = place * frames_here + f + i - REACH + i // REACH
                slot = jnp.minimum(jnp.maximum(far, 0), ctx - 1) - place * frames_here + REACH
                row = pl.multiple_of(slot * FRAME, FRAME)
                second = sel_ref[f, i] == 1
                to = pl.ds(pl.multiple_of(FRAME + i * BLK, BLK), BLK)
                for which, dst in ((0, ks), (1, vs)):
                    dst[to, :] = jnp.where(
                        second,
                        kv[h, which, pl.ds(row + BLK, BLK), :],
                        kv[h, which, pl.ds(row, BLK), :],
                    )
                return carry

            lax.fori_loop(0, SLOTS, pick, 0)

            def one_block(b, carry):
                rows = pl.ds(pl.multiple_of(f * FRAME + b * BLK, BLK), BLK)
                scores = lax.dot_general(
                    qb[h, rows, :], ks[...], (((1,), (1,)), ((), ())),
                    preferred_element_type=jnp.float32,
                )
                scores = scores * scale2 + bias_ref[f * BPF + b]
                weights = jnp.exp2(scores - jnp.max(scores, axis=1, keepdims=True))
                total = jnp.sum(weights, axis=1, keepdims=True)
                mixed = jnp.dot(
                    weights.astype(jnp.bfloat16), vs[...], preferred_element_type=jnp.float32
                )
                ob[h, rows, :] = (mixed / total).astype(jnp.bfloat16)
                return carry

            lax.fori_loop(0, BPF, one_block, 0)
            return carry

        lax.fori_loop(0, frames_here, one_frame, 0)

    def give_back(h):
        for k in range(1, GROUP):
            j = (me + k) % GROUP
            pltpu.make_async_remote_copy(
                src_ref=ob.at[h, pl.ds(pl.multiple_of(j * tokens, tokens), tokens)],
                dst_ref=out_ref.at[:, columns(me, h)],
                send_sem=out_sent.at[h], recv_sem=out_in.at[0],
                device_id=member(j), device_id_type=MESH,
            ).start()
        pltpu.make_async_copy(ob.at[h, q_rows], out_ref.at[:, columns(me, h)], out_in.at[0]).start()

    def step(t, carry):
        @pl.when((t >= 1) & (t < heads))
        def _():
            await_bytes(kv.at[t, :, pl.ds(REACH * FRAME, here)], kv_in.at[t])
            ring_start(1, t)

        for s in range(1, hops):
            @pl.when((t >= s) & (t < heads + s))
            def _():
                ring_arrived(s, t - s)
                ring_start(s + 1, t - s)

        @pl.when(t >= hops)
        def _():
            ring_arrived(hops, t - hops)
            await_bytes(qb.at[t - hops], q_in.at[t - hops])
            attend(t - hops)
            give_back(t - hops)

        return carry

    for k in range(GROUP):
        row = REACH * FRAME + (me + GROUP - k) % GROUP * tokens
        piece = kv.at[0, :, pl.ds(pl.multiple_of(row, tokens), tokens)]
        await_bytes(piece, first_in.at[k])
        for way in (0, 1):
            @pl.when(sends(way, 1))
            def _():
                to = row - here if way == 0 else row + here
                pltpu.make_async_remote_copy(
                    src_ref=piece, dst_ref=kv.at[0, :, pl.ds(pl.multiple_of(to, tokens), tokens)],
                    send_sem=ring_sent.at[way, 0, 0], recv_sem=ring_in.at[way, 0, 0],
                    device_id=beside(1 if way == 0 else -1), device_id_type=MESH,
                ).start()

    lax.fori_loop(0, heads + hops, step, 0)

    def finish(h, carry):
        others = (GROUP - 1) * tokens
        await_bytes(kv.at[h, :, pl.ds(0, others)], kv_sent.at[h])
        await_bytes(qb.at[h, pl.ds(0, others)], q_sent.at[h])
        await_bytes(ob.at[h, pl.ds(0, others)], out_sent.at[h])
        for s in range(1, hops + 1):
            for way in (0, 1):
                @pl.when(sends(way, s))
                def _():
                    ring_copy(way, s, h).wait_send()
        return carry

    lax.fori_loop(0, heads, finish, 0)
    await_bytes(out_ref, out_in.at[0])


def tables(kv_list, place, frames_here, frames):
    lists = lax.dynamic_slice_in_dim(kv_list, place * frames_here * BPF, frames_here * BPF, 0)
    lists = lists.reshape(frames_here, BPF, 1, -1)
    steps = jnp.array([d for d in range(-REACH, REACH + 1) if d != 0], jnp.int32)
    far = place * frames_here + jnp.arange(frames_here, dtype=jnp.int32)[:, None] + steps[None, :]
    inside = (far >= 0) & (far < frames)
    has = [jnp.any(lists == (far * BPF + b)[:, None, :, None], axis=3) for b in range(BPF)]
    listed = (has[0] | has[1]) & inside[:, None, :]
    sel = jnp.any(has[1], axis=1).astype(jnp.int32)
    bias = jnp.where(listed, 0.0, very_low).astype(jnp.float32)
    bias = jnp.concatenate([jnp.zeros((frames_here, BPF, BPF), jnp.float32), bias], axis=2)
    bias = jnp.repeat(bias.reshape(frames_here * BPF, BPF + SLOTS), BLK, axis=1)
    return sel, bias.reshape(frames_here * BPF, 1, KEYS)


def ring_attention(q_proj, k_proj, v_proj, kv_list):
    ctx, rep, uly = lax.axis_size("ctx"), lax.axis_size("rep"), lax.axis_size("uly")
    tokens, width = q_proj.shape
    heads = width // HD // GROUP
    inner = GROUP // (rep * uly)
    here = GROUP * tokens
    frames_here = here // FRAME
    hops = -(-REACH // frames_here)
    sel, bias = tables(kv_list, lax.axis_index("ctx") // inner, frames_here, ctx)
    window = (frames_here + SLOTS) * FRAME
    any_space = pl.BlockSpec(memory_space=pl.ANY)
    dma = pltpu.SemaphoreType.DMA
    return pl.pallas_call(
        functools.partial(ring_kernel, (ctx, rep, uly, tokens, heads)),
        out_shape=jax.ShapeDtypeStruct((tokens, width), jnp.bfloat16),
        in_specs=[
            pl.BlockSpec(memory_space=pltpu.SMEM),
            pl.BlockSpec(memory_space=pltpu.VMEM),
            any_space, any_space, any_space,
        ],
        out_specs=any_space,
        scratch_shapes=[
            pltpu.VMEM((heads, 2, window, HD), jnp.bfloat16),
            pltpu.VMEM((heads, here, HD), jnp.bfloat16),
            pltpu.VMEM((heads, here, HD), jnp.bfloat16),
            pltpu.VMEM((KEYS, HD), jnp.bfloat16),
            pltpu.VMEM((KEYS, HD), jnp.bfloat16),
            dma((GROUP,)), dma((heads,)), dma((heads,)), dma((heads,)), dma((heads,)),
            dma((2, hops, heads)), dma((2, hops, heads)), dma((1,)), dma((heads,)),
        ],
        compiler_params=pltpu.CompilerParams(
            collective_id=0, has_side_effects=True, vmem_limit_bytes=56 * 1024 * 1024
        ),
    )(sel, bias, q_proj, k_proj, v_proj)


PLANE = 4
NEAR = 3 * PLANE * FRAME
NEAR_KEYS = NEAR // 2 + BLK
FAR_SLOTS = 3
FAR = (2 * FAR_SLOTS - 1) * BLK
FAR_KEYS = FAR_SLOTS * BLK
STEPS = 2 * REACH + 1
PEERS = (2, 1, 3, 4, 6, 5, 7)


def plane_kernel(ctx, heads, list_ref, q_ref, k_ref, v_ref, out_ref,
                 lists, sel, listed, bias_near, bias_far, near, far, chosen, qb, ob, part, high, low, ks, vs,
                 list_in, own_in, beside_in, plane_in, q_in, ring_in, far_in, out_in,
                 plane_sent, q_sent, ring_sent, far_sent, out_sent, ready):
    here = PLANE * FRAME
    places = ctx // PLANE
    c = lax.axis_index("ctx")
    u = lax.axis_index("uly")
    place = c // PLANE
    me = (c % PLANE) * BPF + u

    def member(j):
        return {"ctx": place * PLANE + j // BPF, "uly": j % BPF}

    def beside(way):
        return {"ctx": c + (PLANE if way == 0 else -PLANE)}

    def peer(k):
        bits = (me % 2, (me // 2) % 2, me // 4)
        return sum((1 - bit if (k >> n) & 1 else bit) << n for n, bit in enumerate(bits))

    has = (place <= places - 2, place >= 1)
    gets = (place >= 1, place <= places - 2)
    sends_far = ((place >= 1) & (place <= places - 2),) * 2
    gets_far = (place >= 2, place <= places - 3)

    def columns(owner, h):
        return pl.ds(pl.multiple_of((owner * heads + h) * HD, HD), HD)

    def rows_of(j, base=0):
        return pl.ds(pl.multiple_of(base + j * BLK, BLK), BLK)

    def await_bytes(ref, sem):
        pltpu.make_async_copy(ref, ref, sem).wait()

    def fetch_own(h, carry):
        for which, src in enumerate((k_ref, v_ref)):
            pltpu.make_async_copy(
                src.at[:, columns(me, h)], near.at[h, which, rows_of(me, here)], own_in.at[h]
            ).start()
        return carry

    barrier = pltpu.get_barrier_semaphore()
    @pl.when(has[0])
    def _():
        pl.semaphore_signal(barrier, inc=1, device_id=beside(0), device_id_type=MESH)

    for k in PEERS:
        pl.semaphore_signal(barrier, inc=1, device_id=member(peer(k)), device_id_type=MESH)
    lax.fori_loop(0, heads, fetch_own, 0)
    pl.semaphore_wait(barrier, GROUP - 1 + jnp.minimum(place, 1))

    @pl.when(has[1])
    def _():
        pl.semaphore_signal(ready, inc=1, device_id=beside(1), device_id_type=MESH)

    lands = (0, 2 * here)

    def ring_piece(h, j, ways=(0, 1)):
        for way in ways:
            @pl.when(has[way])
            def _():
                pltpu.make_async_remote_copy(
                    src_ref=near.at[h, :, rows_of(j, here)], dst_ref=near.at[h, :, rows_of(j, lands[way])],
                    send_sem=ring_sent.at[way, h], recv_sem=ring_in.at[way, h],
                    device_id=beside(way), device_id_type=MESH,
                ).start()

    def share_kv(h, carry):
        for k in PEERS:
            j = peer(k)
            for which, src in enumerate((k_ref, v_ref)):
                pltpu.make_async_remote_copy(
                    src_ref=src.at[:, columns(j, h)], dst_ref=near.at[h, which, rows_of(me, here)],
                    send_sem=plane_sent.at[h], recv_sem=(beside_in if k == 2 else plane_in).at[h],
                    device_id=member(j), device_id_type=MESH,
                ).start()
        return carry

    def share_q(h, carry):
        for k in PEERS:
            j = peer(k)
            pltpu.make_async_remote_copy(
                src_ref=q_ref.at[:, columns(j, h)], dst_ref=qb.at[h, rows_of(me)],
                send_sem=q_sent.at[h], recv_sem=q_in.at[h],
                device_id=member(j), device_id_type=MESH,
            ).start()
        pltpu.make_async_copy(q_ref.at[:, columns(me, h)], qb.at[h, rows_of(me)], q_in.at[h]).start()
        return carry

    def own_left(h, carry):
        await_bytes(near.at[h, :, pl.ds(here, BLK)], own_in.at[h])
        ring_piece(h, me, (1,))
        return carry

    def own_right(h, carry):
        ring_piece(h, me, (0,))
        return carry

    lax.fori_loop(0, heads, own_left, 0)
    lax.fori_loop(0, heads, share_kv, 0)

    @pl.when(has[0])
    def _():
        pl.semaphore_wait(ready, 1)

    lax.fori_loop(0, heads, own_right, 0)
    lax.fori_loop(0, heads, share_q, 0)
    get_lists = pltpu.make_async_copy(list_ref, lists, list_in.at[0])
    get_lists.start()

    def ring_beside(h, carry):
        await_bytes(near.at[h, :, pl.ds(here, BLK)], beside_in.at[h])
        ring_piece(h, peer(2))
        return carry

    lax.fori_loop(0, heads, ring_beside, 0)

    for way in (0, 1):
        @pl.when(jnp.logical_not(gets[way]))
        def _():
            def clear(h, carry):
                for which in (0, 1):
                    near[h, which, pl.ds(lands[way], here), :] = jnp.zeros((here, HD), jnp.bfloat16)
                return carry

            lax.fori_loop(0, heads, clear, 0)

        @pl.when(jnp.logical_not(gets_far[way]))
        def _():
            def clear(h, carry):
                for which in (0, 1):
                    far[h, way, which] = jnp.zeros((FAR, HD), jnp.bfloat16)
                return carry

            lax.fori_loop(0, heads, clear, 0)

    get_lists.wait()

    def count(row, block):
        return sum((lists[j, row] == block).astype(jnp.int32) for j in range(lists.shape[0]))

    def tables(n, carry):
        a, d = n // STEPS, n % STEPS
        target = place * PLANE + a + d - REACH
        block = jnp.where(target < 0, -BLK, target * BPF)
        second = 0
        for b in range(BPF):
            row = (place * PLANE + a) * BPF + b
            one = count(row, block + 1)
            listed[a * BPF + b, d] = jnp.minimum(count(row, block) + one, 1)
            second = second + one
        sel[a, d] = jnp.minimum(second, 1)
        return carry

    lax.fori_loop(0, PLANE * STEPS, tables, 0)

    def fill(ref, r, slot, d):
        value = jnp.where(listed[r, d] == 1, 0.0, very_low)
        ref[r, :, pl.ds(pl.multiple_of(slot * BLK, BLK), BLK)] = jnp.full((1, BLK), value, jnp.float32)

    def biases(r, carry):
        a = r // BPF
        bias_near[r, :, pl.ds(0, FRAME)] = jnp.zeros((1, FRAME), jnp.float32)

        def one_near(i, carry):
            w = i + (i + REACH - PLANE - a) // REACH
            fill(bias_near, r, BPF + i, jnp.minimum(w + REACH - PLANE - a, STEPS - 1))
            return carry

        def one_far(i, carry):
            right = (i + a) // FAR_SLOTS
            fill(bias_far, r, i, i + right * (STEPS - FAR_SLOTS))
            return carry

        lax.fori_loop(0, 3 * PLANE - 1, one_near, 0)
        lax.fori_loop(0, FAR_SLOTS, one_far, 0)
        return carry

    lax.fori_loop(0, PLANE * BPF, biases, 0)

    def ring_rest(h, carry):
        await_bytes(near.at[h, :, pl.ds(here, here - BPF * BLK)], plane_in.at[h])
        for k in PEERS[1:]:
            ring_piece(h, peer(k))
        return carry

    lax.fori_loop(0, heads, ring_rest, 0)

    frames = ctx
    onward = (
        (jnp.minimum((place + 1) * PLANE, frames - 1), place * PLANE - PLANE + 1),
        (jnp.maximum((place - 1) * PLANE + PLANE - 1, 0), place * PLANE + PLANE + 2),
    )
    takes_second = [
        (count(f * BPF, g * BPF + 1) + count(f * BPF + 1, g * BPF + 1)) > 0 for f, g in onward
    ]

    def far_copy(way, n, h):
        b = 3 - n if way == 0 else 2 * PLANE + n
        whole = n < FAR_SLOTS - 1
        rows = FRAME if whole else BLK
        return pltpu.make_async_remote_copy(
            src_ref=near.at[h, :, pl.ds(b * FRAME, rows)] if whole else chosen.at[h, way],
            dst_ref=far.at[h, way, :, pl.ds(n * FRAME, rows)],
            send_sem=far_sent.at[way, n, h], recv_sem=far_in.at[way, n, h],
            device_id=beside(way), device_id_type=MESH,
        )

    def attend_near(h):
        def one_frame(a, carry):
            own = pl.multiple_of((PLANE + a) * FRAME, FRAME)
            ks[pl.ds(0, FRAME), :] = near[h, 0, pl.ds(own, FRAME), :]
            vs[pl.ds(0, FRAME), :] = near[h, 1, pl.ds(own, FRAME), :]

            def pick(i, carry):
                w = i + (i + REACH - PLANE - a) // REACH
                row = pl.multiple_of(w * FRAME, FRAME)
                second = sel[a, jnp.minimum(w + REACH - PLANE - a, STEPS - 1)] == 1
                to = pl.ds(pl.multiple_of(FRAME + i * BLK, BLK), BLK)
                for which, dst in ((0, ks), (1, vs)):
                    dst[to, :] = jnp.where(
                        second, near[h, which, pl.ds(row + BLK, BLK), :], near[h, which, pl.ds(row, BLK), :]
                    )
                return carry

            lax.fori_loop(0, 3 * PLANE - 1, pick, 0)
            rows = pl.ds(pl.multiple_of(a * FRAME, FRAME), FRAME)
            scores = lax.dot_general(
                qb[h, rows, :], ks[...], (((1,), (1,)), ((), ())), preferred_element_type=jnp.float32
            ).reshape(BPF, BLK, NEAR_KEYS)
            scores = scores * scale2 + bias_near[pl.ds(a * BPF, BPF)]
            top = jnp.max(scores, axis=2, keepdims=True)
            weights = jnp.exp2(scores - top)
            total = jnp.sum(weights, axis=2, keepdims=True)
            part[h, rows, :] = jnp.dot(
                weights.reshape(FRAME, NEAR_KEYS).astype(jnp.bfloat16), vs[...],
                preferred_element_type=jnp.float32,
            )
            high[h, rows, :] = jnp.broadcast_to(top, (BPF, BLK, HD)).reshape(FRAME, HD)
            low[h, rows, :] = jnp.broadcast_to(total, (BPF, BLK, HD)).reshape(FRAME, HD)
            return carry

        lax.fori_loop(0, PLANE, one_frame, 0)

    def attend_far(h, a):
        def pick(i, carry):
            right = (i + a) // FAR_SLOTS
            pair = (1 - right) * (FAR_SLOTS - 1 - a - i) + right * (i + a - FAR_SLOTS)
            whole = 1 - pair // (FAR_SLOTS - 1)
            row = pl.multiple_of(pair * FRAME, FRAME)
            row_b = pl.multiple_of(pair * FRAME + whole * BLK, BLK)
            second = sel[a, i + right * (STEPS - FAR_SLOTS)] == 1
            to = pl.ds(pl.multiple_of(i * BLK, BLK), BLK)
            for which, dst in ((0, ks), (1, vs)):
                dst[to, :] = jnp.where(
                    second, far[h, right, which, pl.ds(row_b, BLK), :], far[h, right, which, pl.ds(row, BLK), :]
                )
            return carry

        lax.fori_loop(0, FAR_SLOTS, pick, 0)
        rows = pl.ds(pl.multiple_of(a * FRAME, FRAME), FRAME)
        keys = pl.ds(0, FAR_KEYS)
        scores = lax.dot_general(
            qb[h, rows, :], ks[keys, :], (((1,), (1,)), ((), ())), preferred_element_type=jnp.float32
        ).reshape(BPF, BLK, FAR_KEYS)
        scores = (scores * scale2 + bias_far[pl.ds(a * BPF, BPF)]).reshape(FRAME, FAR_KEYS)
        before = high[h, rows, :]
        top = jnp.maximum(before, jnp.max(scores, axis=1, keepdims=True))
        weights = jnp.exp2(scores - jnp.concatenate([top] * FAR_SLOTS, axis=1))
        fade = jnp.exp2(before - top)
        total = fade * low[h, rows, :] + jnp.sum(weights, axis=1, keepdims=True)
        mixed = fade * part[h, rows, :] + jnp.dot(
            weights.astype(jnp.bfloat16), vs[keys, :], preferred_element_type=jnp.float32
        )
        ob[h, rows, :] = (mixed / total).astype(jnp.bfloat16)

    def give_back(h, a):
        for b in range(BPF):
            j = a * BPF + b

            @pl.when(j != me)
            def _():
                pltpu.make_async_remote_copy(
                    src_ref=ob.at[h, rows_of(j)], dst_ref=out_ref.at[:, columns(me, h)],
                    send_sem=out_sent.at[h], recv_sem=out_in.at[0],
                    device_id=member(j), device_id_type=MESH,
                ).start()

            @pl.when(j == me)
            def _():
                pltpu.make_async_copy(ob.at[h, rows_of(j)], out_ref.at[:, columns(me, h)], out_in.at[0]).start()

    def first_phase(h, carry):
        for way in (0, 1):
            @pl.when(gets[way])
            def _():
                await_bytes(near.at[h, :, pl.ds(lands[way], here)], ring_in.at[way, h])

        for way in (0, 1):
            @pl.when(sends_far[way])
            def _():
                frame = 1 if way == 0 else 2 * PLANE + 2
                for which in (0, 1):
                    chosen[h, way, which] = jnp.where(
                        takes_second[way],
                        near[h, which, pl.ds(frame * FRAME + BLK, BLK), :],
                        near[h, which, pl.ds(frame * FRAME, BLK), :],
                    )
                for n in range(FAR_SLOTS):
                    far_copy(way, n, h).start()

        await_bytes(qb.at[h], q_in.at[h])
        attend_near(h)
        return carry

    lax.fori_loop(0, heads, first_phase, 0)

    both = gets_far[0] & gets_far[1]
    falling = jnp.where(gets_far[0], 1, 0)

    others = (GROUP - 1) * BLK

    def await_far_sent(h):
        for way in (0, 1):
            @pl.when(sends_far[way])
            def _():
                for n in range(FAR_SLOTS):
                    far_copy(way, n, h).wait_send()

    def await_out_sent(h):
        await_bytes(ob.at[h, pl.ds(0, others)], out_sent.at[h])

    def second_phase(h, carry):
        await_bytes(near.at[h, :, pl.ds(0, others)], plane_sent.at[h])
        await_bytes(qb.at[h, pl.ds(0, others)], q_sent.at[h])
        for way in (0, 1):
            @pl.when(has[way])
            def _():
                await_bytes(near.at[h, :, pl.ds(0, here)], ring_sent.at[way, h])

        @pl.when(h >= 1)
        def _():
            await_far_sent(h - 1)
            await_out_sent(h - 1)

        for way in (0, 1):
            @pl.when(both)
            def _():
                for n in range(FAR_SLOTS):
                    far_copy(way, n, h).wait_recv()

        for n in range(PLANE):
            if n >= 1:
                for way in (0, 1):
                    @pl.when(gets_far[way] & jnp.logical_not(both))
                    def _():
                        far_copy(way, n - 1, h).wait_recv()
            a = falling * (PLANE - 1 - n) + (1 - falling) * n
            attend_far(h, a)
            give_back(h, a)
        return carry

    lax.fori_loop(0, heads, second_phase, 0)

    await_far_sent(heads - 1)
    await_out_sent(heads - 1)
    await_bytes(out_ref, out_in.at[0])


def plane_attention(q_proj, k_proj, v_proj, kv_list):
    ctx = lax.axis_size("ctx")
    tokens, width = q_proj.shape
    heads = width // HD // GROUP
    here = PLANE * FRAME
    lists = kv_list.T
    any_space = pl.BlockSpec(memory_space=pl.ANY)
    dma = pltpu.SemaphoreType.DMA
    bf16, f32 = jnp.bfloat16, jnp.float32
    return pl.pallas_call(
        functools.partial(plane_kernel, ctx, heads),
        out_shape=jax.ShapeDtypeStruct((tokens, width), bf16),
        in_specs=[any_space] * 4,
        out_specs=any_space,
        scratch_shapes=[
            pltpu.SMEM(lists.shape, jnp.int32),
            pltpu.SMEM((PLANE, STEPS), jnp.int32),
            pltpu.SMEM((PLANE * BPF, STEPS), jnp.int32),
            pltpu.VMEM((PLANE * BPF, 1, NEAR_KEYS), f32),
            pltpu.VMEM((PLANE * BPF, 1, FAR_KEYS), f32),
            pltpu.VMEM((heads, 2, NEAR, HD), bf16),
            pltpu.VMEM((heads, 2, 2, FAR, HD), bf16),
            pltpu.VMEM((heads, 2, 2, BLK, HD), bf16),
            pltpu.VMEM((heads, here, HD), bf16),
            pltpu.VMEM((heads, here, HD), bf16),
            pltpu.VMEM((heads, here, HD), f32),
            pltpu.VMEM((heads, here, HD), f32),
            pltpu.VMEM((heads, here, HD), f32),
            pltpu.VMEM((NEAR_KEYS, HD), bf16),
            pltpu.VMEM((NEAR_KEYS, HD), bf16),
            dma((1,)), dma((heads,)), dma((heads,)), dma((heads,)), dma((heads,)), dma((2, heads)),
            dma((2, FAR_SLOTS, heads)), dma((1,)),
            dma((heads,)), dma((heads,)), dma((2, heads)), dma((2, FAR_SLOTS, heads)), dma((heads,)),
            pltpu.SemaphoreType.REGULAR,
        ],
        compiler_params=pltpu.CompilerParams(
            collective_id=0, has_side_effects=True, vmem_limit_bytes=30 * 1024 * 1024
        ),
    )(*[pltpu.with_memory_space_constraint(x, pltpu.HBM) for x in (lists, q_proj, k_proj, v_proj)])


def on_device(q_proj, k_proj, v_proj, kv_list):
    rep, uly = lax.axis_size("rep"), lax.axis_size("uly")
    if rep == 1 and uly == BPF and q_proj.shape[0] == BLK and lax.axis_size("ctx") % PLANE == 0:
        return plane_attention(q_proj, k_proj, v_proj, kv_list)
    return ring_attention(q_proj, k_proj, v_proj, kv_list)


def solution(mesh):
    rows = P(("groups", "ctx", "rep", "uly"), None)
    return jax.shard_map(
        on_device,
        mesh=mesh,
        in_specs=(rows, rows, rows, P("groups", None)),
        out_specs=rows,
        check_vma=False,
    )
```
